512 devices in a mesh: dp: 16 (over z, core), tensor: 8 (over y), pipe: 4 (over x).
Axes of the slice: x: 4, y: 8, z: 8, core: 2. Of those that a mesh axis runs over, the one named last changes fastest.
Arguments:
- query: bfloat16 [4, 4096, 8, 640], P('pipe', 'dp', 'tensor'), may hold values from -40 to 40
- keys_values: bfloat16 [4, 4096, 8, 256], P('pipe', 'dp', 'tensor'), may hold values from -4 to 4
- doc_lengths: int32 [4, 8], P('pipe'), may hold values from 1 to 3072, 4096 in all within a row
- incoming_output_grad: bfloat16 [4, 4096, 8, 640], P('pipe', ('dp', 'tensor')), may hold values from -6 to 6
Outputs:
- attn_out: bfloat16 [4, 4096, 8, 640], P('pipe', 'dp', 'tensor')
- grad_query: bfloat16 [4, 4096, 8, 640], P('pipe', 'dp', 'tensor')
- grad_keys_values: bfloat16 [4, 4096, 8, 256], P('pipe', 'dp', 'tensor')
The draws below stay inside these ranges and needn't reach their ends.
Inputs may be any that keep to these rules, and one draw needn't show every extreme that they name: `doc_lengths`: each row sums to 4096; no document is longer than 3072 positions, and some document of each row is exactly that long.
All inputs are finite; a program needn't handle non-finite values.
Results may differ from the reference program's by a relative error of at most 0.04.
Values may be sent and summed in bfloat16 or wider, within the bound.
No kernel may reach another device: no remote copies, remote signals or barrier semaphores. Data moves between devices by JAX's collectives and lax.ppermute only.
A program may use at most 64 MiB of HBM per device.

```python
import math
import jax
import jax.numpy as jnp
import numpy as np
from jax import lax

KEY_VALUE_HEADS = 8
HEAD_SIZE = 128
QUERY_PER_KV = 5
DOCS = 8
RELAY_SECTIONS = 4
SEQUENCE_LENGTH = 4096
MOST = 3072


def draw_query(key, part):
    array_shape = (RELAY_SECTIONS, SEQUENCE_LENGTH, KEY_VALUE_HEADS, QUERY_PER_KV, HEAD_SIZE)
    value_rows = jnp.clip(jax.random.normal(jax.random.fold_in(key, 3), array_shape, jnp.float32), -4.0, 4.0)
    return value_rows.reshape(RELAY_SECTIONS, SEQUENCE_LENGTH, KEY_VALUE_HEADS, QUERY_PER_KV * HEAD_SIZE).astype(jnp.bfloat16)


def draw_keys_values(key, part):
    array_shape = (RELAY_SECTIONS, SEQUENCE_LENGTH, KEY_VALUE_HEADS, HEAD_SIZE)
    key_part = jnp.clip(jax.random.normal(jax.random.fold_in(key, 4), array_shape, jnp.float32), -4.0, 4.0)
    value_part = jnp.clip(jax.random.normal(jax.random.fold_in(key, 5), array_shape, jnp.float32), -4.0, 4.0)
    return jnp.concatenate([key_part, value_part], axis=3).astype(jnp.bfloat16)


def levels(stream_key, dims, shards, smallest, largest):
    loudness, own = 1.0, jax.random.fold_in(stream_key, 6)
    for dim, parts in shards:
        steps = jnp.exp(jax.random.uniform(jax.random.fold_in(own, dim), (parts,), jnp.float32, smallest / len(shards), largest / len(shards)))
        loudness = loudness * jnp.repeat(steps, dims[dim] // parts).reshape([-1 if axis == dim else 1 for axis in range(len(dims))])
    return loudness


def profile(count, total, bound, slope):
    loads = [(1 << 20) // math.isqrt(grade ** slope) + 1 for grade in range(2, count + 1)]
    rest, counts = total - bound - (count - 1), [1] * (count - 1)
    while rest > 0:
        movable = [i for i in range(count - 1) if counts[i] < bound]
        mass, remaining = sum([loads[i] for i in movable]), rest
        for i in movable:
            extra = min(bound - counts[i], max(1, remaining * loads[i] // mass), rest)
            counts[i] = counts[i] + extra
            rest = rest - extra
    return np.array([bound] + counts)


def uneven(rng, amount, total, limit, slope):
    if amount == 2:
        one = jax.random.randint(rng, (), max(1, total - limit), min(limit, total - 1) + 1)
        return jnp.stack([one, total - one])
    sizes = jnp.asarray(profile(amount, total, limit, slope), jnp.int32)
    pairs = (amount - 1) // 2
    source_of, sink = sizes[1:1 + 2 * pairs:2], sizes[2:2 + 2 * pairs:2]
    slack = jnp.minimum(source_of - 1, limit - sink)
    passed = jax.random.randint(jax.random.fold_in(rng, 1), (pairs,), 0, 1 << 20) % (slack + 1)
    sizes = sizes.at[1:1 + 2 * pairs:2].set(source_of - passed).at[2:2 + 2 * pairs:2].set(sink + passed)
    return sizes[jax.random.permutation(jax.random.fold_in(rng, 2), amount)]


def gaussian(rng, dims, width, limit, split=(), held_as=jnp.bfloat16):
    array = width * jax.random.normal(rng, dims, jnp.float32)
    if split:
        array = array * levels(rng, dims, split, -0.22, 0.18)
    return jnp.clip(array, -limit, limit).astype(held_as)


def setup_inputs(seed: int = 0) -> dict:
    key_of = jax.random.split(jax.random.key(seed), 5)
    return {
        "query": draw_query(jax.random.fold_in(key_of[4], 71), 0),
        "keys_values": draw_keys_values(jax.random.fold_in(key_of[4], 71), 0),
        "doc_lengths": jax.vmap(lambda own: uneven(own, DOCS, SEQUENCE_LENGTH, MOST, 2))(jax.random.split(key_of[2], RELAY_SECTIONS)).reshape((RELAY_SECTIONS, DOCS)).astype(jnp.int32),
        "incoming_output_grad": gaussian(key_of[3], (RELAY_SECTIONS, SEQUENCE_LENGTH, KEY_VALUE_HEADS, QUERY_PER_KV * HEAD_SIZE), 1.0, 6.0, ((0, 4), (1, 128))),
    }


NEG_LARGE = -1e+30

def by_head(grouped_heads):
    return grouped_heads.reshape(SEQUENCE_LENGTH, KEY_VALUE_HEADS, QUERY_PER_KV, HEAD_SIZE).transpose(1, 2, 0, 3).reshape(KEY_VALUE_HEADS * QUERY_PER_KV, SEQUENCE_LENGTH, HEAD_SIZE)

def from_head(head_split):
    return head_split.reshape(KEY_VALUE_HEADS, QUERY_PER_KV, SEQUENCE_LENGTH, HEAD_SIZE).transpose(2, 0, 1, 3).reshape(SEQUENCE_LENGTH, KEY_VALUE_HEADS, QUERY_PER_KV * HEAD_SIZE)

def section_pass(query_section, pairs_section, lengths, cotangent):
    positions = jnp.arange(SEQUENCE_LENGTH, dtype=jnp.int32)
    doc_ends = jnp.cumsum(lengths).astype(jnp.int32)
    documents = lax.optimization_barrier(jnp.sum((positions[:, None] >= doc_ends[None, :]).astype(jnp.int32), axis=1))
    allowed = (positions[None, :] <= positions[:, None]) & (documents[None, :] == documents[:, None])
    inv_root = 1.0 / math.sqrt(HEAD_SIZE)
    head_queries = by_head(query_section)
    head_grads = by_head(cotangent)
    head_keys = jnp.repeat(pairs_section[:, :, :HEAD_SIZE].transpose(1, 0, 2), QUERY_PER_KV, axis=0)
    head_values = jnp.repeat(pairs_section[:, :, HEAD_SIZE:].transpose(1, 0, 2), QUERY_PER_KV, axis=0)

    def one_head(operands):
        query_head, key_head, value_head, grad_head = operands
        scores = jnp.dot(query_head, key_head.T, preferred_element_type=jnp.float32) * inv_root
        scores = jnp.where(allowed, scores, NEG_LARGE)
        rowmax = lax.optimization_barrier(jnp.max(scores, axis=1))
        numerators = jnp.where(allowed, jnp.exp(scores - rowmax[:, None]), 0.0)
        totals = lax.optimization_barrier(jnp.sum(numerators, axis=1))
        weights = numerators.astype(jnp.bfloat16)
        head_out = (jnp.dot(weights, value_head, preferred_element_type=jnp.float32) / totals[:, None]).astype(jnp.bfloat16)
        log_totals = rowmax + jnp.log(totals)
        probs = jnp.where(allowed, jnp.exp(scores - log_totals[:, None]), 0.0)
        probs_low = probs.astype(jnp.bfloat16)
        delta = lax.optimization_barrier(jnp.sum(grad_head.astype(jnp.float32) * head_out.astype(jnp.float32), axis=1))
        value_grad = jnp.dot(probs_low.T, grad_head, preferred_element_type=jnp.float32)
        prob_grad = jnp.dot(grad_head, value_head.T, preferred_element_type=jnp.float32)
        score_grad = (probs * (prob_grad - delta[:, None])).astype(jnp.bfloat16)
        query_grad = (jnp.dot(score_grad, key_head, preferred_element_type=jnp.float32) * inv_root).astype(jnp.bfloat16)
        key_grad = jnp.dot(score_grad.T, query_head, preferred_element_type=jnp.float32) * inv_root
        return (head_out, query_grad, key_grad, value_grad)
    head_out, query_grads, key_gradient_rows, value_gradient_rows = lax.map(one_head, (head_queries, head_keys, head_values, head_grads))
    summed_key_grad = key_gradient_rows.reshape(KEY_VALUE_HEADS, QUERY_PER_KV, SEQUENCE_LENGTH, HEAD_SIZE).sum(axis=1)
    summed_value_grad = value_gradient_rows.reshape(KEY_VALUE_HEADS, QUERY_PER_KV, SEQUENCE_LENGTH, HEAD_SIZE).sum(axis=1)
    pair_grads = jnp.concatenate([summed_key_grad, summed_value_grad], axis=2).transpose(1, 0, 2).astype(jnp.bfloat16)
    return (from_head(head_out), from_head(query_grads), pair_grads)

def reference(query, keys_values, doc_lengths, incoming_output_grad):
    outputs = []
    query_grads = []
    pair_grads = []
    for section_index in range(RELAY_SECTIONS):
        cotangent = incoming_output_grad[(section_index + 1) % RELAY_SECTIONS]
        result_out, result_query, result_pairs = section_pass(query[section_index], keys_values[section_index], doc_lengths[section_index], cotangent)
        outputs.append(result_out)
        query_grads.append(result_query)
        pair_grads.append(result_pairs)
    return (jnp.stack(outputs), jnp.stack(query_grads), jnp.stack(pair_grads))
```

```python
import functools
import math

import jax
import jax.numpy as jnp
from jax import lax
from jax.experimental import pallas as pl
from jax.experimental.pallas import tpu as pltpu
from jax.sharding import Mesh, PartitionSpec as P

NEG_LARGE = -1e30
LOG2E = math.log2(math.e)
HEAD = 128
LONGEST = 3072


def matmul(left, right):
    return jnp.dot(left, right, preferred_element_type=jnp.float32)


def block_mask(block, rows, bounds_ref, starts_ref):
    key_pos = block * rows + lax.broadcasted_iota(jnp.int32, (rows, rows), 0)
    query_pos = bounds_ref[0] * rows + lax.broadcasted_iota(jnp.int32, (rows, rows), 1)
    return (key_pos <= query_pos) & (key_pos >= starts_ref[...])


def over_blocks(visit, bounds_ref):
    own, first, clear = bounds_ref[0], bounds_ref[1], bounds_ref[2]

    def masked(step, unused):
        visit(jnp.where(step == 0, own, first + step - 1), True)
        return unused

    def plain(block, unused):
        visit(block, False)
        return unused

    lax.fori_loop(0, clear - first + 1, masked, 0)
    lax.fori_loop(clear, own, plain, 0)


def forward_kernel(
    bounds_ref, starts_ref, turned_ref, pairs_ref, turned_grad_ref,
    out_ref, log_ref, delta_ref, top_ref, total_ref, acc_ref,
):
    rows = starts_ref.shape[1]
    heads = turned_ref.shape[1] // rows
    scale = LOG2E / math.sqrt(HEAD)
    top_ref[...] = jnp.full_like(top_ref, NEG_LARGE)
    total_ref[...] = jnp.zeros_like(total_ref)
    acc_ref[...] = jnp.zeros_like(acc_ref)

    def visit(block, masked):
        at = pl.ds(pl.multiple_of(block * rows, rows), rows)
        keys = pairs_ref[at, :HEAD]
        turned_values = pairs_ref[at, HEAD:].T
        if masked:
            allowed = block_mask(block, rows, bounds_ref, starts_ref)
        for head in range(heads):
            span = slice(head * rows, (head + 1) * rows)
            scores = matmul(keys, turned_ref[:, span]) * scale
            if masked:
                scores = jnp.where(allowed, scores, NEG_LARGE)
            before = top_ref[:, span]
            top = jnp.maximum(before, jnp.max(scores, axis=0, keepdims=True))
            numerators = jnp.exp2(scores - top)
            factor = jnp.exp2(before - top)
            top_ref[:, span] = top
            total_ref[:, span] = total_ref[:, span] * factor + jnp.sum(
                numerators, axis=0, keepdims=True
            )
            acc_ref[:, span] = acc_ref[:, span] * factor + matmul(
                turned_values, numerators.astype(jnp.bfloat16)
            )

    over_blocks(visit, bounds_ref)
    totals = total_ref[...]
    log_ref[...] = top_ref[...] + jnp.log2(totals)
    for head in range(heads):
        span = slice(head * rows, (head + 1) * rows)
        result = (acc_ref[:, span] / total_ref[:, span]).astype(jnp.bfloat16)
        delta_ref[:, span] = jnp.sum(
            result.astype(jnp.float32) * turned_grad_ref[:, span].astype(jnp.float32),
            axis=0,
            keepdims=True,
        )
        out_ref[:, head * HEAD : (head + 1) * HEAD] = result.T


def backward_kernel(
    bounds_ref, starts_ref, query_ref, grad_ref, turned_ref, turned_grad_ref,
    pairs_ref, log_ref, delta_ref, query_grad_ref, pair_grad_ref, acc_ref,
):
    rows = starts_ref.shape[1]
    heads = turned_ref.shape[1] // rows
    root = 1.0 / math.sqrt(HEAD)
    scale = LOG2E * root
    acc_ref[...] = jnp.zeros_like(acc_ref)
    pair_grad_ref[...] = jnp.zeros_like(pair_grad_ref)
    half = pair_grad_ref.shape[0] // 2
    own = bounds_ref[0]

    def visit(block, masked):
        at = pl.ds(pl.multiple_of(block * rows, rows), rows)
        keys = pairs_ref[at, :HEAD]
        values = pairs_ref[at, HEAD:]
        turned_keys = keys.T
        if masked:
            allowed = block_mask(block, rows, bounds_ref, starts_ref)
        key_grad = jnp.zeros((rows, HEAD), jnp.float32)
        value_grad = jnp.zeros((rows, HEAD), jnp.float32)
        for head in range(heads):
            span = slice(head * rows, (head + 1) * rows)
            columns = slice(head * HEAD, (head + 1) * HEAD)
            scores = matmul(keys, turned_ref[:, span]) * scale
            if masked:
                scores = jnp.where(allowed, scores, NEG_LARGE)
            probs = jnp.exp2(scores - log_ref[:, span])
            prob_grad = matmul(values, turned_grad_ref[:, span])
            score_grad = (probs * (prob_grad - delta_ref[:, span])).astype(jnp.bfloat16)
            value_grad += matmul(probs.astype(jnp.bfloat16), grad_ref[:, columns])
            key_grad += matmul(score_grad, query_ref[:, columns])
            acc_ref[:, span] += matmul(turned_keys, score_grad)
        back = own // 2 - block // 2
        other = jnp.where(block % 2 == own % 2, 0, half)
        to = pl.ds(pl.multiple_of(other + back * rows, rows), rows)
        pair_grad_ref[to, :HEAD] = (key_grad * root).astype(jnp.bfloat16)
        pair_grad_ref[to, HEAD:] = value_grad.astype(jnp.bfloat16)

    over_blocks(visit, bounds_ref)
    for head in range(heads):
        span = slice(head * rows, (head + 1) * rows)
        turned = (acc_ref[:, span] * root).astype(jnp.bfloat16)
        query_grad_ref[:, head * HEAD : (head + 1) * HEAD] = turned.T


def smem():
    return pl.BlockSpec(memory_space=pltpu.SMEM)


def vmem():
    return pl.BlockSpec(memory_space=pltpu.VMEM)


def forward(bounds, starts, turned, pairs, turned_grad, rows):
    wide = turned.shape[1]
    columns = wide // rows * HEAD
    return pl.pallas_call(
        forward_kernel,
        out_shape=(
            jax.ShapeDtypeStruct((rows, columns), jnp.bfloat16),
            jax.ShapeDtypeStruct((1, wide), jnp.float32),
            jax.ShapeDtypeStruct((1, wide), jnp.float32),
        ),
        in_specs=[smem()] + [vmem()] * 4,
        out_specs=(vmem(),) * 3,
        scratch_shapes=[
            pltpu.VMEM((1, wide), jnp.float32),
            pltpu.VMEM((1, wide), jnp.float32),
            pltpu.VMEM((HEAD, wide), jnp.float32),
        ],
        compiler_params=pltpu.CompilerParams(vmem_limit_bytes=40 << 20),
        name="attend_forward",
    )(bounds, starts, turned, pairs, turned_grad)


def backward(bounds, starts, query, grad, turned, turned_grad, pairs, log_totals, delta, slots):
    rows = query.shape[0]
    wide = turned.shape[1]
    return pl.pallas_call(
        backward_kernel,
        out_shape=(
            jax.ShapeDtypeStruct(query.shape, jnp.bfloat16),
            jax.ShapeDtypeStruct((2 * slots * rows, 2 * HEAD), jnp.bfloat16),
        ),
        in_specs=[smem()] + [vmem()] * 8,
        out_specs=(vmem(),) * 2,
        scratch_shapes=[pltpu.VMEM((HEAD, wide), jnp.float32)],
        compiler_params=pltpu.CompilerParams(vmem_limit_bytes=40 << 20),
        name="attend_backward",
    )(bounds, starts, query, grad, turned, turned_grad, pairs, log_totals, delta)


def turn(array):
    rows, columns = array.shape
    heads = columns // HEAD
    return array.reshape(rows, heads, HEAD).transpose(2, 1, 0).reshape(HEAD, heads * rows)


def block_bounds(lengths, own, rows):
    ends = jnp.cumsum(lengths)
    begins = ends - lengths
    positions = own * rows + jnp.arange(rows, dtype=jnp.int32)
    starts = jnp.max(jnp.where(begins[:, None] <= positions[None, :], begins[:, None], 0), axis=0)
    first = starts[0] // rows
    clear = jnp.minimum((starts[-1] + rows - 1) // rows, own)
    return jnp.stack([own, first, clear]).astype(jnp.int32), starts[None, :]


def swap_cores(value):
    return lax.ppermute(value, "core", [(0, 1), (1, 0)])


def per_device(query, keys_values, doc_lengths, incoming_output_grad):
    chips = lax.axis_size("chip")
    query = query[0, :, 0, :]
    pairs = keys_values[0, :, 0, :]
    rows = query.shape[0]
    own = lax.axis_index("chip") * 2 + lax.axis_index("core")
    every_pair = lax.all_gather(pairs, ("chip", "core"), axis=0, tiled=True)
    sections = lax.axis_size("pipe")
    arrived = lax.ppermute(
        incoming_output_grad, "pipe", [(s, (s - 1) % sections) for s in range(sections)]
    )
    grad = lax.all_to_all(arrived, "tensor", split_axis=2, concat_axis=1, tiled=True)[0, :, 0, :]
    bounds, starts = block_bounds(doc_lengths[0], own, rows)
    turned, turned_grad = turn(query), turn(grad)
    outputs, log_totals, delta = forward(bounds, starts, turned, every_pair, turned_grad, rows)
    reach = min((LONGEST + 2 * rows - 1) // (2 * rows), chips - 1)
    slots = reach + 1
    query_grad, partial = backward(
        bounds, starts, query, grad, turned, turned_grad, every_pair, log_totals, delta, slots
    )
    half = slots * rows
    mine = partial[:half].astype(jnp.float32) + swap_cores(partial[half:]).astype(jnp.float32)
    mine = mine.reshape(slots, rows, 2 * HEAD)
    sums = mine[0]
    low = mine.astype(jnp.bfloat16)
    for back in range(1, slots):
        sums += lax.ppermute(
            low[back], "chip", [(c, c - back) for c in range(back, chips)]
        ).astype(jnp.float32)
    pair_grad = sums.astype(jnp.bfloat16)
    return (outputs[None, :, None, :], query_grad[None, :, None, :], pair_grad[None, :, None, :])


def solution(mesh):
    shape = mesh.devices.shape
    split = Mesh(
        mesh.devices.reshape((shape[0] // 2, 2) + shape[1:]), ("chip", "core", "tensor", "pipe")
    )
    dp = ("chip", "core")
    by_head = P("pipe", dp, "tensor", None)
    in_specs = (by_head, by_head, P("pipe", None), P("pipe", dp + ("tensor",), None, None))
    return jax.shard_map(
        per_device, mesh=split, in_specs=in_specs, out_specs=(by_head,) * 3, check_vma=False
    )
```

```python
import functools
import math

import jax
import jax.numpy as jnp
from jax import lax
from jax.experimental import pallas as pl
from jax.experimental.pallas import tpu as pltpu
from jax.sharding import Mesh, PartitionSpec as P

NEG_LARGE = -1e30
LOG2E = math.log2(math.e)
HEAD = 128
LONGEST = 3072
TOP, TOTAL, INNER = 0, 1, 2


def matmul(left, right):
    return jnp.dot(left, right, preferred_element_type=jnp.float32)


def fold(array):
    return array.reshape(array.shape[0] // 8, 8, array.shape[1])


def forward_kernel(
    bounds_ref, starts_ref, turned_ref, pairs_ref, turned_grad_ref,
    weights_ref, acc_ref, stats_ref, scores_ref, top_ref,
):
    rows = starts_ref.shape[2]
    groups = turned_ref.shape[1] // rows
    heads = groups // 2
    scale = LOG2E / math.sqrt(HEAD)
    chip, own, clear, last = bounds_ref[0], bounds_ref[1], bounds_ref[3], bounds_ref[4]
    top_ref[...] = jnp.full_like(top_ref, NEG_LARGE)
    acc_ref[...] = jnp.zeros_like(acc_ref)

    def measure(back, masked):
        at = pl.ds(pl.multiple_of((chip - back) * rows, rows), rows)
        to = pl.ds(pl.multiple_of(back * rows, rows), rows)
        keys = pairs_ref[at, :HEAD]
        allowed = []
        if masked:
            key_pos = (own - 2 * back) * rows + lax.broadcasted_iota(jnp.int32, (rows, rows), 0)
            across = lax.broadcasted_iota(jnp.int32, (rows, rows), 1)
            for slot in range(2):
                query_pos = bounds_ref[1 + slot] * rows + across
                allowed.append((key_pos <= query_pos) & (key_pos >= starts_ref[slot]))
        for group in range(groups):
            span = slice(group * rows, (group + 1) * rows)
            scores = matmul(keys, turned_ref[:, span])
            if masked:
                scores = jnp.where(allowed[group // heads], scores, NEG_LARGE)
            scores_ref[to, span] = scores
            top_ref[:, span] = jnp.maximum(top_ref[:, span], jnp.max(fold(scores), axis=0))

    def masked(step, unused):
        measure(jnp.where(step == 0, 0, clear + step), True)
        return unused

    def plain(back, unused):
        measure(back, False)
        return unused

    lax.fori_loop(0, last - clear + 1, masked, 0)
    lax.fori_loop(1, clear + 1, plain, 0)
    top = jnp.max(top_ref[...], axis=0, keepdims=True) * scale
    stats_ref[TOP : TOP + 1, :] = top
    top_ref[...] = jnp.broadcast_to(top, top_ref.shape)

    def weigh(back, unused):
        at = pl.ds(pl.multiple_of((chip - back) * rows, rows), rows)
        to = pl.ds(pl.multiple_of(back * rows, rows), rows)
        turned_values = jnp.concatenate(
            [pairs_ref[at, HEAD:].T, jnp.ones((16, rows), jnp.bfloat16)], axis=0
        )
        for group in range(groups):
            span = slice(group * rows, (group + 1) * rows)
            weights_ref[to, span] = jnp.exp2(
                scores_ref[to, span] * scale - top_ref[:1, span]
            ).astype(jnp.bfloat16)
        acc_ref[...] += matmul(turned_values, weights_ref[to, :])
        return unused

    lax.fori_loop(0, last + 1, weigh, 0)
    stats_ref[TOTAL : TOTAL + 1, :] = acc_ref[HEAD : HEAD + 1, :]
    for group in range(groups):
        span = slice(group * rows, (group + 1) * rows)
        stats_ref[INNER : INNER + 1, span] = jnp.sum(
            acc_ref[:HEAD, span] * turned_grad_ref[:, span].astype(jnp.float32),
            axis=0,
            keepdims=True,
        )


def backward_kernel(
    bounds_ref, stats_ref, arrived_ref, acc_ref, turned_grad_ref, query_ref,
    pairs_ref, weights_ref,
    out_ref, out_other_ref, query_grad_ref, query_grad_other_ref, pair_grad_ref,
    scaled_ref, turned_scaled_ref, delta_ref, total_ref, move_ref,
):
    rows = out_ref.shape[0]
    wide = turned_grad_ref.shape[1]
    groups = wide // rows
    heads = groups // 2
    root = 1.0 / math.sqrt(HEAD)
    chip, last = bounds_ref[0], bounds_ref[4]
    total_ref[...] = jnp.zeros_like(total_ref)

    for group in range(groups):
        span = slice(group * rows, (group + 1) * rows)
        there = (group + heads) % groups
        theirs = slice(there * rows, (there + 1) * rows)
        own_top, other_top = stats_ref[TOP : TOP + 1, span], arrived_ref[TOP : TOP + 1, theirs]
        top = jnp.maximum(own_top, other_top)
        own_part, other_part = jnp.exp2(own_top - top), jnp.exp2(other_top - top)

        def whole(row):
            return (
                stats_ref[row : row + 1, span] * own_part
                + arrived_ref[row : row + 1, theirs] * other_part
            )

        inverse = 1.0 / whole(TOTAL)
        part = own_part * inverse
        delta_ref[:, span] = whole(INNER) * inverse * part
        result = acc_ref[:HEAD, span] * part
        column = slice(group % heads * HEAD, (group % heads + 1) * HEAD)
        to_ref = out_ref if group < heads else out_other_ref
        to_ref[:, column] = result.astype(jnp.bfloat16).T
        low = (turned_grad_ref[:, span].astype(jnp.float32) * part).astype(jnp.bfloat16)
        turned_scaled_ref[:, span] = low
        scaled_ref[span, :] = low.T

    def visit(back, unused):
        at = pl.ds(pl.multiple_of((chip - back) * rows, rows), rows)
        to = pl.ds(pl.multiple_of(back * rows, rows), rows)
        values = pairs_ref[at, HEAD:]
        turned_keys = pairs_ref[at, :HEAD].T
        for group in range(groups):
            span = slice(group * rows, (group + 1) * rows)
            prob_grad = matmul(values, turned_scaled_ref[:, span])
            move_ref[:, span] = (
                weights_ref[to, span].astype(jnp.float32) * (prob_grad - delta_ref[:, span])
            ).astype(jnp.bfloat16)
        pair_grad_ref[to, HEAD:] = matmul(weights_ref[to, :], scaled_ref[...]).astype(jnp.bfloat16)
        pair_grad_ref[to, :HEAD] = (matmul(move_ref[...], query_ref[...]) * root).astype(
            jnp.bfloat16
        )
        total_ref[...] += matmul(turned_keys, move_ref[...])
        return unused

    def unseen(back, unused):
        to = pl.ds(pl.multiple_of(back * rows, rows), rows)
        pair_grad_ref[to, :] = jnp.zeros((rows, 2 * HEAD), jnp.bfloat16)
        return unused

    lax.fori_loop(0, last + 1, visit, 0)
    lax.fori_loop(last + 1, pair_grad_ref.shape[0] // rows, unseen, 0)
    for group in range(groups):
        span = slice(group * rows, (group + 1) * rows)
        column = slice(group % heads * HEAD, (group % heads + 1) * HEAD)
        to_ref = query_grad_ref if group < heads else query_grad_other_ref
        to_ref[:, column] = (total_ref[:, span] * root).astype(jnp.bfloat16).T


def smem():
    return pl.BlockSpec(memory_space=pltpu.SMEM)


def vmem():
    return pl.BlockSpec(memory_space=pltpu.VMEM)


def swap_cores(value):
    return lax.ppermute(value, "core", [(0, 1), (1, 0)])


def attend(bounds, starts, queries, grads, pairs, slots, swap=swap_cores):
    rows, columns = queries[0].shape
    heads = columns // HEAD
    wide = 2 * heads * rows
    params = pltpu.CompilerParams(vmem_limit_bytes=40 << 20)
    turned = jnp.concatenate([turn(q) for q in queries], axis=1)
    turned_grad = jnp.concatenate([turn(g) for g in grads], axis=1)
    stacked = jnp.concatenate([stack(q) for q in queries], axis=0)
    weights, acc, stats = pl.pallas_call(
        forward_kernel,
        out_shape=(
            pltpu.VMEM((slots * rows, wide), jnp.bfloat16),
            jax.ShapeDtypeStruct((HEAD + 16, wide), jnp.float32),
            jax.ShapeDtypeStruct((8, wide), jnp.float32),
        ),
        in_specs=[smem()] + [vmem()] * 4,
        out_specs=(vmem(),) * 3,
        scratch_shapes=[
            pltpu.VMEM((slots * rows, wide), jnp.float32),
            pltpu.VMEM((8, wide), jnp.float32),
        ],
        compiler_params=params,
        name="attend_forward",
    )(bounds, starts, turned, pairs, turned_grad)
    arrived = swap(stats)
    half = jax.ShapeDtypeStruct((rows, columns), jnp.bfloat16)
    return pl.pallas_call(
        backward_kernel,
        out_shape=(half,) * 4 + (jax.ShapeDtypeStruct((slots * rows, 2 * HEAD), jnp.bfloat16),),
        in_specs=[smem()] + [vmem()] * 7,
        out_specs=(vmem(),) * 5,
        scratch_shapes=[
            pltpu.VMEM((wide, HEAD), jnp.bfloat16),
            pltpu.VMEM((HEAD, wide), jnp.bfloat16),
            pltpu.VMEM((1, wide), jnp.float32),
            pltpu.VMEM((HEAD, wide), jnp.float32),
            pltpu.VMEM((rows, wide), jnp.bfloat16),
        ],
        compiler_params=params,
        name="attend_backward",
    )(bounds, stats, arrived, acc, turned_grad, stacked, pairs, weights)


def turn(array):
    rows, columns = array.shape
    heads = columns // HEAD
    return array.reshape(rows, heads, HEAD).transpose(2, 1, 0).reshape(HEAD, heads * rows)


def stack(array):
    rows, columns = array.shape
    heads = columns // HEAD
    return array.reshape(rows, heads, HEAD).transpose(1, 0, 2).reshape(heads * rows, HEAD)


def block_bounds(lengths, chip, core, rows):
    own, other = 2 * chip + core, 2 * chip + 1 - core
    ends = jnp.cumsum(lengths)
    begins = ends - lengths

    def starts_of(positions):
        here = begins[:, None] <= positions[None, :]
        return jnp.max(jnp.where(here, begins[:, None], 0), axis=0)

    span = jnp.arange(rows, dtype=jnp.int32)
    starts = jnp.stack([starts_of(own * rows + span), starts_of(other * rows + span)])
    edges = starts_of(jnp.stack([2 * chip * rows, (2 * chip + 2) * rows - 1]))
    last = (own - edges[0] // rows) // 2
    clear = jnp.maximum((own - (edges[1] + rows - 1) // rows) // 2, 0)
    bounds = jnp.stack([chip, own, other, clear, last]).astype(jnp.int32)
    return bounds, starts[:, None, :]


def per_device(query, keys_values, doc_lengths, incoming_output_grad):
    chips = lax.axis_size("chip")
    query = query[0, :, 0, :]
    pairs = keys_values[0, :, 0, :]
    rows = query.shape[0]
    every_pair = lax.all_gather(pairs, "chip", axis=0, tiled=True)
    sections = lax.axis_size("pipe")
    arrived = lax.ppermute(
        incoming_output_grad, "pipe", [(s, (s - 1) % sections) for s in range(sections)]
    )
    grad = lax.all_to_all(arrived, "tensor", split_axis=2, concat_axis=1, tiled=True)[0, :, 0, :]
    bounds, starts = block_bounds(
        doc_lengths[0], lax.axis_index("chip"), lax.axis_index("core"), rows
    )
    reach = min((LONGEST + 2 * rows - 1) // (2 * rows), chips - 1)
    slots = reach + 1
    out, out_other, query_grad, query_grad_other, partial = attend(
        bounds, starts, (query, swap_cores(query)), (grad, swap_cores(grad)), every_pair, slots
    )

    def add(mine, theirs):
        return (mine.astype(jnp.float32) + theirs.astype(jnp.float32)).astype(jnp.bfloat16)

    out = add(out, swap_cores(out_other))
    query_grad = add(query_grad, swap_cores(query_grad_other))
    partial = partial.reshape(slots, rows, 2 * HEAD)
    sums = partial[0].astype(jnp.float32)
    for back in range(1, slots):
        sums += lax.ppermute(
            partial[back], "chip", [(c, c - back) for c in range(back, chips)]
        ).astype(jnp.float32)
    pair_grad = sums.astype(jnp.bfloat16)
    return (out[None, :, None, :], query_grad[None, :, None, :], pair_grad[None, :, None, :])


def solution(mesh):
    shape = mesh.devices.shape
    split = Mesh(
        mesh.devices.reshape((shape[0] // 2, 2) + shape[1:]), ("chip", "core", "tensor", "pipe")
    )
    dp = ("chip", "core")
    by_head = P("pipe", dp, "tensor", None)
    in_specs = (by_head, by_head, P("pipe", None), P("pipe", dp + ("tensor",), None, None))
    return jax.shard_map(
        per_device, mesh=split, in_specs=in_specs, out_specs=(by_head,) * 3, check_vma=False
    )
```

```python
import functools
import math

import jax
import jax.numpy as jnp
from jax import lax
from jax.experimental import pallas as pl
from jax.experimental.pallas import tpu as pltpu
from jax.sharding import Mesh, PartitionSpec as P

NEG_LARGE = -1e30
LOG2E = math.log2(math.e)
HEAD = 128
LONGEST = 3072
EXTRA = 16


def matmul(left, right):
    return jnp.dot(left, right, preferred_element_type=jnp.float32)


def fold(array):
    return array.reshape(array.shape[0] // 8, 8, array.shape[1])


def forward_kernel(
    bounds_ref, starts_ref, turned_ref, pairs_ref,
    kept_ref, acc_ref, stats_ref, sent_ref, scores_ref, top_ref, weights_ref, kept_sem,
):
    rows = starts_ref.shape[2]
    groups = turned_ref.shape[1] // rows
    heads = groups // 2
    scale = LOG2E / math.sqrt(HEAD)
    chip, own, clear, last = bounds_ref[0], bounds_ref[1], bounds_ref[3], bounds_ref[4]
    top_ref[...] = jnp.full_like(top_ref, NEG_LARGE)
    acc_ref[...] = jnp.zeros_like(acc_ref)

    def measure(back, masked):
        at = pl.ds(pl.multiple_of((chip - back) * rows, rows), rows)
        to = pl.ds(pl.multiple_of(back * rows, rows), rows)
        keys = pairs_ref[at, :HEAD]
        allowed = []
        if masked:
            key_pos = (own - 2 * back) * rows + lax.broadcasted_iota(jnp.int32, (rows, rows), 0)
            across = lax.broadcasted_iota(jnp.int32, (rows, rows), 1)
            for slot in range(2):
                query_pos = bounds_ref[1 + slot] * rows + across
                allowed.append((key_pos <= query_pos) & (key_pos >= starts_ref[slot]))
        for group in range(groups):
            span = slice(group * rows, (group + 1) * rows)
            scores = matmul(keys, turned_ref[:, span])
            if masked:
                scores = jnp.where(allowed[group // heads], scores, NEG_LARGE)
            scores_ref[to, span] = scores
            top_ref[:, span] = jnp.maximum(top_ref[:, span], jnp.max(fold(scores), axis=0))

    def masked(step, unused):
        measure(jnp.where(step == 0, 0, clear + step), True)
        return unused

    def plain(back, unused):
        measure(back, False)
        return unused

    lax.fori_loop(0, last - clear + 1, masked, 0)
    lax.fori_loop(1, clear + 1, plain, 0)
    top = jnp.max(top_ref[...], axis=0, keepdims=True) * scale
    top_ref[...] = jnp.broadcast_to(top, top_ref.shape)

    def weigh(back, unused):
        at = pl.ds(pl.multiple_of((chip - back) * rows, rows), rows)
        to = pl.ds(pl.multiple_of(back * rows, rows), rows)
        turned_values = jnp.concatenate(
            [pairs_ref[at, HEAD:].T, jnp.ones((16, rows), jnp.bfloat16)], axis=0
        )
        for group in range(groups):
            span = slice(group * rows, (group + 1) * rows)
            weights_ref[to, span] = jnp.exp2(
                scores_ref[to, span] * scale - top_ref[:1, span]
            ).astype(jnp.bfloat16)
        keep(back).start()
        acc_ref[...] += matmul(turned_values, weights_ref[to, :])
        return unused

    def keep(back):
        to = pl.ds(pl.multiple_of(back * rows, rows), rows)
        return pltpu.make_async_copy(weights_ref.at[to], kept_ref.at[to], kept_sem.at[back])

    def kept(back, unused):
        keep(back).wait()
        return unused

    lax.fori_loop(0, last + 1, weigh, 0)
    totals = acc_ref[HEAD : HEAD + 1, :]
    log_totals = top_ref[:1, :] + jnp.log2(totals)
    stats_ref[...] = jnp.concatenate([top_ref[:1, :], log_totals] + [top] * 6, axis=0)
    parts, rest = [], log_totals
    for _ in range(3):
        parts.append(rest.astype(jnp.bfloat16))
        rest = rest - parts[-1].astype(jnp.float32)
    sent_ref[HEAD:, :] = jnp.concatenate(
        parts + [jnp.zeros((EXTRA - 3, totals.shape[1]), jnp.bfloat16)], axis=0
    )
    inverse = 1.0 / totals
    for group in range(groups):
        span = slice(group * rows, (group + 1) * rows)
        result = acc_ref[:HEAD, span] * inverse[:, span]
        acc_ref[:HEAD, span] = result
        sent_ref[:HEAD, span] = result.astype(jnp.bfloat16)
    lax.fori_loop(0, last + 1, kept, 0)


def fetch(slot, kept_ref, weights_ref, kept_sem, rows):
    def copy(back):
        of = pl.ds(pl.multiple_of(back * rows, rows), rows)
        to = pl.ds(pl.multiple_of((back - slot) * rows, rows), rows)
        return pltpu.make_async_copy(kept_ref.at[of], weights_ref.at[to], kept_sem.at[back - slot])

    return copy


def fetch_all(first, stop, copy):
    def start(back, unused):
        copy(back).start()
        return unused

    lax.fori_loop(first, stop, start, 0)


def accumulate(
    first, stop, chip, pairs_ref, weights_ref, copy, query_ref,
    scaled_ref, turned_scaled_ref, delta_ref, total_ref, move_ref, pair_grad_ref, slot,
):
    rows = move_ref.shape[0]
    groups = move_ref.shape[1] // rows
    root = 1.0 / math.sqrt(HEAD)

    def visit(back, unused):
        at = pl.ds(pl.multiple_of((chip - back) * rows, rows), rows)
        to = pl.ds(pl.multiple_of((back - slot) * rows, rows), rows)
        values = pairs_ref[at, HEAD:]
        turned_keys = pairs_ref[at, :HEAD].T
        copy(back).wait()
        for group in range(groups):
            span = slice(group * rows, (group + 1) * rows)
            prob_grad = matmul(values, turned_scaled_ref[:, span])
            move_ref[:, span] = (
                weights_ref[to, span].astype(jnp.float32) * (prob_grad - delta_ref[:, span])
            ).astype(jnp.bfloat16)
        pair_grad_ref[to, HEAD:] = matmul(weights_ref[to, :], scaled_ref[...]).astype(jnp.bfloat16)
        pair_grad_ref[to, :HEAD] = (matmul(move_ref[...], query_ref[...]) * root).astype(
            jnp.bfloat16
        )
        total_ref[...] += matmul(turned_keys, move_ref[...])
        return unused

    def unseen(back, unused):
        to = pl.ds(pl.multiple_of((back - slot) * rows, rows), rows)
        pair_grad_ref[to, :] = jnp.zeros((rows, 2 * HEAD), jnp.bfloat16)
        return unused

    lax.fori_loop(first, stop, visit, 0)
    lax.fori_loop(jnp.maximum(first, stop), slot + pair_grad_ref.shape[0] // rows, unseen, 0)


def hand_out(pair_grad_ref, block_refs):
    rows = block_refs[0].shape[0]
    for at, block_ref in enumerate(block_refs):
        block_ref[...] = pair_grad_ref[at * rows : (at + 1) * rows, :]


def backward_far_kernel(
    bounds_ref, stats_ref, arrived_ref, acc_ref, turned_grad_ref, query_ref, pairs_ref, kept_ref,
    out_ref, scaled_ref, turned_scaled_ref, delta_ref, total_ref, *rest, split,
):
    *block_refs, move_ref, pair_grad_ref, weights_ref, kept_sem = rest
    rows = out_ref.shape[0]
    groups = turned_grad_ref.shape[1] // rows
    heads = groups // 2
    copy = fetch(split, kept_ref, weights_ref, kept_sem, rows)
    fetch_all(split, bounds_ref[4] + 1, copy)
    total_ref[...] = jnp.zeros_like(total_ref)
    for group in range(groups):
        span = slice(group * rows, (group + 1) * rows)
        there = (group + heads) % groups
        theirs = slice(there * rows, (there + 1) * rows)
        other_log = arrived_ref[HEAD : HEAD + 1, theirs].astype(jnp.float32)
        for part in range(1, 3):
            other_log += arrived_ref[HEAD + part : HEAD + part + 1, theirs].astype(jnp.float32)
        own_top, own_log = stats_ref[0:1, span], stats_ref[1:2, span]
        most = jnp.maximum(own_log, other_log)
        log_totals = most + jnp.log2(jnp.exp2(own_log - most) + jnp.exp2(other_log - most))
        result = acc_ref[:HEAD, span] * jnp.exp2(own_log - log_totals) + arrived_ref[
            :HEAD, theirs
        ].astype(jnp.float32) * jnp.exp2(other_log - log_totals)
        result = result.astype(jnp.bfloat16)
        if group < heads:
            out_ref[:, group * HEAD : (group + 1) * HEAD] = result.T
        scaled = turned_grad_ref[:, span].astype(jnp.float32) * jnp.exp2(own_top - log_totals)
        delta_ref[:, span] = jnp.sum(result.astype(jnp.float32) * scaled, axis=0, keepdims=True)
        low = scaled.astype(jnp.bfloat16)
        turned_scaled_ref[:, span] = low
        scaled_ref[span, :] = low.T
    accumulate(
        split, bounds_ref[4] + 1, bounds_ref[0], pairs_ref, weights_ref, copy, query_ref,
        scaled_ref, turned_scaled_ref, delta_ref, total_ref, move_ref, pair_grad_ref, split,
    )
    hand_out(pair_grad_ref, block_refs)


def backward_near_kernel(
    bounds_ref, scaled_ref, turned_scaled_ref, delta_ref, begun_ref, query_ref, pairs_ref,
    kept_ref, query_grad_ref, query_grad_other_ref, *rest,
):
    *block_refs, total_ref, move_ref, pair_grad_ref, weights_ref, kept_sem = rest
    rows = query_grad_ref.shape[0]
    groups = turned_scaled_ref.shape[1] // rows
    heads = groups // 2
    root = 1.0 / math.sqrt(HEAD)
    slots = pair_grad_ref.shape[0] // rows
    stop = jnp.minimum(bounds_ref[4] + 1, slots)
    copy = fetch(0, kept_ref, weights_ref, kept_sem, rows)
    fetch_all(0, stop, copy)
    total_ref[...] = begun_ref[...]
    accumulate(
        0, stop, bounds_ref[0], pairs_ref, weights_ref, copy, query_ref,
        scaled_ref, turned_scaled_ref, delta_ref, total_ref, move_ref, pair_grad_ref, 0,
    )
    hand_out(pair_grad_ref, block_refs)
    for group in range(groups):
        span = slice(group * rows, (group + 1) * rows)
        column = slice(group % heads * HEAD, (group % heads + 1) * HEAD)
        to_ref = query_grad_ref if group < heads else query_grad_other_ref
        to_ref[:, column] = (total_ref[:, span] * root).astype(jnp.bfloat16).T


def smem():
    return pl.BlockSpec(memory_space=pltpu.SMEM)


def vmem():
    return pl.BlockSpec(memory_space=pltpu.VMEM)


def hbm():
    return pl.BlockSpec(memory_space=pltpu.HBM)


def swap_cores(value):
    return lax.ppermute(value, "core", [(0, 1), (1, 0)])


def cost(blocks, rows, wide, matmuls):
    return pl.CostEstimate(
        flops=2 * matmuls * blocks * rows * wide * HEAD,
        transcendentals=0,
        bytes_accessed=2 * blocks * rows * wide,
    )


def attend(bounds, starts, queries, grads, pairs, slots, split, send, swap=swap_cores):
    rows, columns = queries[0].shape
    heads = columns // HEAD
    wide = 2 * heads * rows
    turned = jnp.concatenate([turn(q) for q in queries], axis=1)
    turned_grad = jnp.concatenate([turn(g) for g in grads], axis=1)
    stacked = jnp.concatenate([stack(q) for q in queries], axis=0)
    pairs, turned, turned_grad, stacked = lax.optimization_barrier(
        (pairs, turned, turned_grad, stacked)
    )
    weights, acc, stats, sent = pl.pallas_call(
        forward_kernel,
        out_shape=(
            pltpu.HBM((slots * rows, wide), jnp.bfloat16),
            jax.ShapeDtypeStruct((HEAD + EXTRA, wide), jnp.float32),
            jax.ShapeDtypeStruct((8, wide), jnp.float32),
            jax.ShapeDtypeStruct((HEAD + EXTRA, wide), jnp.bfloat16),
        ),
        in_specs=[smem()] + [vmem()] * 3,
        out_specs=(hbm(),) + (vmem(),) * 3,
        scratch_shapes=[
            pltpu.VMEM((slots * rows, wide), jnp.float32),
            pltpu.VMEM((8, wide), jnp.float32),
            pltpu.VMEM((slots * rows, wide), jnp.bfloat16),
            pltpu.SemaphoreType.DMA((slots,)),
        ],
        compiler_params=pltpu.CompilerParams(vmem_limit_bytes=36 << 20),
        cost_estimate=cost(slots, rows, wide, 2),
        name="attend_forward",
    )(bounds, starts, turned, pairs)
    weights = pltpu.with_memory_space_constraint(weights, pltpu.HBM)
    arrived = swap(sent)
    half = jax.ShapeDtypeStruct((rows, columns), jnp.bfloat16)
    params = pltpu.CompilerParams(vmem_limit_bytes=20 << 20)
    move = pltpu.VMEM((rows, wide), jnp.bfloat16)

    def held(blocks):
        return [
            pltpu.VMEM((blocks * rows, 2 * HEAD), jnp.bfloat16),
            pltpu.VMEM((blocks * rows, wide), jnp.bfloat16),
            pltpu.SemaphoreType.DMA((blocks,)),
        ]

    block = jax.ShapeDtypeStruct((rows, 2 * HEAD), jnp.bfloat16)
    out, scaled, turned_scaled, delta, total, *far = pl.pallas_call(
        functools.partial(backward_far_kernel, split=split),
        out_shape=(
            half,
            jax.ShapeDtypeStruct((wide, HEAD), jnp.bfloat16),
            jax.ShapeDtypeStruct((HEAD, wide), jnp.bfloat16),
            jax.ShapeDtypeStruct((1, wide), jnp.float32),
            jax.ShapeDtypeStruct((HEAD, wide), jnp.float32),
        )
        + (block,) * (slots - split),
        in_specs=[smem()] + [vmem()] * 6 + [hbm()],
        out_specs=(vmem(),) * (5 + slots - split),
        scratch_shapes=[move] + held(slots - split),
        compiler_params=params,
        cost_estimate=cost(slots - split, rows, wide, 4),
        name="attend_backward_far",
    )(bounds, stats, arrived, acc, turned_grad, stacked, pairs, weights)
    sent_far = send(far)
    query_grad, query_grad_other, *near = pl.pallas_call(
        backward_near_kernel,
        out_shape=(half, half) + (block,) * split,
        in_specs=[smem()] + [vmem()] * 6 + [hbm()],
        out_specs=(vmem(),) * (2 + split),
        scratch_shapes=[pltpu.VMEM((HEAD, wide), jnp.float32), move] + held(split),
        compiler_params=params,
        cost_estimate=cost(split, rows, wide, 4),
        name="attend_backward_near",
    )(bounds, scaled, turned_scaled, delta, total, stacked, pairs, weights)
    return out, query_grad, query_grad_other, near, sent_far


def turn(array):
    rows, columns = array.shape
    heads = columns // HEAD
    return array.reshape(rows, heads, HEAD).transpose(2, 1, 0).reshape(HEAD, heads * rows)


def stack(array):
    rows, columns = array.shape
    heads = columns // HEAD
    return array.reshape(rows, heads, HEAD).transpose(1, 0, 2).reshape(heads * rows, HEAD)


def block_bounds(lengths, chip, core, rows):
    own, other = 2 * chip + core, 2 * chip + 1 - core
    ends = jnp.cumsum(lengths)
    begins = ends - lengths

    def starts_of(positions):
        here = begins[:, None] <= positions[None, :]
        return jnp.max(jnp.where(here, begins[:, None], 0), axis=0)

    span = jnp.arange(rows, dtype=jnp.int32)
    starts = jnp.stack([starts_of(own * rows + span), starts_of(other * rows + span)])
    edges = starts_of(jnp.stack([2 * chip * rows, (2 * chip + 2) * rows - 1]))
    last = (own - edges[0] // rows) // 2
    clear = jnp.maximum((own - (edges[1] + rows - 1) // rows) // 2, 0)
    bounds = jnp.stack([chip, own, other, clear, last]).astype(jnp.int32)
    return bounds, starts[:, None, :]


def per_device(query, keys_values, doc_lengths, incoming_output_grad):
    chips = lax.axis_size("chip")
    query = query[0, :, 0, :]
    pairs = keys_values[0, :, 0, :]
    rows = query.shape[0]
    every_pair = lax.all_gather(pairs, "chip", axis=0, tiled=True)
    sections = lax.axis_size("pipe")
    arrived = lax.ppermute(
        incoming_output_grad, "pipe", [(s, (s - 1) % sections) for s in range(sections)]
    )
    grad = lax.all_to_all(arrived, "tensor", split_axis=2, concat_axis=1, tiled=True)[0, :, 0, :]
    bounds, starts = block_bounds(
        doc_lengths[0], lax.axis_index("chip"), lax.axis_index("core"), rows
    )
    reach = min((LONGEST + 2 * rows - 1) // (2 * rows), chips - 1)
    slots = reach + 1
    split = (slots + 1) // 2

    def send(blocks, first):
        return [
            lax.ppermute(block, "chip", [(c, c - first - at) for c in range(first + at, chips)])
            for at, block in enumerate(blocks)
        ]

    out, query_grad, query_grad_other, near, far = attend(
        bounds, starts, (query, swap_cores(query)), (grad, swap_cores(grad)), every_pair, slots,
        split, functools.partial(send, first=split),
    )
    near, far = lax.optimization_barrier((near, far))
    sums = near[0].astype(jnp.float32)
    for sent in far + send(near[1:], 1):
        sums += sent.astype(jnp.float32)
    pair_grad = sums.astype(jnp.bfloat16)
    query_grad = query_grad.astype(jnp.float32) + swap_cores(query_grad_other).astype(jnp.float32)
    query_grad = query_grad.astype(jnp.bfloat16)
    return (out[None, :, None, :], query_grad[None, :, None, :], pair_grad[None, :, None, :])


def solution(mesh):
    shape = mesh.devices.shape
    split = Mesh(
        mesh.devices.reshape((shape[0] // 2, 2) + shape[1:]), ("chip", "core", "tensor", "pipe")
    )
    dp = ("chip", "core")
    by_head = P("pipe", dp, "tensor", None)
    in_specs = (by_head, by_head, P("pipe", None), P("pipe", dp + ("tensor",), None, None))
    return jax.shard_map(
        per_device, mesh=split, in_specs=in_specs, out_specs=(by_head,) * 3, check_vma=False
    )
```

```python
import functools
import math

import jax
import jax.numpy as jnp
from jax import lax
from jax.experimental import pallas as pl
from jax.experimental.pallas import tpu as pltpu
from jax.sharding import Mesh, PartitionSpec as P

NEG_LARGE = -1e30
LOG2E = math.log2(math.e)
HEAD = 128
LONGEST = 3072
EXTRA = 16


def matmul(left, right):
    return jnp.dot(left, right, preferred_element_type=jnp.float32)


def fold(array):
    return array.reshape(array.shape[0] // 8, 8, array.shape[1])


def forward_kernel(
    bounds_ref, starts_ref, turned_ref, pairs_ref,
    kept_ref, acc_ref, stats_ref, sent_ref, scores_ref, top_ref, weights_ref, kept_sem,
):
    rows = starts_ref.shape[2]
    groups = turned_ref.shape[1] // rows
    heads = groups // 2
    scale = LOG2E / math.sqrt(HEAD)
    chip, own, clear, last = bounds_ref[0], bounds_ref[1], bounds_ref[3], bounds_ref[4]
    top_ref[...] = jnp.full_like(top_ref, NEG_LARGE)
    acc_ref[...] = jnp.zeros_like(acc_ref)

    def measure(back, masked):
        at = pl.ds(pl.multiple_of((chip - back) * rows, rows), rows)
        to = pl.ds(pl.multiple_of(back * rows, rows), rows)
        keys = pairs_ref[at, :HEAD]
        allowed = []
        if masked:
            key_pos = (own - 2 * back) * rows + lax.broadcasted_iota(jnp.int32, (rows, rows), 0)
            across = lax.broadcasted_iota(jnp.int32, (rows, rows), 1)
            for slot in range(2):
                query_pos = bounds_ref[1 + slot] * rows + across
                allowed.append((key_pos <= query_pos) & (key_pos >= starts_ref[slot]))
        for group in range(groups):
            span = slice(group * rows, (group + 1) * rows)
            scores = matmul(keys, turned_ref[:, span])
            if masked:
                scores = jnp.where(allowed[group // heads], scores, NEG_LARGE)
            scores_ref[to, span] = scores
            top_ref[:, span] = jnp.maximum(top_ref[:, span], jnp.max(fold(scores), axis=0))

    def masked(step, unused):
        measure(jnp.where(step == 0, 0, clear + step), True)
        return unused

    def plain(back, unused):
        measure(back, False)
        return unused

    lax.fori_loop(0, last - clear + 1, masked, 0)
    lax.fori_loop(1, clear + 1, plain, 0)
    top = jnp.max(top_ref[...], axis=0, keepdims=True) * scale
    top_ref[...] = jnp.broadcast_to(top, top_ref.shape)

    def weigh(back, unused):
        at = pl.ds(pl.multiple_of((chip - back) * rows, rows), rows)
        to = pl.ds(pl.multiple_of(back * rows, rows), rows)
        turned_values = jnp.concatenate(
            [pairs_ref[at, HEAD:].T, jnp.ones((16, rows), jnp.bfloat16)], axis=0
        )
        for group in range(groups):
            span = slice(group * rows, (group + 1) * rows)
            weights_ref[to, span] = jnp.exp2(
                scores_ref[to, span] * scale - top_ref[:1, span]
            ).astype(jnp.bfloat16)
        keep(back).start()
        acc_ref[...] += matmul(turned_values, weights_ref[to, :])
        return unused

    def keep(back):
        to = pl.ds(pl.multiple_of(back * rows, rows), rows)
        return pltpu.make_async_copy(weights_ref.at[to], kept_ref.at[to], kept_sem.at[back])

    def kept(back, unused):
        keep(back).wait()
        return unused

    lax.fori_loop(0, last + 1, weigh, 0)
    totals = acc_ref[HEAD : HEAD + 1, :]
    log_totals = top_ref[:1, :] + jnp.log2(totals)
    stats_ref[...] = jnp.concatenate([top_ref[:1, :], log_totals] + [top] * 6, axis=0)
    parts, rest = [], log_totals
    for _ in range(3):
        parts.append(rest.astype(jnp.bfloat16))
        rest = rest - parts[-1].astype(jnp.float32)
    sent_ref[HEAD:, :] = jnp.concatenate(
        parts + [jnp.zeros((EXTRA - 3, totals.shape[1]), jnp.bfloat16)], axis=0
    )
    inverse = 1.0 / totals
    for group in range(groups):
        span = slice(group * rows, (group + 1) * rows)
        result = acc_ref[:HEAD, span] * inverse[:, span]
        acc_ref[:HEAD, span] = result
        sent_ref[:HEAD, span] = result.astype(jnp.bfloat16)
    lax.fori_loop(0, last + 1, kept, 0)


def fetch(slot, kept_ref, weights_ref, kept_sem, rows):
    def copy(back):
        of = pl.ds(pl.multiple_of(back * rows, rows), rows)
        to = pl.ds(pl.multiple_of((back - slot) * rows, rows), rows)
        return pltpu.make_async_copy(kept_ref.at[of], weights_ref.at[to], kept_sem.at[back - slot])

    return copy


def fetch_all(first, stop, copy):
    def start(back, unused):
        copy(back).start()
        return unused

    lax.fori_loop(first, stop, start, 0)


def accumulate(
    first, stop, chip, pairs_ref, weights_ref, copy, query_ref,
    scaled_ref, turned_scaled_ref, delta_ref, total_ref, move_ref, pair_grad_ref, slot,
):
    rows = move_ref.shape[0]
    groups = move_ref.shape[1] // rows
    root = 1.0 / math.sqrt(HEAD)

    def visit(back, unused):
        at = pl.ds(pl.multiple_of((chip - back) * rows, rows), rows)
        to = pl.ds(pl.multiple_of((back - slot) * rows, rows), rows)
        values = pairs_ref[at, HEAD:]
        turned_keys = pairs_ref[at, :HEAD].T
        copy(back).wait()
        for group in range(groups):
            span = slice(group * rows, (group + 1) * rows)
            prob_grad = matmul(values, turned_scaled_ref[:, span])
            move_ref[:, span] = (
                weights_ref[to, span].astype(jnp.float32) * (prob_grad - delta_ref[:, span])
            ).astype(jnp.bfloat16)
        pair_grad_ref[to, HEAD:] = matmul(weights_ref[to, :], scaled_ref[...]).astype(jnp.bfloat16)
        pair_grad_ref[to, :HEAD] = (matmul(move_ref[...], query_ref[...]) * root).astype(
            jnp.bfloat16
        )
        total_ref[...] += matmul(turned_keys, move_ref[...])
        return unused

    def unseen(back, unused):
        to = pl.ds(pl.multiple_of((back - slot) * rows, rows), rows)
        pair_grad_ref[to, :] = jnp.zeros((rows, 2 * HEAD), jnp.bfloat16)
        return unused

    lax.fori_loop(first, stop, visit, 0)
    lax.fori_loop(jnp.maximum(first, stop), slot + pair_grad_ref.shape[0] // rows, unseen, 0)


def hand_out(pair_grad_ref, block_refs):
    rows = block_refs[0].shape[0]
    for at, block_ref in enumerate(block_refs):
        block_ref[...] = pair_grad_ref[at * rows : (at + 1) * rows, :]


def backward_far_kernel(
    bounds_ref, stats_ref, arrived_ref, acc_ref, turned_grad_ref, query_ref, pairs_ref, kept_ref,
    out_ref, scaled_ref, turned_scaled_ref, delta_ref, total_ref, *rest, split,
):
    *block_refs, move_ref, pair_grad_ref, weights_ref, kept_sem = rest
    rows = out_ref.shape[0]
    groups = turned_grad_ref.shape[1] // rows
    heads = groups // 2
    copy = fetch(split, kept_ref, weights_ref, kept_sem, rows)
    fetch_all(split, bounds_ref[4] + 1, copy)
    total_ref[...] = jnp.zeros_like(total_ref)
    for group in range(groups):
        span = slice(group * rows, (group + 1) * rows)
        there = (group + heads) % groups
        theirs = slice(there * rows, (there + 1) * rows)
        other_log = arrived_ref[HEAD : HEAD + 1, theirs].astype(jnp.float32)
        for part in range(1, 3):
            other_log += arrived_ref[HEAD + part : HEAD + part + 1, theirs].astype(jnp.float32)
        own_top, own_log = stats_ref[0:1, span], stats_ref[1:2, span]
        most = jnp.maximum(own_log, other_log)
        log_totals = most + jnp.log2(jnp.exp2(own_log - most) + jnp.exp2(other_log - most))
        result = acc_ref[:HEAD, span] * jnp.exp2(own_log - log_totals) + arrived_ref[
            :HEAD, theirs
        ].astype(jnp.float32) * jnp.exp2(other_log - log_totals)
        result = result.astype(jnp.bfloat16)
        if group < heads:
            out_ref[:, group * HEAD : (group + 1) * HEAD] = result.T
        scaled = turned_grad_ref[:, span].astype(jnp.float32) * jnp.exp2(own_top - log_totals)
        delta_ref[:, span] = jnp.sum(result.astype(jnp.float32) * scaled, axis=0, keepdims=True)
        low = scaled.astype(jnp.bfloat16)
        turned_scaled_ref[:, span] = low
        scaled_ref[span, :] = low.T
    accumulate(
        split, bounds_ref[4] + 1, bounds_ref[0], pairs_ref, weights_ref, copy, query_ref,
        scaled_ref, turned_scaled_ref, delta_ref, total_ref, move_ref, pair_grad_ref, split,
    )
    hand_out(pair_grad_ref, block_refs)


def backward_near_kernel(
    bounds_ref, scaled_ref, turned_scaled_ref, delta_ref, begun_ref, query_ref, pairs_ref,
    kept_ref, query_grad_ref, query_grad_other_ref, *rest,
):
    *block_refs, total_ref, move_ref, pair_grad_ref, weights_ref, kept_sem = rest
    rows = query_grad_ref.shape[0]
    groups = turned_scaled_ref.shape[1] // rows
    heads = groups // 2
    root = 1.0 / math.sqrt(HEAD)
    slots = pair_grad_ref.shape[0] // rows
    stop = jnp.minimum(bounds_ref[4] + 1, slots)
    copy = fetch(0, kept_ref, weights_ref, kept_sem, rows)
    fetch_all(0, stop, copy)
    total_ref[...] = begun_ref[...]
    accumulate(
        0, stop, bounds_ref[0], pairs_ref, weights_ref, copy, query_ref,
        scaled_ref, turned_scaled_ref, delta_ref, total_ref, move_ref, pair_grad_ref, 0,
    )
    hand_out(pair_grad_ref, block_refs)
    for group in range(groups):
        span = slice(group * rows, (group + 1) * rows)
        column = slice(group % heads * HEAD, (group % heads + 1) * HEAD)
        to_ref = query_grad_ref if group < heads else query_grad_other_ref
        to_ref[:, column] = (total_ref[:, span] * root).astype(jnp.bfloat16).T


def smem():
    return pl.BlockSpec(memory_space=pltpu.SMEM)


def vmem():
    return pl.BlockSpec(memory_space=pltpu.VMEM)


def hbm():
    return pl.BlockSpec(memory_space=pltpu.HBM)


def swap_cores(value):
    return lax.ppermute(value, "core", [(0, 1), (1, 0)])


def cost(blocks, rows, wide, matmuls):
    return pl.CostEstimate(
        flops=2 * matmuls * blocks * rows * wide * HEAD,
        transcendentals=0,
        bytes_accessed=2 * blocks * rows * wide,
    )


def attend(bounds, starts, queries, grads, pairs, slots, split, send, swap=swap_cores):
    rows, columns = queries[0].shape
    heads = columns // HEAD
    wide = 2 * heads * rows
    turned = jnp.concatenate([turn(q) for q in queries], axis=1)
    turned_grad = jnp.concatenate([turn(g) for g in grads], axis=1)
    stacked = jnp.concatenate([stack(q) for q in queries], axis=0)
    pairs, turned, turned_grad, stacked = lax.optimization_barrier(
        (pairs, turned, turned_grad, stacked)
    )
    weights, acc, stats, sent = pl.pallas_call(
        forward_kernel,
        out_shape=(
            pltpu.HBM((slots * rows, wide), jnp.bfloat16),
            jax.ShapeDtypeStruct((HEAD + EXTRA, wide), jnp.float32),
            jax.ShapeDtypeStruct((8, wide), jnp.float32),
            jax.ShapeDtypeStruct((HEAD + EXTRA, wide), jnp.bfloat16),
        ),
        in_specs=[smem()] + [vmem()] * 3,
        out_specs=(hbm(),) + (vmem(),) * 3,
        scratch_shapes=[
            pltpu.VMEM((slots * rows, wide), jnp.float32),
            pltpu.VMEM((8, wide), jnp.float32),
            pltpu.VMEM((slots * rows, wide), jnp.bfloat16),
            pltpu.SemaphoreType.DMA((slots,)),
        ],
        compiler_params=pltpu.CompilerParams(vmem_limit_bytes=36 << 20),
        cost_estimate=cost(slots, rows, wide, 2),
        name="attend_forward",
    )(bounds, starts, turned, pairs)
    weights = pltpu.with_memory_space_constraint(weights, pltpu.HBM)
    arrived = swap(sent)
    half = jax.ShapeDtypeStruct((rows, columns), jnp.bfloat16)
    params = pltpu.CompilerParams(vmem_limit_bytes=20 << 20)
    move = pltpu.VMEM((rows, wide), jnp.bfloat16)

    def held(blocks):
        return [
            pltpu.VMEM((blocks * rows, 2 * HEAD), jnp.bfloat16),
            pltpu.VMEM((blocks * rows, wide), jnp.bfloat16),
            pltpu.SemaphoreType.DMA((blocks,)),
        ]

    block = jax.ShapeDtypeStruct((rows, 2 * HEAD), jnp.bfloat16)
    out, scaled, turned_scaled, delta, total, *far = pl.pallas_call(
        functools.partial(backward_far_kernel, split=split),
        out_shape=(
            half,
            jax.ShapeDtypeStruct((wide, HEAD), jnp.bfloat16),
            jax.ShapeDtypeStruct((HEAD, wide), jnp.bfloat16),
            jax.ShapeDtypeStruct((1, wide), jnp.float32),
            jax.ShapeDtypeStruct((HEAD, wide), jnp.float32),
        )
        + (block,) * (slots - split),
        in_specs=[smem()] + [vmem()] * 6 + [hbm()],
        out_specs=(vmem(),) * (5 + slots - split),
        scratch_shapes=[move] + held(slots - split),
        compiler_params=params,
        cost_estimate=cost(slots - split, rows, wide, 4),
        name="attend_backward_far",
    )(bounds, stats, arrived, acc, turned_grad, stacked, pairs, weights)
    sent_far = send(far)
    query_grad, query_grad_other, *near = pl.pallas_call(
        backward_near_kernel,
        out_shape=(half, half) + (block,) * split,
        in_specs=[smem()] + [vmem()] * 6 + [hbm()],
        out_specs=(vmem(),) * (2 + split),
        scratch_shapes=[pltpu.VMEM((HEAD, wide), jnp.float32), move] + held(split),
        compiler_params=params,
        cost_estimate=cost(split, rows, wide, 4),
        name="attend_backward_near",
    )(bounds, scaled, turned_scaled, delta, total, stacked, pairs, weights)
    return out, query_grad, query_grad_other, near, sent_far


def turn(array):
    rows, columns = array.shape
    heads = columns // HEAD
    return array.reshape(rows, heads, HEAD).transpose(2, 1, 0).reshape(HEAD, heads * rows)


def stack(array):
    rows, columns = array.shape
    heads = columns // HEAD
    return array.reshape(rows, heads, HEAD).transpose(1, 0, 2).reshape(heads * rows, HEAD)


def block_bounds(lengths, chip, core, rows):
    own, other = 2 * chip + core, 2 * chip + 1 - core
    ends = jnp.cumsum(lengths)
    begins = ends - lengths

    def starts_of(positions):
        here = begins[:, None] <= positions[None, :]
        return jnp.max(jnp.where(here, begins[:, None], 0), axis=0)

    span = jnp.arange(rows, dtype=jnp.int32)
    starts = jnp.stack([starts_of(own * rows + span), starts_of(other * rows + span)])
    edges = starts_of(jnp.stack([2 * chip * rows, (2 * chip + 2) * rows - 1]))
    last = (own - edges[0] // rows) // 2
    clear = jnp.maximum((own - (edges[1] + rows - 1) // rows) // 2, 0)
    bounds = jnp.stack([chip, own, other, clear, last]).astype(jnp.int32)
    return bounds, starts[:, None, :]


def per_device(query, keys_values, doc_lengths, incoming_output_grad):
    chips = lax.axis_size("chip")
    query = query[0, :, 0, :]
    pairs = keys_values[0, :, 0, :]
    rows = query.shape[0]
    every_pair = lax.all_gather(pairs, "chip", axis=0, tiled=True)
    sections = lax.axis_size("pipe")
    arrived = lax.ppermute(
        incoming_output_grad, "pipe", [(s, (s - 1) % sections) for s in range(sections)]
    )
    grad = lax.all_to_all(arrived, "tensor", split_axis=2, concat_axis=1, tiled=True)[0, :, 0, :]
    bounds, starts = block_bounds(
        doc_lengths[0], lax.axis_index("chip"), lax.axis_index("core"), rows
    )
    reach = min((LONGEST + 2 * rows - 1) // (2 * rows), chips - 1)
    slots = reach + 1
    split = (slots + 1) // 2

    def send(blocks, first):
        return [
            lax.ppermute(block, "chip", [(c, c - first - at) for c in range(first + at, chips)])
            for at, block in enumerate(blocks)
        ]

    out, query_grad, query_grad_other, near, far = attend(
        bounds, starts, (query, swap_cores(query)), (grad, swap_cores(grad)), every_pair, slots,
        split, functools.partial(send, first=split),
    )
    sums = near[0].astype(jnp.float32)
    for sent in far:
        sums += sent.astype(jnp.float32)
    sums = lax.optimization_barrier(sums)
    for sent in send(near[1:], 1):
        sums += sent.astype(jnp.float32)
    pair_grad = sums.astype(jnp.bfloat16)
    query_grad = query_grad.astype(jnp.float32) + swap_cores(query_grad_other).astype(jnp.float32)
    query_grad = query_grad.astype(jnp.bfloat16)
    return (out[None, :, None, :], query_grad[None, :, None, :], pair_grad[None, :, None, :])


def solution(mesh):
    shape = mesh.devices.shape
    split = Mesh(
        mesh.devices.reshape((shape[0] // 2, 2) + shape[1:]), ("chip", "core", "tensor", "pipe")
    )
    dp = ("chip", "core")
    by_head = P("pipe", dp, "tensor", None)
    in_specs = (by_head, by_head, P("pipe", None), P("pipe", dp + ("tensor",), None, None))
    return jax.shard_map(
        per_device, mesh=split, in_specs=in_specs, out_specs=(by_head,) * 3, check_vma=False
    )
```

```python
import functools
import math

import jax
import jax.numpy as jnp
from jax import lax
from jax.experimental import pallas as pl
from jax.experimental.pallas import tpu as pltpu
from jax.sharding import Mesh, PartitionSpec as P

NEG_LARGE = -1e30
LOG2E = math.log2(math.e)
HEAD = 128
LONGEST = 3072
EXTRA = 16


def matmul(left, right):
    return jnp.dot(left, right, preferred_element_type=jnp.float32)


def fold(array):
    return array.reshape(array.shape[0] // 8, 8, array.shape[1])


def forward_kernel(
    bounds_ref, starts_ref, turned_ref, *rest,
):
    *block_refs, kept_ref, pairs_ref, acc_ref, stats_ref, sent_ref = rest[:-4]
    scores_ref, top_ref, weights_ref, kept_sem = rest[-4:]
    rows = starts_ref.shape[2]
    groups = turned_ref.shape[1] // rows
    heads = groups // 2
    scale = LOG2E / math.sqrt(HEAD)
    own, clear, last = bounds_ref[0], bounds_ref[2], bounds_ref[3]
    for back, block_ref in enumerate(block_refs):
        pairs_ref[back * rows : (back + 1) * rows, :] = block_ref[...]
    top_ref[...] = jnp.full_like(top_ref, NEG_LARGE)
    acc_ref[...] = jnp.zeros_like(acc_ref)

    def measure(back, masked):
        to = pl.ds(pl.multiple_of(back * rows, rows), rows)
        keys = pairs_ref[to, :HEAD]
        allowed = []
        if masked:
            key_pos = (own - 2 * back) * rows + lax.broadcasted_iota(jnp.int32, (rows, rows), 0)
            across = lax.broadcasted_iota(jnp.int32, (rows, rows), 1)
            for slot in range(2):
                query_pos = bounds_ref[slot] * rows + across
                allowed.append((key_pos <= query_pos) & (key_pos >= starts_ref[slot]))
        for group in range(groups):
            span = slice(group * rows, (group + 1) * rows)
            scores = matmul(keys, turned_ref[:, span])
            if masked:
                scores = jnp.where(allowed[group // heads], scores, NEG_LARGE)
            scores_ref[to, span] = scores
            top_ref[:, span] = jnp.maximum(top_ref[:, span], jnp.max(fold(scores), axis=0))

    def masked(step, unused):
        measure(jnp.where(step == 0, 0, clear + step), True)
        return unused

    def plain(back, unused):
        measure(back, False)
        return unused

    lax.fori_loop(0, last - clear + 1, masked, 0)
    lax.fori_loop(1, clear + 1, plain, 0)
    top = jnp.max(top_ref[...], axis=0, keepdims=True) * scale
    top_ref[...] = jnp.broadcast_to(top, top_ref.shape)

    def weigh(back, unused):
        to = pl.ds(pl.multiple_of(back * rows, rows), rows)
        turned_values = jnp.concatenate(
            [pairs_ref[to, HEAD:].T, jnp.ones((16, rows), jnp.bfloat16)], axis=0
        )
        for group in range(groups):
            span = slice(group * rows, (group + 1) * rows)
            weights_ref[to, span] = jnp.exp2(
                scores_ref[to, span] * scale - top_ref[:1, span]
            ).astype(jnp.bfloat16)
        keep(back).start()
        acc_ref[...] += matmul(turned_values, weights_ref[to, :])
        return unused

    def keep(back):
        to = pl.ds(pl.multiple_of(back * rows, rows), rows)
        return pltpu.make_async_copy(weights_ref.at[to], kept_ref.at[to], kept_sem.at[back])

    def kept(back, unused):
        keep(back).wait()
        return unused

    lax.fori_loop(0, last + 1, weigh, 0)
    totals = acc_ref[HEAD : HEAD + 1, :]
    log_totals = top_ref[:1, :] + jnp.log2(totals)
    stats_ref[...] = jnp.concatenate([top_ref[:1, :], log_totals] + [top] * 6, axis=0)
    parts, rest = [], log_totals
    for _ in range(3):
        parts.append(rest.astype(jnp.bfloat16))
        rest = rest - parts[-1].astype(jnp.float32)
    sent_ref[HEAD:, :] = jnp.concatenate(
        parts + [jnp.zeros((EXTRA - 3, totals.shape[1]), jnp.bfloat16)], axis=0
    )
    inverse = 1.0 / totals
    for group in range(groups):
        span = slice(group * rows, (group + 1) * rows)
        result = acc_ref[:HEAD, span] * inverse[:, span]
        acc_ref[:HEAD, span] = result
        sent_ref[:HEAD, span] = result.astype(jnp.bfloat16)
    lax.fori_loop(0, last + 1, kept, 0)


def fetch(slot, kept_ref, weights_ref, kept_sem, rows):
    def copy(back):
        of = pl.ds(pl.multiple_of(back * rows, rows), rows)
        to = pl.ds(pl.multiple_of((back - slot) * rows, rows), rows)
        return pltpu.make_async_copy(kept_ref.at[of], weights_ref.at[to], kept_sem.at[back - slot])

    return copy


def fetch_all(first, stop, copy):
    def start(back, unused):
        copy(back).start()
        return unused

    lax.fori_loop(first, stop, start, 0)


def accumulate(
    first, stop, pairs_ref, weights_ref, copy, query_ref,
    scaled_ref, turned_scaled_ref, delta_ref, total_ref, move_ref, pair_grad_ref, slot,
):
    rows = move_ref.shape[0]
    groups = move_ref.shape[1] // rows
    root = 1.0 / math.sqrt(HEAD)

    def visit(back, unused):
        at = pl.ds(pl.multiple_of(back * rows, rows), rows)
        to = pl.ds(pl.multiple_of((back - slot) * rows, rows), rows)
        values = pairs_ref[at, HEAD:]
        turned_keys = pairs_ref[at, :HEAD].T
        copy(back).wait()
        for group in range(groups):
            span = slice(group * rows, (group + 1) * rows)
            prob_grad = matmul(values, turned_scaled_ref[:, span])
            move_ref[:, span] = (
                weights_ref[to, span].astype(jnp.float32) * (prob_grad - delta_ref[:, span])
            ).astype(jnp.bfloat16)
        pair_grad_ref[to, HEAD:] = matmul(weights_ref[to, :], scaled_ref[...]).astype(jnp.bfloat16)
        pair_grad_ref[to, :HEAD] = (matmul(move_ref[...], query_ref[...]) * root).astype(
            jnp.bfloat16
        )
        total_ref[...] += matmul(turned_keys, move_ref[...])
        return unused

    def unseen(back, unused):
        to = pl.ds(pl.multiple_of((back - slot) * rows, rows), rows)
        pair_grad_ref[to, :] = jnp.zeros((rows, 2 * HEAD), jnp.bfloat16)
        return unused

    lax.fori_loop(first, stop, visit, 0)
    lax.fori_loop(jnp.maximum(first, stop), slot + pair_grad_ref.shape[0] // rows, unseen, 0)


def hand_out(pair_grad_ref, block_refs):
    rows = block_refs[0].shape[0]
    for at, block_ref in enumerate(block_refs):
        block_ref[...] = pair_grad_ref[at * rows : (at + 1) * rows, :]


def backward_far_kernel(
    bounds_ref, stats_ref, arrived_ref, acc_ref, turned_grad_ref, query_ref, pairs_ref, kept_ref,
    out_ref, scaled_ref, turned_scaled_ref, delta_ref, total_ref, *rest, split,
):
    *block_refs, move_ref, pair_grad_ref, weights_ref, kept_sem = rest
    rows = out_ref.shape[0]
    groups = turned_grad_ref.shape[1] // rows
    heads = groups // 2
    copy = fetch(split, kept_ref, weights_ref, kept_sem, rows)
    fetch_all(split, bounds_ref[3] + 1, copy)
    total_ref[...] = jnp.zeros_like(total_ref)
    for group in range(groups):
        span = slice(group * rows, (group + 1) * rows)
        there = (group + heads) % groups
        theirs = slice(there * rows, (there + 1) * rows)
        other_log = arrived_ref[HEAD : HEAD + 1, theirs].astype(jnp.float32)
        for part in range(1, 3):
            other_log += arrived_ref[HEAD + part : HEAD + part + 1, theirs].astype(jnp.float32)
        own_top, own_log = stats_ref[0:1, span], stats_ref[1:2, span]
        most = jnp.maximum(own_log, other_log)
        log_totals = most + jnp.log2(jnp.exp2(own_log - most) + jnp.exp2(other_log - most))
        result = acc_ref[:HEAD, span] * jnp.exp2(own_log - log_totals) + arrived_ref[
            :HEAD, theirs
        ].astype(jnp.float32) * jnp.exp2(other_log - log_totals)
        result = result.astype(jnp.bfloat16)
        if group < heads:
            out_ref[:, group * HEAD : (group + 1) * HEAD] = result.T
        scaled = turned_grad_ref[:, span].astype(jnp.float32) * jnp.exp2(own_top - log_totals)
        delta_ref[:, span] = jnp.sum(result.astype(jnp.float32) * scaled, axis=0, keepdims=True)
        low = scaled.astype(jnp.bfloat16)
        turned_scaled_ref[:, span] = low
        scaled_ref[span, :] = low.T
    accumulate(
        split, bounds_ref[3] + 1, pairs_ref, weights_ref, copy, query_ref,
        scaled_ref, turned_scaled_ref, delta_ref, total_ref, move_ref, pair_grad_ref, split,
    )
    hand_out(pair_grad_ref, block_refs)


def backward_near_kernel(
    bounds_ref, scaled_ref, turned_scaled_ref, delta_ref, begun_ref, query_ref, pairs_ref,
    kept_ref, query_grad_ref, query_grad_other_ref, *rest,
):
    *block_refs, total_ref, move_ref, pair_grad_ref, weights_ref, kept_sem = rest
    rows = query_grad_ref.shape[0]
    groups = turned_scaled_ref.shape[1] // rows
    heads = groups // 2
    root = 1.0 / math.sqrt(HEAD)
    slots = pair_grad_ref.shape[0] // rows
    stop = jnp.minimum(bounds_ref[3] + 1, slots)
    copy = fetch(0, kept_ref, weights_ref, kept_sem, rows)
    fetch_all(0, stop, copy)
    total_ref[...] = begun_ref[...]
    accumulate(
        0, stop, pairs_ref, weights_ref, copy, query_ref,
        scaled_ref, turned_scaled_ref, delta_ref, total_ref, move_ref, pair_grad_ref, 0,
    )
    hand_out(pair_grad_ref, block_refs)
    for group in range(groups):
        span = slice(group * rows, (group + 1) * rows)
        column = slice(group % heads * HEAD, (group % heads + 1) * HEAD)
        to_ref = query_grad_ref if group < heads else query_grad_other_ref
        to_ref[:, column] = (total_ref[:, span] * root).astype(jnp.bfloat16).T


def smem():
    return pl.BlockSpec(memory_space=pltpu.SMEM)


def vmem():
    return pl.BlockSpec(memory_space=pltpu.VMEM)


def hbm():
    return pl.BlockSpec(memory_space=pltpu.HBM)


def swap_cores(value):
    return lax.ppermute(value, "core", [(0, 1), (1, 0)])


def cost(blocks, rows, wide, matmuls):
    return pl.CostEstimate(
        flops=2 * matmuls * blocks * rows * wide * HEAD,
        transcendentals=0,
        bytes_accessed=2 * blocks * rows * wide,
    )


def attend(bounds, starts, queries, grads, blocks, split, send, swap=swap_cores):
    slots = len(blocks)
    rows, columns = queries[0].shape
    heads = columns // HEAD
    wide = 2 * heads * rows
    turned = jnp.concatenate([turn(q) for q in queries], axis=1)
    turned_grad = jnp.concatenate([turn(g) for g in grads], axis=1)
    stacked = jnp.concatenate([stack(q) for q in queries], axis=0)
    blocks, turned, turned_grad, stacked = lax.optimization_barrier(
        (blocks, turned, turned_grad, stacked)
    )
    weights, pairs, acc, stats, sent = pl.pallas_call(
        forward_kernel,
        out_shape=(
            pltpu.HBM((slots * rows, wide), jnp.bfloat16),
            jax.ShapeDtypeStruct((slots * rows, 2 * HEAD), jnp.bfloat16),
            jax.ShapeDtypeStruct((HEAD + EXTRA, wide), jnp.float32),
            jax.ShapeDtypeStruct((8, wide), jnp.float32),
            jax.ShapeDtypeStruct((HEAD + EXTRA, wide), jnp.bfloat16),
        ),
        in_specs=[smem()] + [vmem()] * (2 + slots),
        out_specs=(hbm(),) + (vmem(),) * 4,
        scratch_shapes=[
            pltpu.VMEM((slots * rows, wide), jnp.float32),
            pltpu.VMEM((8, wide), jnp.float32),
            pltpu.VMEM((slots * rows, wide), jnp.bfloat16),
            pltpu.SemaphoreType.DMA((slots,)),
        ],
        compiler_params=pltpu.CompilerParams(vmem_limit_bytes=36 << 20),
        cost_estimate=cost(slots, rows, wide, 2),
        name="attend_forward",
    )(bounds, starts, turned, *blocks)
    weights = pltpu.with_memory_space_constraint(weights, pltpu.HBM)
    arrived = swap(sent)
    half = jax.ShapeDtypeStruct((rows, columns), jnp.bfloat16)
    params = pltpu.CompilerParams(vmem_limit_bytes=20 << 20)
    move = pltpu.VMEM((rows, wide), jnp.bfloat16)

    def held(blocks):
        return [
            pltpu.VMEM((blocks * rows, 2 * HEAD), jnp.bfloat16),
            pltpu.VMEM((blocks * rows, wide), jnp.bfloat16),
            pltpu.SemaphoreType.DMA((blocks,)),
        ]

    block = jax.ShapeDtypeStruct((rows, 2 * HEAD), jnp.bfloat16)
    out, scaled, turned_scaled, delta, total, *far = pl.pallas_call(
        functools.partial(backward_far_kernel, split=split),
        out_shape=(
            half,
            jax.ShapeDtypeStruct((wide, HEAD), jnp.bfloat16),
            jax.ShapeDtypeStruct((HEAD, wide), jnp.bfloat16),
            jax.ShapeDtypeStruct((1, wide), jnp.float32),
            jax.ShapeDtypeStruct((HEAD, wide), jnp.float32),
        )
        + (block,) * (slots - split),
        in_specs=[smem()] + [vmem()] * 6 + [hbm()],
        out_specs=(vmem(),) * (5 + slots - split),
        scratch_shapes=[move] + held(slots - split),
        compiler_params=params,
        cost_estimate=cost(slots - split, rows, wide, 4),
        name="attend_backward_far",
    )(bounds, stats, arrived, acc, turned_grad, stacked, pairs, weights)
    sent_far = send(far)
    query_grad, query_grad_other, *near = pl.pallas_call(
        backward_near_kernel,
        out_shape=(half, half) + (block,) * split,
        in_specs=[smem()] + [vmem()] * 6 + [hbm()],
        out_specs=(vmem(),) * (2 + split),
        scratch_shapes=[pltpu.VMEM((HEAD, wide), jnp.float32), move] + held(split),
        compiler_params=params,
        cost_estimate=cost(split, rows, wide, 4),
        name="attend_backward_near",
    )(bounds, scaled, turned_scaled, delta, total, stacked, pairs, weights)
    return out, query_grad, query_grad_other, near, sent_far


def turn(array):
    rows, columns = array.shape
    heads = columns // HEAD
    return array.reshape(rows, heads, HEAD).transpose(2, 1, 0).reshape(HEAD, heads * rows)


def stack(array):
    rows, columns = array.shape
    heads = columns // HEAD
    return array.reshape(rows, heads, HEAD).transpose(1, 0, 2).reshape(heads * rows, HEAD)


def block_bounds(lengths, chip, core, rows):
    own, other = 2 * chip + core, 2 * chip + 1 - core
    ends = jnp.cumsum(lengths)
    begins = ends - lengths

    def starts_of(positions):
        here = begins[:, None] <= positions[None, :]
        return jnp.max(jnp.where(here, begins[:, None], 0), axis=0)

    span = jnp.arange(rows, dtype=jnp.int32)
    starts = jnp.stack([starts_of(own * rows + span), starts_of(other * rows + span)])
    edges = starts_of(jnp.stack([2 * chip * rows, (2 * chip + 2) * rows - 1]))
    last = (own - edges[0] // rows) // 2
    clear = jnp.maximum((own - (edges[1] + rows - 1) // rows) // 2, 0)
    bounds = jnp.stack([own, other, clear, last]).astype(jnp.int32)
    return bounds, starts[:, None, :]


def per_device(query, keys_values, doc_lengths, incoming_output_grad):
    chips = lax.axis_size("chip")
    query = query[0, :, 0, :]
    pairs = keys_values[0, :, 0, :]
    rows = query.shape[0]
    reach = min((LONGEST + 2 * rows - 1) // (2 * rows), chips - 1)
    slots = reach + 1
    blocks = [pairs] + [
        lax.ppermute(pairs, "chip", [(c, c + back) for c in range(chips - back)])
        for back in range(1, slots)
    ]
    sections = lax.axis_size("pipe")
    arrived = lax.ppermute(
        incoming_output_grad, "pipe", [(s, (s - 1) % sections) for s in range(sections)]
    )
    arrived, *blocks[1:3] = lax.optimization_barrier((arrived, *blocks[1:3]))
    grad = lax.all_to_all(arrived, "tensor", split_axis=2, concat_axis=1, tiled=True)[0, :, 0, :]
    bounds, starts = block_bounds(
        doc_lengths[0], lax.axis_index("chip"), lax.axis_index("core"), rows
    )
    split = (slots + 1) // 2

    def send(blocks, first):
        return [
            lax.ppermute(block, "chip", [(c, c - first - at) for c in range(first + at, chips)])
            for at, block in enumerate(blocks)
        ]

    out, query_grad, query_grad_other, near, far = attend(
        bounds, starts, (query, swap_cores(query)), (grad, swap_cores(grad)), blocks,
        split, functools.partial(send, first=split),
    )
    sums = near[0].astype(jnp.float32)
    for sent in far:
        sums += sent.astype(jnp.float32)
    sums = lax.optimization_barrier(sums)
    for sent in send(near[1:], 1):
        sums += sent.astype(jnp.float32)
    pair_grad = sums.astype(jnp.bfloat16)
    query_grad = query_grad.astype(jnp.float32) + swap_cores(query_grad_other).astype(jnp.float32)
    query_grad = query_grad.astype(jnp.bfloat16)
    return (out[None, :, None, :], query_grad[None, :, None, :], pair_grad[None, :, None, :])


def solution(mesh):
    shape = mesh.devices.shape
    split = Mesh(
        mesh.devices.reshape((shape[0] // 2, 2) + shape[1:]), ("chip", "core", "tensor", "pipe")
    )
    dp = ("chip", "core")
    by_head = P("pipe", dp, "tensor", None)
    in_specs = (by_head, by_head, P("pipe", None), P("pipe", dp + ("tensor",), None, None))
    return jax.shard_map(
        per_device, mesh=split, in_specs=in_specs, out_specs=(by_head,) * 3, check_vma=False
    )
```

```python
import functools
import math

import jax
import jax.numpy as jnp
from jax import lax
from jax.experimental import pallas as pl
from jax.experimental.pallas import tpu as pltpu
from jax.sharding import Mesh, PartitionSpec as P

NEG_LARGE = -1e30
LOG2E = math.log2(math.e)
HEAD = 128
LONGEST = 3072
EXTRA = 16


def matmul(left, right):
    return jnp.dot(left, right, preferred_element_type=jnp.float32)


def fold(array):
    return array.reshape(array.shape[0] // 8, 8, array.shape[1])


def forward_kernel(
    bounds_ref, starts_ref, turned_ref, *rest,
):
    *block_refs, kept_ref, pairs_ref, acc_ref, stats_ref, sent_ref = rest[:-5]
    scores_ref, top_ref, weights_ref, kept_sem, block_sem = rest[-5:]
    rows = starts_ref.shape[2]
    groups = turned_ref.shape[1] // rows
    heads = groups // 2
    scale = LOG2E / math.sqrt(HEAD)
    own, clear, last = bounds_ref[0], bounds_ref[2], bounds_ref[3]

    def bring(block_ref, back):
        to = pl.ds(pl.multiple_of(back * rows, rows), rows)
        return pltpu.make_async_copy(block_ref, pairs_ref.at[to], block_sem.at[back])

    for back, block_ref in enumerate(block_refs):
        @pl.when(back <= last)
        def start():
            bring(block_ref, back).start()

    top_ref[...] = jnp.full_like(top_ref, NEG_LARGE)
    acc_ref[...] = jnp.zeros_like(acc_ref)

    def measure(back, masked):
        to = pl.ds(pl.multiple_of(back * rows, rows), rows)
        bring(block_refs[0], back).wait()
        keys = pairs_ref[to, :HEAD]
        allowed = []
        if masked:
            key_pos = (own - 2 * back) * rows + lax.broadcasted_iota(jnp.int32, (rows, rows), 0)
            across = lax.broadcasted_iota(jnp.int32, (rows, rows), 1)
            for slot in range(2):
                query_pos = bounds_ref[slot] * rows + across
                allowed.append((key_pos <= query_pos) & (key_pos >= starts_ref[slot]))
        for group in range(groups):
            span = slice(group * rows, (group + 1) * rows)
            scores = matmul(keys, turned_ref[:, span])
            if masked:
                scores = jnp.where(allowed[group // heads], scores, NEG_LARGE)
            scores_ref[to, span] = scores
            top_ref[:, span] = jnp.maximum(top_ref[:, span], jnp.max(fold(scores), axis=0))

    def masked(step, unused):
        measure(jnp.where(step == 0, 0, clear + step), True)
        return unused

    def plain(back, unused):
        measure(back, False)
        return unused

    lax.fori_loop(0, last - clear + 1, masked, 0)
    lax.fori_loop(1, clear + 1, plain, 0)
    top = jnp.max(top_ref[...], axis=0, keepdims=True) * scale
    top_ref[...] = jnp.broadcast_to(top, top_ref.shape)

    def weigh(back, unused):
        to = pl.ds(pl.multiple_of(back * rows, rows), rows)
        turned_values = jnp.concatenate(
            [pairs_ref[to, HEAD:].T, jnp.ones((16, rows), jnp.bfloat16)], axis=0
        )
        for group in range(groups):
            span = slice(group * rows, (group + 1) * rows)
            weights_ref[to, span] = jnp.exp2(
                scores_ref[to, span] * scale - top_ref[:1, span]
            ).astype(jnp.bfloat16)
        keep(back).start()
        acc_ref[...] += matmul(turned_values, weights_ref[to, :])
        return unused

    def keep(back):
        to = pl.ds(pl.multiple_of(back * rows, rows), rows)
        return pltpu.make_async_copy(weights_ref.at[to], kept_ref.at[to], kept_sem.at[back])

    def kept(back, unused):
        keep(back).wait()
        return unused

    lax.fori_loop(0, last + 1, weigh, 0)
    totals = acc_ref[HEAD : HEAD + 1, :]
    log_totals = top_ref[:1, :] + jnp.log2(totals)
    stats_ref[...] = jnp.concatenate([top_ref[:1, :], log_totals] + [top] * 6, axis=0)
    parts, rest = [], log_totals
    for _ in range(3):
        parts.append(rest.astype(jnp.bfloat16))
        rest = rest - parts[-1].astype(jnp.float32)
    sent_ref[HEAD:, :] = jnp.concatenate(
        parts + [jnp.zeros((EXTRA - 3, totals.shape[1]), jnp.bfloat16)], axis=0
    )
    inverse = 1.0 / totals
    for group in range(groups):
        span = slice(group * rows, (group + 1) * rows)
        result = acc_ref[:HEAD, span] * inverse[:, span]
        acc_ref[:HEAD, span] = result
        sent_ref[:HEAD, span] = result.astype(jnp.bfloat16)
    lax.fori_loop(0, last + 1, kept, 0)


def fetch(slot, kept_ref, weights_ref, kept_sem, rows):
    def copy(back):
        of = pl.ds(pl.multiple_of(back * rows, rows), rows)
        to = pl.ds(pl.multiple_of((back - slot) * rows, rows), rows)
        return pltpu.make_async_copy(kept_ref.at[of], weights_ref.at[to], kept_sem.at[back - slot])

    return copy


def fetch_all(first, stop, copy):
    def start(back, unused):
        copy(back).start()
        return unused

    lax.fori_loop(first, stop, start, 0)


def accumulate(
    first, stop, pairs_ref, weights_ref, copy, query_ref,
    scaled_ref, turned_scaled_ref, delta_ref, total_ref, move_ref, pair_grad_ref, slot,
):
    rows = move_ref.shape[0]
    groups = move_ref.shape[1] // rows
    root = 1.0 / math.sqrt(HEAD)

    def visit(back, unused):
        at = pl.ds(pl.multiple_of(back * rows, rows), rows)
        to = pl.ds(pl.multiple_of((back - slot) * rows, rows), rows)
        values = pairs_ref[at, HEAD:]
        turned_keys = pairs_ref[at, :HEAD].T
        copy(back).wait()
        for group in range(groups):
            span = slice(group * rows, (group + 1) * rows)
            prob_grad = matmul(values, turned_scaled_ref[:, span])
            move_ref[:, span] = (
                weights_ref[to, span].astype(jnp.float32) * (prob_grad - delta_ref[:, span])
            ).astype(jnp.bfloat16)
        pair_grad_ref[to, HEAD:] = matmul(weights_ref[to, :], scaled_ref[...]).astype(jnp.bfloat16)
        pair_grad_ref[to, :HEAD] = (matmul(move_ref[...], query_ref[...]) * root).astype(
            jnp.bfloat16
        )
        total_ref[...] += matmul(turned_keys, move_ref[...])
        return unused

    def unseen(back, unused):
        to = pl.ds(pl.multiple_of((back - slot) * rows, rows), rows)
        pair_grad_ref[to, :] = jnp.zeros((rows, 2 * HEAD), jnp.bfloat16)
        return unused

    lax.fori_loop(first, stop, visit, 0)
    lax.fori_loop(jnp.maximum(first, stop), slot + pair_grad_ref.shape[0] // rows, unseen, 0)


def hand_out(pair_grad_ref, block_refs):
    rows = block_refs[0].shape[0]
    for at, block_ref in enumerate(block_refs):
        block_ref[...] = pair_grad_ref[at * rows : (at + 1) * rows, :]


def backward_far_kernel(
    bounds_ref, stats_ref, arrived_ref, acc_ref, grad_ref, grad_other_ref, query_ref, pairs_ref,
    kept_ref,
    out_ref, scaled_ref, turned_scaled_ref, delta_ref, total_ref, *rest, split,
):
    *block_refs, move_ref, pair_grad_ref, weights_ref, kept_sem = rest
    rows = out_ref.shape[0]
    heads = grad_ref.shape[1] // HEAD
    groups = 2 * heads
    copy = fetch(split, kept_ref, weights_ref, kept_sem, rows)
    fetch_all(split, bounds_ref[3] + 1, copy)
    total_ref[...] = jnp.zeros_like(total_ref)
    for group in range(groups):
        span = slice(group * rows, (group + 1) * rows)
        there = (group + heads) % groups
        theirs = slice(there * rows, (there + 1) * rows)
        other_log = arrived_ref[HEAD : HEAD + 1, theirs].astype(jnp.float32)
        for part in range(1, 3):
            other_log += arrived_ref[HEAD + part : HEAD + part + 1, theirs].astype(jnp.float32)
        own_top, own_log = stats_ref[0:1, span], stats_ref[1:2, span]
        most = jnp.maximum(own_log, other_log)
        log_totals = most + jnp.log2(jnp.exp2(own_log - most) + jnp.exp2(other_log - most))
        result = acc_ref[:HEAD, span] * jnp.exp2(own_log - log_totals) + arrived_ref[
            :HEAD, theirs
        ].astype(jnp.float32) * jnp.exp2(other_log - log_totals)
        result = result.astype(jnp.bfloat16)
        column = slice(group % heads * HEAD, (group % heads + 1) * HEAD)
        if group < heads:
            out_ref[:, column] = result.T
        grads = (grad_ref if group < heads else grad_other_ref)[:, column].T
        scaled = grads.astype(jnp.float32) * jnp.exp2(own_top - log_totals)
        delta_ref[:, span] = jnp.sum(result.astype(jnp.float32) * scaled, axis=0, keepdims=True)
        low = scaled.astype(jnp.bfloat16)
        turned_scaled_ref[:, span] = low
        scaled_ref[span, :] = low.T
    accumulate(
        split, bounds_ref[3] + 1, pairs_ref, weights_ref, copy, query_ref,
        scaled_ref, turned_scaled_ref, delta_ref, total_ref, move_ref, pair_grad_ref, split,
    )
    hand_out(pair_grad_ref, block_refs)


def backward_near_kernel(
    bounds_ref, scaled_ref, turned_scaled_ref, delta_ref, begun_ref, query_ref, pairs_ref,
    kept_ref, query_grad_ref, query_grad_other_ref, *rest,
):
    *block_refs, total_ref, move_ref, pair_grad_ref, weights_ref, kept_sem = rest
    rows = query_grad_ref.shape[0]
    groups = turned_scaled_ref.shape[1] // rows
    heads = groups // 2
    root = 1.0 / math.sqrt(HEAD)
    slots = pair_grad_ref.shape[0] // rows
    stop = jnp.minimum(bounds_ref[3] + 1, slots)
    copy = fetch(0, kept_ref, weights_ref, kept_sem, rows)
    fetch_all(0, stop, copy)
    total_ref[...] = begun_ref[...]
    accumulate(
        0, stop, pairs_ref, weights_ref, copy, query_ref,
        scaled_ref, turned_scaled_ref, delta_ref, total_ref, move_ref, pair_grad_ref, 0,
    )
    hand_out(pair_grad_ref, block_refs)
    for group in range(groups):
        span = slice(group * rows, (group + 1) * rows)
        column = slice(group % heads * HEAD, (group % heads + 1) * HEAD)
        to_ref = query_grad_ref if group < heads else query_grad_other_ref
        to_ref[:, column] = (total_ref[:, span] * root).astype(jnp.bfloat16).T


def smem():
    return pl.BlockSpec(memory_space=pltpu.SMEM)


def vmem():
    return pl.BlockSpec(memory_space=pltpu.VMEM)


def hbm():
    return pl.BlockSpec(memory_space=pltpu.HBM)


def swap_cores(value):
    return lax.ppermute(value, "core", [(0, 1), (1, 0)])


def cost(blocks, rows, wide, matmuls):
    return pl.CostEstimate(
        flops=2 * matmuls * blocks * rows * wide * HEAD,
        transcendentals=0,
        bytes_accessed=2 * blocks * rows * wide,
    )


def attend(bounds, starts, queries, grad, blocks, split, send, swap=swap_cores):
    slots = len(blocks)
    rows, columns = queries[0].shape
    heads = columns // HEAD
    wide = 2 * heads * rows
    turned = jnp.concatenate([turn(q) for q in queries], axis=1)
    stacked = jnp.concatenate([stack(q) for q in queries], axis=0)
    blocks, turned, stacked = lax.optimization_barrier((blocks, turned, stacked))
    blocks = [pltpu.with_memory_space_constraint(block, pltpu.HBM) for block in blocks]
    weights, pairs, acc, stats, sent = pl.pallas_call(
        forward_kernel,
        out_shape=(
            pltpu.HBM((slots * rows, wide), jnp.bfloat16),
            jax.ShapeDtypeStruct((slots * rows, 2 * HEAD), jnp.bfloat16),
            jax.ShapeDtypeStruct((HEAD + EXTRA, wide), jnp.float32),
            jax.ShapeDtypeStruct((8, wide), jnp.float32),
            jax.ShapeDtypeStruct((HEAD + EXTRA, wide), jnp.bfloat16),
        ),
        in_specs=[smem()] + [vmem()] * 2 + [hbm()] * slots,
        out_specs=(hbm(),) + (vmem(),) * 4,
        scratch_shapes=[
            pltpu.VMEM((slots * rows, wide), jnp.float32),
            pltpu.VMEM((8, wide), jnp.float32),
            pltpu.VMEM((slots * rows, wide), jnp.bfloat16),
            pltpu.SemaphoreType.DMA((slots,)),
            pltpu.SemaphoreType.DMA((slots,)),
        ],
        compiler_params=pltpu.CompilerParams(vmem_limit_bytes=36 << 20),
        cost_estimate=cost(slots, rows, wide, 2),
        name="attend_forward",
    )(bounds, starts, turned, *blocks)
    weights = pltpu.with_memory_space_constraint(weights, pltpu.HBM)
    arrived = swap(sent)
    grad, stats = lax.optimization_barrier((grad, stats))
    grad_other = swap(grad)
    half = jax.ShapeDtypeStruct((rows, columns), jnp.bfloat16)
    params = pltpu.CompilerParams(vmem_limit_bytes=20 << 20)
    move = pltpu.VMEM((rows, wide), jnp.bfloat16)

    def held(blocks):
        return [
            pltpu.VMEM((blocks * rows, 2 * HEAD), jnp.bfloat16),
            pltpu.VMEM((blocks * rows, wide), jnp.bfloat16),
            pltpu.SemaphoreType.DMA((blocks,)),
        ]

    block = jax.ShapeDtypeStruct((rows, 2 * HEAD), jnp.bfloat16)
    out, scaled, turned_scaled, delta, total, *far = pl.pallas_call(
        functools.partial(backward_far_kernel, split=split),
        out_shape=(
            half,
            jax.ShapeDtypeStruct((wide, HEAD), jnp.bfloat16),
            jax.ShapeDtypeStruct((HEAD, wide), jnp.bfloat16),
            jax.ShapeDtypeStruct((1, wide), jnp.float32),
            jax.ShapeDtypeStruct((HEAD, wide), jnp.float32),
        )
        + (block,) * (slots - split),
        in_specs=[smem()] + [vmem()] * 7 + [hbm()],
        out_specs=(vmem(),) * (5 + slots - split),
        scratch_shapes=[move] + held(slots - split),
        compiler_params=params,
        cost_estimate=cost(slots - split, rows, wide, 4),
        name="attend_backward_far",
    )(bounds, stats, arrived, acc, grad, grad_other, stacked, pairs, weights)
    sent_far = send(far)
    query_grad, query_grad_other, *near = pl.pallas_call(
        backward_near_kernel,
        out_shape=(half, half) + (block,) * split,
        in_specs=[smem()] + [vmem()] * 6 + [hbm()],
        out_specs=(vmem(),) * (2 + split),
        scratch_shapes=[pltpu.VMEM((HEAD, wide), jnp.float32), move] + held(split),
        compiler_params=params,
        cost_estimate=cost(split, rows, wide, 4),
        name="attend_backward_near",
    )(bounds, scaled, turned_scaled, delta, total, stacked, pairs, weights)
    return out, query_grad, query_grad_other, near, sent_far


def turn(array):
    rows, columns = array.shape
    heads = columns // HEAD
    return array.reshape(rows, heads, HEAD).transpose(2, 1, 0).reshape(HEAD, heads * rows)


def stack(array):
    rows, columns = array.shape
    heads = columns // HEAD
    return array.reshape(rows, heads, HEAD).transpose(1, 0, 2).reshape(heads * rows, HEAD)


def block_bounds(lengths, chip, core, rows):
    own, other = 2 * chip + core, 2 * chip + 1 - core
    ends = jnp.cumsum(lengths)
    begins = ends - lengths

    def starts_of(positions):
        here = begins[:, None] <= positions[None, :]
        return jnp.max(jnp.where(here, begins[:, None], 0), axis=0)

    span = jnp.arange(rows, dtype=jnp.int32)
    starts = jnp.stack([starts_of(own * rows + span), starts_of(other * rows + span)])
    edges = starts_of(jnp.stack([2 * chip * rows, (2 * chip + 2) * rows - 1]))
    last = (own - edges[0] // rows) // 2
    clear = jnp.maximum((own - (edges[1] + rows - 1) // rows) // 2, 0)
    bounds = jnp.stack([own, other, clear, last]).astype(jnp.int32)
    return bounds, starts[:, None, :]


def per_device(query, keys_values, doc_lengths, incoming_output_grad):
    chips = lax.axis_size("chip")
    query = query[0, :, 0, :]
    pairs = keys_values[0, :, 0, :]
    rows = query.shape[0]
    reach = min((LONGEST + 2 * rows - 1) // (2 * rows), chips - 1)
    slots = reach + 1
    blocks = [pairs] + [
        lax.ppermute(pairs, "chip", [(c, c + back) for c in range(chips - back)])
        for back in range(1, slots)
    ]
    sections = lax.axis_size("pipe")
    arrived = lax.ppermute(
        incoming_output_grad, "pipe", [(s, (s - 1) % sections) for s in range(sections)]
    )
    arrived, *blocks[1:3] = lax.optimization_barrier((arrived, *blocks[1:3]))
    grad = lax.all_to_all(arrived, "tensor", split_axis=2, concat_axis=1, tiled=True)[0, :, 0, :]
    bounds, starts = block_bounds(
        doc_lengths[0], lax.axis_index("chip"), lax.axis_index("core"), rows
    )
    split = (slots + 1) // 2

    def send(blocks, first):
        return [
            lax.ppermute(block, "chip", [(c, c - first - at) for c in range(first + at, chips)])
            for at, block in enumerate(blocks)
        ]

    out, query_grad, query_grad_other, near, far = attend(
        bounds, starts, (query, swap_cores(query)), grad, blocks,
        split, functools.partial(send, first=split),
    )
    sums = near[0].astype(jnp.float32)
    for sent in far:
        sums += sent.astype(jnp.float32)
    sums = lax.optimization_barrier(sums)
    for sent in send(near[1:], 1):
        sums += sent.astype(jnp.float32)
    pair_grad = sums.astype(jnp.bfloat16)
    query_grad = query_grad.astype(jnp.float32) + swap_cores(query_grad_other).astype(jnp.float32)
    query_grad = query_grad.astype(jnp.bfloat16)
    return (out[None, :, None, :], query_grad[None, :, None, :], pair_grad[None, :, None, :])


def solution(mesh):
    shape = mesh.devices.shape
    split = Mesh(
        mesh.devices.reshape((shape[0] // 2, 2) + shape[1:]), ("chip", "core", "tensor", "pipe")
    )
    dp = ("chip", "core")
    by_head = P("pipe", dp, "tensor", None)
    in_specs = (by_head, by_head, P("pipe", None), P("pipe", dp + ("tensor",), None, None))
    return jax.shard_map(
        per_device, mesh=split, in_specs=in_specs, out_specs=(by_head,) * 3, check_vma=False
    )
```

```python
import functools
import math

import jax
import jax.numpy as jnp
from jax import lax
from jax.experimental import pallas as pl
from jax.experimental.pallas import tpu as pltpu
from jax.sharding import Mesh, PartitionSpec as P

NEG_LARGE = -1e30
LOG2E = math.log2(math.e)
HEAD = 128
LONGEST = 3072
EXTRA = 16


def matmul(left, right):
    return jnp.dot(left, right, preferred_element_type=jnp.float32)


def fold(array):
    return array.reshape(array.shape[0] // 8, 8, array.shape[1])


def begins_of(lengths_ref):
    begins = [jnp.int32(0)]
    for doc in range(lengths_ref.shape[0] - 1):
        begins.append(begins[-1] + lengths_ref[doc])
    return begins


def start_of(position, begins):
    start = jnp.zeros_like(position)
    for begin in begins:
        start = jnp.where(begin <= position, begin, start)
    return start


def last_of(begins, place_ref, rows):
    chip, core = place_ref[0], place_ref[1]
    first = start_of(2 * chip * rows, begins)
    return lax.div(2 * chip + core - lax.div(first, jnp.int32(rows)), jnp.int32(2))


def clear_of(begins, place_ref, rows):
    chip, core = place_ref[0], place_ref[1]
    start = start_of((2 * chip + 2) * rows - 1, begins)
    blocks = 2 * chip + core - lax.div(start + rows - 1, jnp.int32(rows))
    return jnp.maximum(lax.div(blocks, jnp.int32(2)), 0)


def stack(to_ref, query_refs):
    rows = query_refs[0].shape[0]
    heads = query_refs[0].shape[1] // HEAD
    for group in range(2 * heads):
        column = slice(group % heads * HEAD, (group % heads + 1) * HEAD)
        to_ref[group * rows : (group + 1) * rows, :] = query_refs[group // heads][:, column]


def forward_kernel(
    lengths_ref, place_ref, query_ref, query_other_ref, *rest,
):
    *block_refs, kept_ref, pairs_ref, acc_ref, stats_ref, sent_ref = rest[:-7]
    scores_ref, top_ref, weights_ref, turned_ref, starts_ref, kept_sem, block_sem = rest[-7:]
    rows = query_ref.shape[0]
    heads = query_ref.shape[1] // HEAD
    groups = 2 * heads
    scale = LOG2E / math.sqrt(HEAD)
    begins = begins_of(lengths_ref)
    last, clear = last_of(begins, place_ref, rows), clear_of(begins, place_ref, rows)
    own = 2 * place_ref[0] + place_ref[1]
    shards = (own, 2 * place_ref[0] + 1 - place_ref[1])

    def bring(block_ref, back):
        to = pl.ds(pl.multiple_of(back * rows, rows), rows)
        return pltpu.make_async_copy(block_ref, pairs_ref.at[to], block_sem.at[back])

    for back, block_ref in enumerate(block_refs):
        @pl.when(back <= last)
        def start():
            bring(block_ref, back).start()

    along = lax.broadcasted_iota(jnp.int32, (1, rows), 1)
    for slot, rows_ref in enumerate((query_ref, query_other_ref)):
        starts_ref[slot] = start_of(shards[slot] * rows + along, begins)
        for head in range(heads):
            span = slice((slot * heads + head) * rows, (slot * heads + head + 1) * rows)
            turned_ref[:, span] = rows_ref[:, head * HEAD : (head + 1) * HEAD].T
    top_ref[...] = jnp.full_like(top_ref, NEG_LARGE)
    acc_ref[...] = jnp.zeros_like(acc_ref)

    def measure(back, masked):
        to = pl.ds(pl.multiple_of(back * rows, rows), rows)
        bring(block_refs[0], back).wait()
        keys = pairs_ref[to, :HEAD]
        allowed = []
        if masked:
            key_pos = (own - 2 * back) * rows + lax.broadcasted_iota(jnp.int32, (rows, rows), 0)
            across = lax.broadcasted_iota(jnp.int32, (rows, rows), 1)
            for slot in range(2):
                query_pos = shards[slot] * rows + across
                allowed.append((key_pos <= query_pos) & (key_pos >= starts_ref[slot]))
        for group in range(groups):
            span = slice(group * rows, (group + 1) * rows)
            scores = matmul(keys, turned_ref[:, span])
            if masked:
                scores = jnp.where(allowed[group // heads], scores, NEG_LARGE)
            scores_ref[to, span] = scores
            top_ref[:, span] = jnp.maximum(top_ref[:, span], jnp.max(fold(scores), axis=0))

    def masked(step, unused):
        measure(jnp.where(step == 0, 0, clear + step), True)
        return unused

    def plain(back, unused):
        measure(back, False)
        return unused

    lax.fori_loop(0, last - clear + 1, masked, 0)
    lax.fori_loop(1, clear + 1, plain, 0)
    top = jnp.max(top_ref[...], axis=0, keepdims=True) * scale
    top_ref[...] = jnp.broadcast_to(top, top_ref.shape)

    def weigh(back, unused):
        to = pl.ds(pl.multiple_of(back * rows, rows), rows)
        turned_values = jnp.concatenate(
            [pairs_ref[to, HEAD:].T, jnp.ones((16, rows), jnp.bfloat16)], axis=0
        )
        for group in range(groups):
            span = slice(group * rows, (group + 1) * rows)
            weights_ref[to, span] = jnp.exp2(
                scores_ref[to, span] * scale - top_ref[:1, span]
            ).astype(jnp.bfloat16)
        keep(back).start()
        acc_ref[...] += matmul(turned_values, weights_ref[to, :])
        return unused

    def keep(back):
        to = pl.ds(pl.multiple_of(back * rows, rows), rows)
        return pltpu.make_async_copy(weights_ref.at[to], kept_ref.at[to], kept_sem.at[back])

    def kept(back, unused):
        keep(back).wait()
        return unused

    lax.fori_loop(0, last + 1, weigh, 0)
    totals = acc_ref[HEAD : HEAD + 1, :]
    log_totals = top_ref[:1, :] + jnp.log2(totals)
    stats_ref[...] = jnp.concatenate([top_ref[:1, :], log_totals] + [top] * 6, axis=0)
    parts, rest = [], log_totals
    for _ in range(3):
        parts.append(rest.astype(jnp.bfloat16))
        rest = rest - parts[-1].astype(jnp.float32)
    sent_ref[HEAD:, :] = jnp.concatenate(
        parts + [jnp.zeros((EXTRA - 3, totals.shape[1]), jnp.bfloat16)], axis=0
    )
    inverse = 1.0 / totals
    for group in range(groups):
        span = slice(group * rows, (group + 1) * rows)
        result = acc_ref[:HEAD, span] * inverse[:, span]
        acc_ref[:HEAD, span] = result
        sent_ref[:HEAD, span] = result.astype(jnp.bfloat16)
    lax.fori_loop(0, last + 1, kept, 0)


def fetch(slot, kept_ref, weights_ref, kept_sem, rows):
    def copy(back):
        of = pl.ds(pl.multiple_of(back * rows, rows), rows)
        to = pl.ds(pl.multiple_of((back - slot) * rows, rows), rows)
        return pltpu.make_async_copy(kept_ref.at[of], weights_ref.at[to], kept_sem.at[back - slot])

    return copy


def fetch_all(first, stop, copy):
    def start(back, unused):
        copy(back).start()
        return unused

    lax.fori_loop(first, stop, start, 0)


def accumulate(
    first, stop, pairs_ref, weights_ref, copy, query_ref,
    scaled_ref, turned_scaled_ref, delta_ref, total_ref, move_ref, pair_grad_ref, slot,
):
    rows = move_ref.shape[0]
    groups = move_ref.shape[1] // rows
    root = 1.0 / math.sqrt(HEAD)

    def visit(back, unused):
        at = pl.ds(pl.multiple_of(back * rows, rows), rows)
        to = pl.ds(pl.multiple_of((back - slot) * rows, rows), rows)
        values = pairs_ref[at, HEAD:]
        turned_keys = pairs_ref[at, :HEAD].T
        copy(back).wait()
        for group in range(groups):
            span = slice(group * rows, (group + 1) * rows)
            prob_grad = matmul(values, turned_scaled_ref[:, span])
            move_ref[:, span] = (
                weights_ref[to, span].astype(jnp.float32) * (prob_grad - delta_ref[:, span])
            ).astype(jnp.bfloat16)
        pair_grad_ref[to, HEAD:] = matmul(weights_ref[to, :], scaled_ref[...]).astype(jnp.bfloat16)
        pair_grad_ref[to, :HEAD] = (matmul(move_ref[...], query_ref[...]) * root).astype(
            jnp.bfloat16
        )
        total_ref[...] += matmul(turned_keys, move_ref[...])
        return unused

    def unseen(back, unused):
        to = pl.ds(pl.multiple_of((back - slot) * rows, rows), rows)
        pair_grad_ref[to, :] = jnp.zeros((rows, 2 * HEAD), jnp.bfloat16)
        return unused

    lax.fori_loop(first, stop, visit, 0)
    lax.fori_loop(jnp.maximum(first, stop), slot + pair_grad_ref.shape[0] // rows, unseen, 0)


def hand_out(pair_grad_ref, block_refs):
    rows = block_refs[0].shape[0]
    for at, block_ref in enumerate(block_refs):
        block_ref[...] = pair_grad_ref[at * rows : (at + 1) * rows, :]


def backward_far_kernel(
    lengths_ref, place_ref, stats_ref, arrived_ref, acc_ref, grad_ref, grad_other_ref,
    query_ref, query_other_ref, pairs_ref, kept_ref,
    out_ref, scaled_ref, turned_scaled_ref, delta_ref, total_ref, *rest, split,
):
    *block_refs, move_ref, stacked_ref, pair_grad_ref, weights_ref, kept_sem = rest
    rows = out_ref.shape[0]
    heads = grad_ref.shape[1] // HEAD
    groups = 2 * heads
    copy = fetch(split, kept_ref, weights_ref, kept_sem, rows)
    last = last_of(begins_of(lengths_ref), place_ref, rows)
    fetch_all(split, last + 1, copy)
    stack(stacked_ref, (query_ref, query_other_ref))
    total_ref[...] = jnp.zeros_like(total_ref)
    for group in range(groups):
        span = slice(group * rows, (group + 1) * rows)
        there = (group + heads) % groups
        theirs = slice(there * rows, (there + 1) * rows)
        other_log = arrived_ref[HEAD : HEAD + 1, theirs].astype(jnp.float32)
        for part in range(1, 3):
            other_log += arrived_ref[HEAD + part : HEAD + part + 1, theirs].astype(jnp.float32)
        own_top, own_log = stats_ref[0:1, span], stats_ref[1:2, span]
        most = jnp.maximum(own_log, other_log)
        log_totals = most + jnp.log2(jnp.exp2(own_log - most) + jnp.exp2(other_log - most))
        result = acc_ref[:HEAD, span] * jnp.exp2(own_log - log_totals) + arrived_ref[
            :HEAD, theirs
        ].astype(jnp.float32) * jnp.exp2(other_log - log_totals)
        result = result.astype(jnp.bfloat16)
        column = slice(group % heads * HEAD, (group % heads + 1) * HEAD)
        if group < heads:
            out_ref[:, column] = result.T
        grads = (grad_ref if group < heads else grad_other_ref)[:, column].T
        scaled = grads.astype(jnp.float32) * jnp.exp2(own_top - log_totals)
        delta_ref[:, span] = jnp.sum(result.astype(jnp.float32) * scaled, axis=0, keepdims=True)
        low = scaled.astype(jnp.bfloat16)
        turned_scaled_ref[:, span] = low
        scaled_ref[span, :] = low.T
    accumulate(
        split, last + 1, pairs_ref, weights_ref, copy, stacked_ref,
        scaled_ref, turned_scaled_ref, delta_ref, total_ref, move_ref, pair_grad_ref, split,
    )
    hand_out(pair_grad_ref, block_refs)


def backward_near_kernel(
    lengths_ref, place_ref, scaled_ref, turned_scaled_ref, delta_ref, begun_ref,
    query_ref, query_other_ref, pairs_ref, kept_ref, query_grad_ref, query_grad_other_ref, *rest,
):
    *block_refs, total_ref, move_ref, stacked_ref, pair_grad_ref, weights_ref, kept_sem = rest
    rows = query_grad_ref.shape[0]
    groups = turned_scaled_ref.shape[1] // rows
    heads = groups // 2
    root = 1.0 / math.sqrt(HEAD)
    slots = len(block_refs)
    stop = jnp.minimum(last_of(begins_of(lengths_ref), place_ref, rows) + 1, slots)
    copy = fetch(0, kept_ref, weights_ref, kept_sem, rows)
    fetch_all(0, stop, copy)
    stack(stacked_ref, (query_ref, query_other_ref))
    total_ref[...] = begun_ref[...]
    accumulate(
        0, stop, pairs_ref, weights_ref, copy, stacked_ref,
        scaled_ref, turned_scaled_ref, delta_ref, total_ref, move_ref, pair_grad_ref, 0,
    )
    hand_out(pair_grad_ref, block_refs)
    for group in range(groups):
        span = slice(group * rows, (group + 1) * rows)
        column = slice(group % heads * HEAD, (group % heads + 1) * HEAD)
        to_ref = query_grad_ref if group < heads else query_grad_other_ref
        to_ref[:, column] = (total_ref[:, span] * root).astype(jnp.bfloat16).T


def smem():
    return pl.BlockSpec(memory_space=pltpu.SMEM)


def vmem():
    return pl.BlockSpec(memory_space=pltpu.VMEM)


def hbm():
    return pl.BlockSpec(memory_space=pltpu.HBM)


def swap_cores(value):
    return lax.ppermute(value, "core", [(0, 1), (1, 0)])


def cost(blocks, rows, wide, matmuls):
    return pl.CostEstimate(
        flops=2 * matmuls * blocks * rows * wide * HEAD,
        transcendentals=0,
        bytes_accessed=2 * blocks * rows * wide,
    )


def attend(lengths, place, queries, grad, blocks, split, send, swap=swap_cores):
    slots = len(blocks)
    rows, columns = queries[0].shape
    heads = columns // HEAD
    wide = 2 * heads * rows
    blocks, queries = lax.optimization_barrier((blocks, queries))
    blocks = [pltpu.with_memory_space_constraint(block, pltpu.HBM) for block in blocks]
    weights, pairs, acc, stats, sent = pl.pallas_call(
        forward_kernel,
        out_shape=(
            pltpu.HBM((slots * rows, wide), jnp.bfloat16),
            jax.ShapeDtypeStruct((slots * rows, 2 * HEAD), jnp.bfloat16),
            jax.ShapeDtypeStruct((HEAD + EXTRA, wide), jnp.float32),
            jax.ShapeDtypeStruct((8, wide), jnp.float32),
            jax.ShapeDtypeStruct((HEAD + EXTRA, wide), jnp.bfloat16),
        ),
        in_specs=[smem()] * 2 + [vmem()] * 2 + [hbm()] * slots,
        out_specs=(hbm(),) + (vmem(),) * 4,
        scratch_shapes=[
            pltpu.VMEM((slots * rows, wide), jnp.float32),
            pltpu.VMEM((8, wide), jnp.float32),
            pltpu.VMEM((slots * rows, wide), jnp.bfloat16),
            pltpu.VMEM((HEAD, wide), jnp.bfloat16),
            pltpu.VMEM((2, 1, rows), jnp.int32),
            pltpu.SemaphoreType.DMA((slots,)),
            pltpu.SemaphoreType.DMA((slots,)),
        ],
        compiler_params=pltpu.CompilerParams(vmem_limit_bytes=36 << 20),
        cost_estimate=cost(slots, rows, wide, 2),
        name="attend_forward",
    )(lengths, place, *queries, *blocks)
    weights = pltpu.with_memory_space_constraint(weights, pltpu.HBM)
    arrived = swap(sent)
    grad, stats = lax.optimization_barrier((grad, stats))
    grad_other = swap(grad)
    half = jax.ShapeDtypeStruct((rows, columns), jnp.bfloat16)
    params = pltpu.CompilerParams(vmem_limit_bytes=20 << 20)
    move = pltpu.VMEM((rows, wide), jnp.bfloat16)

    def held(blocks):
        return [
            pltpu.VMEM((wide, HEAD), jnp.bfloat16),
            pltpu.VMEM((blocks * rows, 2 * HEAD), jnp.bfloat16),
            pltpu.VMEM((blocks * rows, wide), jnp.bfloat16),
            pltpu.SemaphoreType.DMA((blocks,)),
        ]

    block = jax.ShapeDtypeStruct((rows, 2 * HEAD), jnp.bfloat16)
    out, scaled, turned_scaled, delta, total, *far = pl.pallas_call(
        functools.partial(backward_far_kernel, split=split),
        out_shape=(
            half,
            jax.ShapeDtypeStruct((wide, HEAD), jnp.bfloat16),
            jax.ShapeDtypeStruct((HEAD, wide), jnp.bfloat16),
            jax.ShapeDtypeStruct((1, wide), jnp.float32),
            jax.ShapeDtypeStruct((HEAD, wide), jnp.float32),
        )
        + (block,) * (slots - split),
        in_specs=[smem()] * 2 + [vmem()] * 8 + [hbm()],
        out_specs=(vmem(),) * (5 + slots - split),
        scratch_shapes=[move] + held(slots - split),
        compiler_params=params,
        cost_estimate=cost(slots - split, rows, wide, 4),
        name="attend_backward_far",
    )(lengths, place, stats, arrived, acc, grad, grad_other, *queries, pairs, weights)
    sent_far = send(far)
    query_grad, query_grad_other, *near = pl.pallas_call(
        backward_near_kernel,
        out_shape=(half, half) + (block,) * split,
        in_specs=[smem()] * 2 + [vmem()] * 7 + [hbm()],
        out_specs=(vmem(),) * (2 + split),
        scratch_shapes=[pltpu.VMEM((HEAD, wide), jnp.float32), move] + held(split),
        compiler_params=params,
        cost_estimate=cost(split, rows, wide, 4),
        name="attend_backward_near",
    )(lengths, place, scaled, turned_scaled, delta, total, *queries, pairs, weights)
    return out, query_grad, query_grad_other, near, sent_far


def per_device(query, keys_values, doc_lengths, incoming_output_grad):
    chips = lax.axis_size("chip")
    query = query[0, :, 0, :]
    pairs = keys_values[0, :, 0, :]
    rows = query.shape[0]
    reach = min((LONGEST + 2 * rows - 1) // (2 * rows), chips - 1)
    slots = reach + 1
    blocks = [pairs] + [
        lax.ppermute(pairs, "chip", [(c, c + back) for c in range(chips - back)])
        for back in range(1, slots)
    ]
    sections = lax.axis_size("pipe")
    arrived = lax.ppermute(
        incoming_output_grad, "pipe", [(s, (s - 1) % sections) for s in range(sections)]
    )
    arrived, *blocks[1:3] = lax.optimization_barrier((arrived, *blocks[1:3]))
    grad = lax.all_to_all(arrived, "tensor", split_axis=2, concat_axis=1, tiled=True)[0, :, 0, :]
    place = jnp.stack([lax.axis_index("chip"), lax.axis_index("core")]).astype(jnp.int32)
    split = (slots + 1) // 2

    def send(blocks, first):
        return [
            lax.ppermute(block, "chip", [(c, c - first - at) for c in range(first + at, chips)])
            for at, block in reversed(list(enumerate(blocks)))
        ]

    out, query_grad, query_grad_other, near, far = attend(
        doc_lengths[0], place, (query, swap_cores(query)), grad, blocks,
        split, functools.partial(send, first=split),
    )
    sums = near[0].astype(jnp.float32)
    for sent in far:
        sums += sent.astype(jnp.float32)
    sums = lax.optimization_barrier(sums)
    for sent in send(near[1:], 1):
        sums += sent.astype(jnp.float32)
    pair_grad = sums.astype(jnp.bfloat16)
    query_grad = query_grad.astype(jnp.float32) + swap_cores(query_grad_other).astype(jnp.float32)
    query_grad = query_grad.astype(jnp.bfloat16)
    return (out[None, :, None, :], query_grad[None, :, None, :], pair_grad[None, :, None, :])


def solution(mesh):
    shape = mesh.devices.shape
    split = Mesh(
        mesh.devices.reshape((shape[0] // 2, 2) + shape[1:]), ("chip", "core", "tensor", "pipe")
    )
    dp = ("chip", "core")
    by_head = P("pipe", dp, "tensor", None)
    in_specs = (by_head, by_head, P("pipe", None), P("pipe", dp + ("tensor",), None, None))
    return jax.shard_map(
        per_device, mesh=split, in_specs=in_specs, out_specs=(by_head,) * 3, check_vma=False
    )
```

```python
import functools
import math

import jax
import jax.numpy as jnp
from jax import lax
from jax.experimental import pallas as pl
from jax.experimental.pallas import tpu as pltpu
from jax.sharding import Mesh, PartitionSpec as P

NEG_LARGE = -1e30
LOG2E = math.log2(math.e)
HEAD = 128
LONGEST = 3072
EXTRA = 16


def matmul(left, right):
    return jnp.dot(left, right, preferred_element_type=jnp.float32)


def fold(array):
    return array.reshape(array.shape[0] // 8, 8, array.shape[1])


def begins_of(place_ref):
    begins = [jnp.int32(0)]
    for at in range(2, place_ref.shape[0] - 1):
        begins.append(begins[-1] + place_ref[at])
    return begins


def start_of(position, begins):
    start = jnp.zeros_like(position)
    for begin in begins:
        start = jnp.where(begin <= position, begin, start)
    return start


def last_of(begins, place_ref, rows):
    chip, core = place_ref[0], place_ref[1]
    first = start_of(2 * chip * rows, begins)
    return lax.div(2 * chip + core - lax.div(first, jnp.int32(rows)), jnp.int32(2))


def clear_of(begins, place_ref, rows):
    chip, core = place_ref[0], place_ref[1]
    start = start_of((2 * chip + 2) * rows - 1, begins)
    blocks = 2 * chip + core - lax.div(start + rows - 1, jnp.int32(rows))
    return jnp.maximum(lax.div(blocks, jnp.int32(2)), 0)


def stack(to_ref, query_refs):
    rows = query_refs[0].shape[0]
    heads = query_refs[0].shape[1] // HEAD
    for group in range(2 * heads):
        column = slice(group % heads * HEAD, (group % heads + 1) * HEAD)
        to_ref[group * rows : (group + 1) * rows, :] = query_refs[group // heads][:, column]


def forward_kernel(
    place_ref, query_hbm_ref, query_other_ref, *rest,
):
    *block_refs, kept_ref, pairs_ref, acc_ref, stats_ref, sent_ref = rest[:-9]
    scores_ref, top_ref, weights_ref, turned_ref, starts_ref, query_ref = rest[-9:-3]
    kept_sem, block_sem, query_sem = rest[-3:]
    rows = query_ref.shape[0]
    heads = query_ref.shape[1] // HEAD
    groups = 2 * heads
    scale = LOG2E / math.sqrt(HEAD)
    own_rows = pltpu.make_async_copy(query_hbm_ref, query_ref, query_sem)
    own_rows.start()
    begins = begins_of(place_ref)
    last, clear = last_of(begins, place_ref, rows), clear_of(begins, place_ref, rows)
    own = 2 * place_ref[0] + place_ref[1]
    shards = (own, 2 * place_ref[0] + 1 - place_ref[1])

    def bring(block_ref, back):
        to = pl.ds(pl.multiple_of(back * rows, rows), rows)
        return pltpu.make_async_copy(block_ref, pairs_ref.at[to], block_sem.at[back])

    for back, block_ref in enumerate(block_refs):
        @pl.when(back <= last)
        def start():
            bring(block_ref, back).start()

    along = lax.broadcasted_iota(jnp.int32, (1, rows), 1)
    for slot, rows_ref in ((1, query_other_ref), (0, query_ref)):
        if slot == 0:
            own_rows.wait()
        starts_ref[slot] = start_of(shards[slot] * rows + along, begins)
        for head in range(heads):
            span = slice((slot * heads + head) * rows, (slot * heads + head + 1) * rows)
            turned_ref[:, span] = rows_ref[:, head * HEAD : (head + 1) * HEAD].T
    top_ref[...] = jnp.full_like(top_ref, NEG_LARGE)
    acc_ref[...] = jnp.zeros_like(acc_ref)

    def measure(back, masked, count=1):
        to = pl.ds(pl.multiple_of(back * rows, rows), count * rows)
        for more in range(count):
            bring(block_refs[0], back + more).wait()
        keys = pairs_ref[to, :HEAD]
        allowed = []
        if masked:
            key_pos = (own - 2 * back) * rows + lax.broadcasted_iota(jnp.int32, (rows, rows), 0)
            across = lax.broadcasted_iota(jnp.int32, (rows, rows), 1)
            for slot in range(2):
                query_pos = shards[slot] * rows + across
                allowed.append((key_pos <= query_pos) & (key_pos >= starts_ref[slot]))
        for group in range(groups):
            span = slice(group * rows, (group + 1) * rows)
            scores = matmul(keys, turned_ref[:, span])
            if masked:
                scores = jnp.where(allowed[group // heads], scores, NEG_LARGE)
            scores_ref[to, span] = scores
            top_ref[:, span] = jnp.maximum(top_ref[:, span], jnp.max(fold(scores), axis=0))

    def masked(step, unused):
        measure(jnp.where(step == 0, 0, clear + step), True)
        return unused

    def plain(back, unused):
        measure(back, False)
        return unused

    def two_plain(pair, unused):
        measure(1 + 2 * pair, False, 2)
        return unused

    lax.fori_loop(0, last - clear + 1, masked, 0)
    twos = lax.div(clear, jnp.int32(2))
    lax.fori_loop(0, twos, two_plain, 0)
    lax.fori_loop(1 + 2 * twos, clear + 1, plain, 0)
    top = jnp.max(top_ref[...], axis=0, keepdims=True) * scale
    top_ref[...] = jnp.broadcast_to(top, top_ref.shape)

    def weigh(back, count):
        to = pl.ds(pl.multiple_of(back * rows, rows), count * rows)
        turned_values = jnp.concatenate(
            [pairs_ref[to, HEAD:].T, jnp.ones((16, count * rows), jnp.bfloat16)], axis=0
        )
        for group in range(groups):
            span = slice(group * rows, (group + 1) * rows)
            weights_ref[to, span] = jnp.exp2(
                scores_ref[to, span] * scale - top_ref[:1, span]
            ).astype(jnp.bfloat16)
        for more in range(count):
            keep(back + more).start()
        acc_ref[...] += matmul(turned_values, weights_ref[to, :])

    def weigh_two(pair, unused):
        weigh(2 * pair, 2)
        return unused

    def weigh_one(back, unused):
        weigh(back, 1)
        return unused

    def keep(back):
        to = pl.ds(pl.multiple_of(back * rows, rows), rows)
        return pltpu.make_async_copy(weights_ref.at[to], kept_ref.at[to], kept_sem.at[back])

    def kept(back, unused):
        keep(back).wait()
        return unused

    twos = lax.div(last + 1, jnp.int32(2))
    lax.fori_loop(0, twos, weigh_two, 0)
    lax.fori_loop(2 * twos, last + 1, weigh_one, 0)
    totals = acc_ref[HEAD : HEAD + 1, :]
    log_totals = top_ref[:1, :] + jnp.log2(totals)
    stats_ref[...] = jnp.concatenate([top_ref[:1, :], log_totals] + [top] * 6, axis=0)
    parts, rest = [], log_totals
    for _ in range(3):
        parts.append(rest.astype(jnp.bfloat16))
        rest = rest - parts[-1].astype(jnp.float32)
    sent_ref[HEAD:, :] = jnp.concatenate(
        parts + [jnp.zeros((EXTRA - 3, totals.shape[1]), jnp.bfloat16)], axis=0
    )
    inverse = 1.0 / totals
    for group in range(groups):
        span = slice(group * rows, (group + 1) * rows)
        result = acc_ref[:HEAD, span] * inverse[:, span]
        acc_ref[:HEAD, span] = result
        sent_ref[:HEAD, span] = result.astype(jnp.bfloat16)
    lax.fori_loop(0, last + 1, kept, 0)


def fetch(slot, kept_ref, weights_ref, kept_sem, rows):
    def copy(back):
        of = pl.ds(pl.multiple_of(back * rows, rows), rows)
        to = pl.ds(pl.multiple_of((back - slot) * rows, rows), rows)
        return pltpu.make_async_copy(kept_ref.at[of], weights_ref.at[to], kept_sem.at[back - slot])

    return copy


def fetch_all(first, stop, copy):
    def start(back, unused):
        copy(back).start()
        return unused

    lax.fori_loop(first, stop, start, 0)


def accumulate(
    first, stop, pairs_ref, weights_ref, copy, query_ref,
    scaled_ref, turned_scaled_ref, delta_ref, total_ref, move_ref, pair_grad_ref, slot,
):
    rows = move_ref.shape[0]
    groups = move_ref.shape[1] // rows
    root = 1.0 / math.sqrt(HEAD)

    def visit(back, unused):
        at = pl.ds(pl.multiple_of(back * rows, rows), rows)
        to = pl.ds(pl.multiple_of((back - slot) * rows, rows), rows)
        values = pairs_ref[at, HEAD:]
        turned_keys = pairs_ref[at, :HEAD].T
        copy(back).wait()
        for group in range(groups):
            span = slice(group * rows, (group + 1) * rows)
            prob_grad = matmul(values, turned_scaled_ref[:, span])
            move_ref[:, span] = (
                weights_ref[to, span].astype(jnp.float32) * (prob_grad - delta_ref[:, span])
            ).astype(jnp.bfloat16)
        pair_grad_ref[to, HEAD:] = matmul(weights_ref[to, :], scaled_ref[...]).astype(jnp.bfloat16)
        pair_grad_ref[to, :HEAD] = (matmul(move_ref[...], query_ref[...]) * root).astype(
            jnp.bfloat16
        )
        total_ref[...] += matmul(turned_keys, move_ref[...])
        return unused

    def unseen(back, unused):
        to = pl.ds(pl.multiple_of((back - slot) * rows, rows), rows)
        pair_grad_ref[to, :] = jnp.zeros((rows, 2 * HEAD), jnp.bfloat16)
        return unused

    lax.fori_loop(first, stop, visit, 0)
    lax.fori_loop(jnp.maximum(first, stop), slot + pair_grad_ref.shape[0] // rows, unseen, 0)


def hand_out(pair_grad_ref, block_refs):
    rows = block_refs[0].shape[0]
    for at, block_ref in enumerate(block_refs):
        block_ref[...] = pair_grad_ref[at * rows : (at + 1) * rows, :]


def backward_far_kernel(
    place_ref, stats_ref, arrived_ref, acc_ref, grad_ref, grad_other_ref,
    query_ref, query_other_ref, pairs_ref, kept_ref,
    out_ref, scaled_ref, turned_scaled_ref, delta_ref, total_ref, *rest, split,
):
    *block_refs, move_ref, stacked_ref, pair_grad_ref, weights_ref, kept_sem = rest
    rows = out_ref.shape[0]
    heads = grad_ref.shape[1] // HEAD
    groups = 2 * heads
    copy = fetch(split, kept_ref, weights_ref, kept_sem, rows)
    last = last_of(begins_of(place_ref), place_ref, rows)
    fetch_all(split, last + 1, copy)
    stack(stacked_ref, (query_ref, query_other_ref))
    total_ref[...] = jnp.zeros_like(total_ref)
    for group in range(groups):
        span = slice(group * rows, (group + 1) * rows)
        there = (group + heads) % groups
        theirs = slice(there * rows, (there + 1) * rows)
        other_log = arrived_ref[HEAD : HEAD + 1, theirs].astype(jnp.float32)
        for part in range(1, 3):
            other_log += arrived_ref[HEAD + part : HEAD + part + 1, theirs].astype(jnp.float32)
        own_top, own_log = stats_ref[0:1, span], stats_ref[1:2, span]
        most = jnp.maximum(own_log, other_log)
        log_totals = most + jnp.log2(jnp.exp2(own_log - most) + jnp.exp2(other_log - most))
        result = acc_ref[:HEAD, span] * jnp.exp2(own_log - log_totals) + arrived_ref[
            :HEAD, theirs
        ].astype(jnp.float32) * jnp.exp2(other_log - log_totals)
        result = result.astype(jnp.bfloat16)
        column = slice(group % heads * HEAD, (group % heads + 1) * HEAD)
        if group < heads:
            out_ref[:, column] = result.T
        grads = (grad_ref if group < heads else grad_other_ref)[:, column].T
        scaled = grads.astype(jnp.float32) * jnp.exp2(own_top - log_totals)
        delta_ref[:, span] = jnp.sum(result.astype(jnp.float32) * scaled, axis=0, keepdims=True)
        low = scaled.astype(jnp.bfloat16)
        turned_scaled_ref[:, span] = low
        scaled_ref[span, :] = low.T
    accumulate(
        split, last + 1, pairs_ref, weights_ref, copy, stacked_ref,
        scaled_ref, turned_scaled_ref, delta_ref, total_ref, move_ref, pair_grad_ref, split,
    )
    hand_out(pair_grad_ref, block_refs)


def backward_near_kernel(
    place_ref, scaled_ref, turned_scaled_ref, delta_ref, begun_ref,
    query_ref, query_other_ref, pairs_ref, kept_ref, *rest, first, ends,
):
    *out_refs, move_ref, stacked_ref, pair_grad_ref, weights_ref, kept_sem = rest
    rows = query_ref.shape[0]
    groups = turned_scaled_ref.shape[1] // rows
    heads = groups // 2
    root = 1.0 / math.sqrt(HEAD)
    if ends:
        query_grad_ref, query_grad_other_ref, *block_refs, total_ref = out_refs
    else:
        total_ref, *block_refs = out_refs
    stop = jnp.minimum(last_of(begins_of(place_ref), place_ref, rows) + 1, first + len(block_refs))
    copy = fetch(first, kept_ref, weights_ref, kept_sem, rows)
    fetch_all(first, stop, copy)
    stack(stacked_ref, (query_ref, query_other_ref))
    total_ref[...] = begun_ref[...]
    accumulate(
        first, stop, pairs_ref, weights_ref, copy, stacked_ref,
        scaled_ref, turned_scaled_ref, delta_ref, total_ref, move_ref, pair_grad_ref, first,
    )
    hand_out(pair_grad_ref, block_refs)
    if ends:
        for group in range(groups):
            span = slice(group * rows, (group + 1) * rows)
            column = slice(group % heads * HEAD, (group % heads + 1) * HEAD)
            to_ref = query_grad_ref if group < heads else query_grad_other_ref
            to_ref[:, column] = (total_ref[:, span] * root).astype(jnp.bfloat16).T


def smem():
    return pl.BlockSpec(memory_space=pltpu.SMEM)


def vmem():
    return pl.BlockSpec(memory_space=pltpu.VMEM)


def hbm():
    return pl.BlockSpec(memory_space=pltpu.HBM)


def swap_cores(value):
    return lax.ppermute(value, "core", [(0, 1), (1, 0)])


def cost(blocks, rows, wide, matmuls):
    return pl.CostEstimate(
        flops=2 * matmuls * blocks * rows * wide * HEAD,
        transcendentals=0,
        bytes_accessed=2 * blocks * rows * wide,
    )


def attend(place, queries, grad, blocks, split, send, swap=swap_cores):
    slots = len(blocks)
    rows, columns = queries[0].shape
    heads = columns // HEAD
    wide = 2 * heads * rows
    blocks, queries = lax.optimization_barrier((blocks, queries))
    blocks = [pltpu.with_memory_space_constraint(block, pltpu.HBM) for block in blocks]
    weights, pairs, acc, stats, sent = pl.pallas_call(
        forward_kernel,
        out_shape=(
            pltpu.HBM((slots * rows, wide), jnp.bfloat16),
            jax.ShapeDtypeStruct((slots * rows, 2 * HEAD), jnp.bfloat16),
            jax.ShapeDtypeStruct((HEAD + EXTRA, wide), jnp.float32),
            jax.ShapeDtypeStruct((8, wide), jnp.float32),
            jax.ShapeDtypeStruct((HEAD + EXTRA, wide), jnp.bfloat16),
        ),
        in_specs=[smem()] + [hbm(), vmem()] + [hbm()] * slots,
        out_specs=(hbm(),) + (vmem(),) * 4,
        scratch_shapes=[
            pltpu.VMEM((slots * rows, wide), jnp.float32),
            pltpu.VMEM((8, wide), jnp.float32),
            pltpu.VMEM((slots * rows, wide), jnp.bfloat16),
            pltpu.VMEM((HEAD, wide), jnp.bfloat16),
            pltpu.VMEM((2, 1, rows), jnp.int32),
            pltpu.VMEM((rows, columns), jnp.bfloat16),
            pltpu.SemaphoreType.DMA((slots,)),
            pltpu.SemaphoreType.DMA((slots,)),
            pltpu.SemaphoreType.DMA,
        ],
        compiler_params=pltpu.CompilerParams(vmem_limit_bytes=36 << 20),
        cost_estimate=cost(slots, rows, wide, 2),
        name="attend_forward",
    )(place, pltpu.with_memory_space_constraint(queries[0], pltpu.HBM), queries[1], *blocks)
    weights = pltpu.with_memory_space_constraint(weights, pltpu.HBM)
    arrived = swap(sent)
    grad, stats = lax.optimization_barrier((grad, stats))
    grad_other = swap(grad)
    half = jax.ShapeDtypeStruct((rows, columns), jnp.bfloat16)
    params = pltpu.CompilerParams(vmem_limit_bytes=20 << 20)
    move = pltpu.VMEM((rows, wide), jnp.bfloat16)

    def held(blocks):
        return [
            pltpu.VMEM((wide, HEAD), jnp.bfloat16),
            pltpu.VMEM((blocks * rows, 2 * HEAD), jnp.bfloat16),
            pltpu.VMEM((blocks * rows, wide), jnp.bfloat16),
            pltpu.SemaphoreType.DMA((blocks,)),
        ]

    block = jax.ShapeDtypeStruct((rows, 2 * HEAD), jnp.bfloat16)
    out, scaled, turned_scaled, delta, total, *far = pl.pallas_call(
        functools.partial(backward_far_kernel, split=split),
        out_shape=(
            half,
            jax.ShapeDtypeStruct((wide, HEAD), jnp.bfloat16),
            jax.ShapeDtypeStruct((HEAD, wide), jnp.bfloat16),
            jax.ShapeDtypeStruct((1, wide), jnp.float32),
            jax.ShapeDtypeStruct((HEAD, wide), jnp.float32),
        )
        + (block,) * (slots - split),
        in_specs=[smem()] + [vmem()] * 8 + [hbm()],
        out_specs=(vmem(),) * (5 + slots - split),
        scratch_shapes=[move] + held(slots - split),
        compiler_params=params,
        cost_estimate=cost(slots - split, rows, wide, 4),
        name="attend_backward_far",
    )(place, stats, arrived, acc, grad, grad_other, *queries, pairs, weights)
    sent_far = send(far, split)
    whole = jax.ShapeDtypeStruct((HEAD, wide), jnp.float32)

    def near_call(total, first, count, outs, scratch, ends, name):
        return pl.pallas_call(
            functools.partial(backward_near_kernel, first=first, ends=ends),
            out_shape=outs + (block,) * count,
            in_specs=[smem()] + [vmem()] * 7 + [hbm()],
            out_specs=(vmem(),) * (len(outs) + count),
            scratch_shapes=scratch + [move] + held(count),
            compiler_params=params,
            cost_estimate=cost(count, rows, wide, 4),
            name=name,
        )(place, scaled, turned_scaled, delta, total, *queries, pairs, weights)

    total, *near = near_call(total, 1, split - 1, (whole,), [], False, "attend_backward_near")
    sent_near = send(near, 1)
    query_grad, query_grad_other, own = near_call(
        total, 0, 1, (half, half), [pltpu.VMEM((HEAD, wide), jnp.float32)], True,
        "attend_backward_own",
    )
    return out, query_grad, query_grad_other, own, sent_near, sent_far


def per_device(query, keys_values, doc_lengths, incoming_output_grad):
    chips = lax.axis_size("chip")
    query = query[0, :, 0, :]
    pairs = keys_values[0, :, 0, :]
    rows = query.shape[0]
    reach = min((LONGEST + 2 * rows - 1) // (2 * rows), chips - 1)
    slots = reach + 1
    blocks = [pairs] + [
        lax.ppermute(pairs, "chip", [(c, c + back) for c in range(chips - back)])
        for back in range(1, slots)
    ]
    sections = lax.axis_size("pipe")
    arrived = lax.ppermute(
        incoming_output_grad, "pipe", [(s, (s - 1) % sections) for s in range(sections)]
    )
    arrived, *blocks[1:3] = lax.optimization_barrier((arrived, *blocks[1:3]))
    grad = lax.all_to_all(arrived, "tensor", split_axis=2, concat_axis=1, tiled=True)[0, :, 0, :]
    position = jnp.stack([lax.axis_index("chip"), lax.axis_index("core")]).astype(jnp.int32)
    place = jnp.concatenate([position, doc_lengths[0]])
    split = (slots + 1) // 2

    def send(blocks, first):
        return [
            lax.ppermute(block, "chip", [(c, c - first - at) for c in range(first + at, chips)])
            for at, block in reversed(list(enumerate(blocks)))
        ]

    out, query_grad, query_grad_other, own, near, far = attend(
        place, (query, swap_cores(query)), grad, blocks, split, send
    )
    query_grad = query_grad.astype(jnp.float32) + swap_cores(query_grad_other).astype(jnp.float32)
    query_grad = query_grad.astype(jnp.bfloat16)
    sums = own.astype(jnp.float32)
    for sent in far:
        sums += sent.astype(jnp.float32)
    sums = lax.optimization_barrier(sums)
    for sent in near:
        sums += sent.astype(jnp.float32)
    pair_grad = sums.astype(jnp.bfloat16)
    return (out[None, :, None, :], query_grad[None, :, None, :], pair_grad[None, :, None, :])


def solution(mesh):
    shape = mesh.devices.shape
    split = Mesh(
        mesh.devices.reshape((shape[0] // 2, 2) + shape[1:]), ("chip", "core", "tensor", "pipe")
    )
    dp = ("chip", "core")
    by_head = P("pipe", dp, "tensor", None)
    in_specs = (by_head, by_head, P("pipe", None), P("pipe", dp + ("tensor",), None, None))
    return jax.shard_map(
        per_device, mesh=split, in_specs=in_specs, out_specs=(by_head,) * 3, check_vma=False
    )
```

```python
import functools
import math

import jax
import jax.numpy as jnp
from jax import lax
from jax.experimental import pallas as pl
from jax.experimental.pallas import tpu as pltpu
from jax.sharding import Mesh, PartitionSpec as P

NEG_LARGE = -1e30
LOG2E = math.log2(math.e)
HEAD = 128
LONGEST = 3072
EXTRA = 16


def matmul(left, right):
    return jnp.dot(left, right, preferred_element_type=jnp.float32)


def fold(array):
    return array.reshape(array.shape[0] // 8, 8, array.shape[1])


def begins_of(place_ref):
    begins = [jnp.int32(0)]
    for at in range(2, place_ref.shape[0] - 1):
        begins.append(begins[-1] + place_ref[at])
    return begins


def start_of(position, begins):
    start = jnp.zeros_like(position)
    for begin in begins:
        start = jnp.where(begin <= position, begin, start)
    return start


def last_of(begins, place_ref, rows):
    chip, core = place_ref[0], place_ref[1]
    first = start_of(2 * chip * rows, begins)
    return lax.div(2 * chip + core - lax.div(first, jnp.int32(rows)), jnp.int32(2))


def clear_of(begins, place_ref, rows):
    chip, core = place_ref[0], place_ref[1]
    start = start_of((2 * chip + 2) * rows - 1, begins)
    blocks = 2 * chip + core - lax.div(start + rows - 1, jnp.int32(rows))
    return jnp.maximum(lax.div(blocks, jnp.int32(2)), 0)


def stack(to_ref, query_refs):
    rows = query_refs[0].shape[0]
    heads = query_refs[0].shape[1] // HEAD
    for group in range(2 * heads):
        column = slice(group % heads * HEAD, (group % heads + 1) * HEAD)
        to_ref[group * rows : (group + 1) * rows, :] = query_refs[group // heads][:, column]


def forward_kernel(
    place_ref, query_hbm_ref, query_other_ref, *rest,
):
    *block_refs, kept_ref, pairs_ref, acc_ref, stats_ref, sent_ref = rest[:-9]
    scores_ref, top_ref, weights_ref, turned_ref, starts_ref, query_ref = rest[-9:-3]
    kept_sem, block_sem, query_sem = rest[-3:]
    rows = query_ref.shape[0]
    heads = query_ref.shape[1] // HEAD
    groups = 2 * heads
    scale = LOG2E / math.sqrt(HEAD)
    own_rows = pltpu.make_async_copy(query_hbm_ref, query_ref, query_sem)
    own_rows.start()
    begins = begins_of(place_ref)
    last, clear = last_of(begins, place_ref, rows), clear_of(begins, place_ref, rows)
    own = 2 * place_ref[0] + place_ref[1]
    shards = (own, 2 * place_ref[0] + 1 - place_ref[1])

    def bring(block_ref, back):
        to = pl.ds(pl.multiple_of(back * rows, rows), rows)
        return pltpu.make_async_copy(block_ref, pairs_ref.at[to], block_sem.at[back])

    for back, block_ref in enumerate(block_refs):
        @pl.when(back <= last)
        def start():
            bring(block_ref, back).start()

    along = lax.broadcasted_iota(jnp.int32, (1, rows), 1)
    for slot, rows_ref in ((1, query_other_ref), (0, query_ref)):
        if slot == 0:
            own_rows.wait()
        starts_ref[slot] = start_of(shards[slot] * rows + along, begins)
        for head in range(heads):
            span = slice((slot * heads + head) * rows, (slot * heads + head + 1) * rows)
            turned_ref[:, span] = rows_ref[:, head * HEAD : (head + 1) * HEAD].T
    top_ref[...] = jnp.full_like(top_ref, NEG_LARGE)
    acc_ref[...] = jnp.zeros_like(acc_ref)

    def measure(back, masked, count=1):
        to = pl.ds(pl.multiple_of(back * rows, rows), count * rows)
        for more in range(count):
            bring(block_refs[0], back + more).wait()
        keys = pairs_ref[to, :HEAD]
        allowed = []
        if masked:
            key_pos = (own - 2 * back) * rows + lax.broadcasted_iota(jnp.int32, (rows, rows), 0)
            across = lax.broadcasted_iota(jnp.int32, (rows, rows), 1)
            for slot in range(2):
                query_pos = shards[slot] * rows + across
                allowed.append((key_pos <= query_pos) & (key_pos >= starts_ref[slot]))
        for group in range(groups):
            span = slice(group * rows, (group + 1) * rows)
            scores = matmul(keys, turned_ref[:, span])
            if masked:
                scores = jnp.where(allowed[group // heads], scores, NEG_LARGE)
            scores_ref[to, span] = scores
            top_ref[:, span] = jnp.maximum(top_ref[:, span], jnp.max(fold(scores), axis=0))

    def masked(step, unused):
        measure(jnp.where(step == 0, 0, clear + step), True)
        return unused

    def plain(back, unused):
        measure(back, False)
        return unused

    def two_plain(pair, unused):
        measure(1 + 2 * pair, False, 2)
        return unused

    lax.fori_loop(0, last - clear + 1, masked, 0)
    twos = lax.div(clear, jnp.int32(2))
    lax.fori_loop(0, twos, two_plain, 0)
    lax.fori_loop(1 + 2 * twos, clear + 1, plain, 0)
    top = jnp.max(top_ref[...], axis=0, keepdims=True) * scale
    top_ref[...] = jnp.broadcast_to(top, top_ref.shape)

    def weigh(back, count):
        to = pl.ds(pl.multiple_of(back * rows, rows), count * rows)
        turned_values = jnp.concatenate(
            [pairs_ref[to, HEAD:].T, jnp.ones((16, count * rows), jnp.bfloat16)], axis=0
        )
        for group in range(groups):
            span = slice(group * rows, (group + 1) * rows)
            weights_ref[to, span] = jnp.exp2(
                scores_ref[to, span] * scale - top_ref[:1, span]
            ).astype(jnp.bfloat16)
        for more in range(count):
            keep(back + more).start()
        acc_ref[...] += matmul(turned_values, weights_ref[to, :])

    def weigh_two(pair, unused):
        weigh(2 * pair, 2)
        return unused

    def weigh_one(back, unused):
        weigh(back, 1)
        return unused

    def keep(back):
        to = pl.ds(pl.multiple_of(back * rows, rows), rows)
        return pltpu.make_async_copy(weights_ref.at[to], kept_ref.at[to], kept_sem.at[back])

    def kept(back, unused):
        keep(back).wait()
        return unused

    twos = lax.div(last + 1, jnp.int32(2))
    lax.fori_loop(0, twos, weigh_two, 0)
    lax.fori_loop(2 * twos, last + 1, weigh_one, 0)
    totals = acc_ref[HEAD : HEAD + 1, :]
    log_totals = top_ref[:1, :] + jnp.log2(totals)
    stats_ref[...] = jnp.concatenate([top_ref[:1, :], log_totals] + [top] * 6, axis=0)
    parts, rest = [], log_totals
    for _ in range(3):
        parts.append(rest.astype(jnp.bfloat16))
        rest = rest - parts[-1].astype(jnp.float32)
    sent_ref[HEAD:, :] = jnp.concatenate(
        parts + [jnp.zeros((EXTRA - 3, totals.shape[1]), jnp.bfloat16)], axis=0
    )
    inverse = 1.0 / totals
    for group in range(groups):
        span = slice(group * rows, (group + 1) * rows)
        result = acc_ref[:HEAD, span] * inverse[:, span]
        acc_ref[:HEAD, span] = result
        sent_ref[:HEAD, span] = result.astype(jnp.bfloat16)
    lax.fori_loop(0, last + 1, kept, 0)


def fetch(slot, kept_ref, weights_ref, kept_sem, rows):
    def copy(back):
        of = pl.ds(pl.multiple_of(back * rows, rows), rows)
        to = pl.ds(pl.multiple_of((back - slot) * rows, rows), rows)
        return pltpu.make_async_copy(kept_ref.at[of], weights_ref.at[to], kept_sem.at[back - slot])

    return copy


def fetch_all(first, stop, copy):
    def start(back, unused):
        copy(back).start()
        return unused

    lax.fori_loop(first, stop, start, 0)


def accumulate(
    first, stop, pairs_ref, weights_ref, copy, query_ref,
    scaled_ref, turned_scaled_ref, delta_ref, total_ref, move_ref, pair_grad_ref, slot,
):
    rows = move_ref.shape[0]
    groups = move_ref.shape[1] // rows
    root = 1.0 / math.sqrt(HEAD)

    def visit(back, unused):
        at = pl.ds(pl.multiple_of(back * rows, rows), rows)
        to = pl.ds(pl.multiple_of((back - slot) * rows, rows), rows)
        values = pairs_ref[at, HEAD:]
        turned_keys = pairs_ref[at, :HEAD].T
        copy(back).wait()
        for group in range(groups):
            span = slice(group * rows, (group + 1) * rows)
            prob_grad = matmul(values, turned_scaled_ref[:, span])
            move_ref[:, span] = (
                weights_ref[to, span].astype(jnp.float32) * (prob_grad - delta_ref[:, span])
            ).astype(jnp.bfloat16)
        pair_grad_ref[to, HEAD:] = matmul(weights_ref[to, :], scaled_ref[...]).astype(jnp.bfloat16)
        pair_grad_ref[to, :HEAD] = (matmul(move_ref[...], query_ref[...]) * root).astype(
            jnp.bfloat16
        )
        total_ref[...] += matmul(turned_keys, move_ref[...])
        return unused

    def unseen(back, unused):
        to = pl.ds(pl.multiple_of((back - slot) * rows, rows), rows)
        pair_grad_ref[to, :] = jnp.zeros((rows, 2 * HEAD), jnp.bfloat16)
        return unused

    lax.fori_loop(first, stop, visit, 0)
    lax.fori_loop(jnp.maximum(first, stop), slot + pair_grad_ref.shape[0] // rows, unseen, 0)


def hand_out(pair_grad_ref, block_refs):
    rows = block_refs[0].shape[0]
    for at, block_ref in enumerate(block_refs):
        block_ref[...] = pair_grad_ref[at * rows : (at + 1) * rows, :]


def backward_far_kernel(
    place_ref, stats_ref, arrived_ref, acc_ref, grad_ref, grad_other_ref,
    query_ref, query_other_ref, pairs_ref, kept_ref,
    out_ref, scaled_ref, turned_scaled_ref, delta_ref, total_ref, *rest, split,
):
    *block_refs, move_ref, stacked_ref, pair_grad_ref, weights_ref, kept_sem = rest
    rows = out_ref.shape[0]
    heads = grad_ref.shape[1] // HEAD
    groups = 2 * heads
    copy = fetch(split, kept_ref, weights_ref, kept_sem, rows)
    last = last_of(begins_of(place_ref), place_ref, rows)
    fetch_all(split, last + 1, copy)
    stack(stacked_ref, (query_ref, query_other_ref))
    total_ref[...] = jnp.zeros_like(total_ref)
    for group in range(groups):
        span = slice(group * rows, (group + 1) * rows)
        there = (group + heads) % groups
        theirs = slice(there * rows, (there + 1) * rows)
        other_log = arrived_ref[HEAD : HEAD + 1, theirs].astype(jnp.float32)
        for part in range(1, 3):
            other_log += arrived_ref[HEAD + part : HEAD + part + 1, theirs].astype(jnp.float32)
        own_top, own_log = stats_ref[0:1, span], stats_ref[1:2, span]
        most = jnp.maximum(own_log, other_log)
        log_totals = most + jnp.log2(jnp.exp2(own_log - most) + jnp.exp2(other_log - most))
        result = acc_ref[:HEAD, span] * jnp.exp2(own_log - log_totals) + arrived_ref[
            :HEAD, theirs
        ].astype(jnp.float32) * jnp.exp2(other_log - log_totals)
        result = result.astype(jnp.bfloat16)
        column = slice(group % heads * HEAD, (group % heads + 1) * HEAD)
        if group < heads:
            out_ref[:, column] = result.T
        grads = (grad_ref if group < heads else grad_other_ref)[:, column].T
        scaled = grads.astype(jnp.float32) * jnp.exp2(own_top - log_totals)
        delta_ref[:, span] = jnp.sum(result.astype(jnp.float32) * scaled, axis=0, keepdims=True)
        low = scaled.astype(jnp.bfloat16)
        turned_scaled_ref[:, span] = low
        scaled_ref[span, :] = low.T
    accumulate(
        split, last + 1, pairs_ref, weights_ref, copy, stacked_ref,
        scaled_ref, turned_scaled_ref, delta_ref, total_ref, move_ref, pair_grad_ref, split,
    )
    hand_out(pair_grad_ref, block_refs)


def backward_near_kernel(
    place_ref, scaled_ref, turned_scaled_ref, delta_ref, begun_ref,
    query_ref, query_other_ref, pairs_ref, kept_ref, *rest, first, ends,
):
    *out_refs, move_ref, stacked_ref, pair_grad_ref, weights_ref, kept_sem = rest
    rows = query_ref.shape[0]
    groups = turned_scaled_ref.shape[1] // rows
    heads = groups // 2
    root = 1.0 / math.sqrt(HEAD)
    if ends:
        query_grad_ref, query_grad_other_ref, *block_refs, total_ref = out_refs
    else:
        total_ref, *block_refs = out_refs
    stop = jnp.minimum(last_of(begins_of(place_ref), place_ref, rows) + 1, first + len(block_refs))
    copy = fetch(first, kept_ref, weights_ref, kept_sem, rows)
    fetch_all(first, stop, copy)
    stack(stacked_ref, (query_ref, query_other_ref))
    total_ref[...] = begun_ref[...]
    accumulate(
        first, stop, pairs_ref, weights_ref, copy, stacked_ref,
        scaled_ref, turned_scaled_ref, delta_ref, total_ref, move_ref, pair_grad_ref, first,
    )
    hand_out(pair_grad_ref, block_refs)
    if ends:
        for group in range(groups):
            span = slice(group * rows, (group + 1) * rows)
            column = slice(group % heads * HEAD, (group % heads + 1) * HEAD)
            to_ref = query_grad_ref if group < heads else query_grad_other_ref
            to_ref[:, column] = (total_ref[:, span] * root).astype(jnp.bfloat16).T


def smem():
    return pl.BlockSpec(memory_space=pltpu.SMEM)


def vmem():
    return pl.BlockSpec(memory_space=pltpu.VMEM)


def hbm():
    return pl.BlockSpec(memory_space=pltpu.HBM)


def swap_cores(value):
    return lax.ppermute(value, "core", [(0, 1), (1, 0)])


def cost(blocks, rows, wide, matmuls):
    return pl.CostEstimate(
        flops=2 * matmuls * blocks * rows * wide * HEAD,
        transcendentals=0,
        bytes_accessed=2 * blocks * rows * wide,
    )


def attend(place, queries, grad, blocks, split, send, swap=swap_cores):
    slots = len(blocks)
    rows, columns = queries[0].shape
    heads = columns // HEAD
    wide = 2 * heads * rows
    blocks, queries = lax.optimization_barrier((blocks, queries))
    blocks = [pltpu.with_memory_space_constraint(block, pltpu.HBM) for block in blocks]
    weights, pairs, acc, stats, sent = pl.pallas_call(
        forward_kernel,
        out_shape=(
            pltpu.HBM((slots * rows, wide), jnp.bfloat16),
            jax.ShapeDtypeStruct((slots * rows, 2 * HEAD), jnp.bfloat16),
            jax.ShapeDtypeStruct((HEAD + EXTRA, wide), jnp.float32),
            jax.ShapeDtypeStruct((8, wide), jnp.float32),
            jax.ShapeDtypeStruct((HEAD + EXTRA, wide), jnp.bfloat16),
        ),
        in_specs=[smem()] + [hbm(), vmem()] + [hbm()] * slots,
        out_specs=(hbm(),) + (vmem(),) * 4,
        scratch_shapes=[
            pltpu.VMEM((slots * rows, wide), jnp.float32),
            pltpu.VMEM((8, wide), jnp.float32),
            pltpu.VMEM((slots * rows, wide), jnp.bfloat16),
            pltpu.VMEM((HEAD, wide), jnp.bfloat16),
            pltpu.VMEM((2, 1, rows), jnp.int32),
            pltpu.VMEM((rows, columns), jnp.bfloat16),
            pltpu.SemaphoreType.DMA((slots,)),
            pltpu.SemaphoreType.DMA((slots,)),
            pltpu.SemaphoreType.DMA,
        ],
        compiler_params=pltpu.CompilerParams(vmem_limit_bytes=36 << 20),
        cost_estimate=cost(slots, rows, wide, 2),
        name="attend_forward",
    )(place, pltpu.with_memory_space_constraint(queries[0], pltpu.HBM), queries[1], *blocks)
    weights = pltpu.with_memory_space_constraint(weights, pltpu.HBM)
    arrived = swap(sent)
    grad, stats = lax.optimization_barrier((grad, stats))
    grad_other = swap(grad)
    half = jax.ShapeDtypeStruct((rows, columns), jnp.bfloat16)
    params = pltpu.CompilerParams(vmem_limit_bytes=20 << 20)
    move = pltpu.VMEM((rows, wide), jnp.bfloat16)

    def held(blocks):
        return [
            pltpu.VMEM((wide, HEAD), jnp.bfloat16),
            pltpu.VMEM((blocks * rows, 2 * HEAD), jnp.bfloat16),
            pltpu.VMEM((blocks * rows, wide), jnp.bfloat16),
            pltpu.SemaphoreType.DMA((blocks,)),
        ]

    block = jax.ShapeDtypeStruct((rows, 2 * HEAD), jnp.bfloat16)
    out, scaled, turned_scaled, delta, total, *far = pl.pallas_call(
        functools.partial(backward_far_kernel, split=split),
        out_shape=(
            half,
            jax.ShapeDtypeStruct((wide, HEAD), jnp.bfloat16),
            jax.ShapeDtypeStruct((HEAD, wide), jnp.bfloat16),
            jax.ShapeDtypeStruct((1, wide), jnp.float32),
            jax.ShapeDtypeStruct((HEAD, wide), jnp.float32),
        )
        + (block,) * (slots - split),
        in_specs=[smem()] + [vmem()] * 8 + [hbm()],
        out_specs=(vmem(),) * (5 + slots - split),
        scratch_shapes=[move] + held(slots - split),
        compiler_params=params,
        cost_estimate=cost(slots - split, rows, wide, 4),
        name="attend_backward_far",
    )(place, stats, arrived, acc, grad, grad_other, *queries, pairs, weights)
    sent_far = send(far, split)
    whole = jax.ShapeDtypeStruct((HEAD, wide), jnp.float32)

    def near_call(total, first, count, outs, scratch, ends, name):
        return pl.pallas_call(
            functools.partial(backward_near_kernel, first=first, ends=ends),
            out_shape=outs + (block,) * count,
            in_specs=[smem()] + [vmem()] * 7 + [hbm()],
            out_specs=(vmem(),) * (len(outs) + count),
            scratch_shapes=scratch + [move] + held(count),
            compiler_params=params,
            cost_estimate=cost(count, rows, wide, 4),
            name=name,
        )(place, scaled, turned_scaled, delta, total, *queries, pairs, weights)

    total, *near = near_call(total, 1, split - 1, (whole,), [], False, "attend_backward_near")
    sent_near = send(near, 1)
    query_grad, query_grad_other, own = near_call(
        total, 0, 1, (half, half), [pltpu.VMEM((HEAD, wide), jnp.float32)], True,
        "attend_backward_own",
    )
    return out, query_grad, query_grad_other, own, sent_near, sent_far


def per_device(query, keys_values, doc_lengths, incoming_output_grad):
    chips = lax.axis_size("chip")
    query = query[0, :, 0, :]
    pairs = keys_values[0, :, 0, :]
    rows = query.shape[0]
    reach = min((LONGEST + 2 * rows - 1) // (2 * rows), chips - 1)
    slots = reach + 1
    blocks = [pairs] + [
        lax.ppermute(pairs, "chip", [(c, c + back) for c in range(chips - back)])
        for back in range(1, slots)
    ]
    sections = lax.axis_size("pipe")
    arrived = lax.ppermute(
        incoming_output_grad, "pipe", [(s, (s - 1) % sections) for s in range(sections)]
    )
    arrived, *blocks[-2:] = lax.optimization_barrier((arrived, *blocks[-2:]))
    grad = lax.all_to_all(arrived, "tensor", split_axis=2, concat_axis=1, tiled=True)[0, :, 0, :]
    position = jnp.stack([lax.axis_index("chip"), lax.axis_index("core")]).astype(jnp.int32)
    place = jnp.concatenate([position, doc_lengths[0]])
    split = (slots + 1) // 2

    def send(blocks, first):
        return [
            lax.ppermute(block, "chip", [(c, c - first - at) for c in range(first + at, chips)])
            for at, block in reversed(list(enumerate(blocks)))
        ]

    out, query_grad, query_grad_other, own, near, far = attend(
        place, (query, swap_cores(query)), grad, blocks, split, send
    )
    query_grad = query_grad.astype(jnp.float32) + swap_cores(query_grad_other).astype(jnp.float32)
    query_grad = query_grad.astype(jnp.bfloat16)
    sums = own.astype(jnp.float32)
    for sent in far:
        sums += sent.astype(jnp.float32)
    sums = lax.optimization_barrier(sums)
    for sent in near:
        sums += sent.astype(jnp.float32)
    pair_grad = sums.astype(jnp.bfloat16)
    return (out[None, :, None, :], query_grad[None, :, None, :], pair_grad[None, :, None, :])


def solution(mesh):
    shape = mesh.devices.shape
    split = Mesh(
        mesh.devices.reshape((shape[0] // 2, 2) + shape[1:]), ("chip", "core", "tensor", "pipe")
    )
    dp = ("chip", "core")
    by_head = P("pipe", dp, "tensor", None)
    in_specs = (by_head, by_head, P("pipe", None), P("pipe", dp + ("tensor",), None, None))
    return jax.shard_map(
        per_device, mesh=split, in_specs=in_specs, out_specs=(by_head,) * 3, check_vma=False
    )
```

```python
import functools
import math

import jax
import jax.numpy as jnp
from jax import lax
from jax.experimental import pallas as pl
from jax.experimental.pallas import tpu as pltpu
from jax.sharding import Mesh, PartitionSpec as P

NEG_LARGE = -1e30
LOG2E = math.log2(math.e)
HEAD = 128
LONGEST = 3072
EXTRA = 16


def matmul(left, right):
    return jnp.dot(left, right, preferred_element_type=jnp.float32)


def fold(array):
    return array.reshape(array.shape[0] // 8, 8, array.shape[1])


def begins_of(place_ref):
    begins = [jnp.int32(0)]
    for at in range(2, place_ref.shape[0] - 1):
        begins.append(begins[-1] + place_ref[at])
    return begins


def start_of(position, begins):
    start = jnp.zeros_like(position)
    for begin in begins:
        start = jnp.where(begin <= position, begin, start)
    return start


def last_of(begins, place_ref, rows):
    chip, core = place_ref[0], place_ref[1]
    first = start_of(2 * chip * rows, begins)
    return lax.div(2 * chip + core - lax.div(first, jnp.int32(rows)), jnp.int32(2))


def clear_of(begins, place_ref, rows):
    chip, core = place_ref[0], place_ref[1]
    start = start_of((2 * chip + 2) * rows - 1, begins)
    blocks = 2 * chip + core - lax.div(start + rows - 1, jnp.int32(rows))
    return jnp.maximum(lax.div(blocks, jnp.int32(2)), 0)


def stack(to_ref, query_refs):
    rows = query_refs[0].shape[0]
    heads = query_refs[0].shape[1] // HEAD
    for group in range(2 * heads):
        column = slice(group % heads * HEAD, (group % heads + 1) * HEAD)
        to_ref[group * rows : (group + 1) * rows, :] = query_refs[group // heads][:, column]


def forward_kernel(
    place_ref, query_hbm_ref, query_other_ref, *rest,
):
    *block_refs, kept_ref, pairs_ref, acc_ref, stats_ref, sent_ref = rest[:-9]
    scores_ref, top_ref, weights_ref, turned_ref, starts_ref, query_ref = rest[-9:-3]
    kept_sem, block_sem, query_sem = rest[-3:]
    rows = query_ref.shape[0]
    heads = query_ref.shape[1] // HEAD
    groups = 2 * heads
    scale = LOG2E / math.sqrt(HEAD)
    own_rows = pltpu.make_async_copy(query_hbm_ref, query_ref, query_sem)
    own_rows.start()
    begins = begins_of(place_ref)
    last, clear = last_of(begins, place_ref, rows), clear_of(begins, place_ref, rows)
    own = 2 * place_ref[0] + place_ref[1]
    shards = (own, 2 * place_ref[0] + 1 - place_ref[1])

    def bring(block_ref, back):
        to = pl.ds(pl.multiple_of(back * rows, rows), rows)
        return pltpu.make_async_copy(block_ref, pairs_ref.at[to], block_sem.at[back])

    for back, block_ref in enumerate(block_refs):
        @pl.when(back <= last)
        def start():
            bring(block_ref, back).start()

    along = lax.broadcasted_iota(jnp.int32, (1, rows), 1)
    for slot, rows_ref in ((1, query_other_ref), (0, query_ref)):
        if slot == 0:
            own_rows.wait()
        starts_ref[slot] = start_of(shards[slot] * rows + along, begins)
        for head in range(heads):
            span = slice((slot * heads + head) * rows, (slot * heads + head + 1) * rows)
            turned_ref[:, span] = rows_ref[:, head * HEAD : (head + 1) * HEAD].T
    top_ref[...] = jnp.full_like(top_ref, NEG_LARGE)
    acc_ref[...] = jnp.zeros_like(acc_ref)

    def measure(back, masked, count=1):
        to = pl.ds(pl.multiple_of(back * rows, rows), count * rows)
        for more in range(count):
            bring(block_refs[0], back + more).wait()
        keys = pairs_ref[to, :HEAD]
        allowed = []
        if masked:
            key_pos = (own - 2 * back) * rows + lax.broadcasted_iota(jnp.int32, (rows, rows), 0)
            across = lax.broadcasted_iota(jnp.int32, (rows, rows), 1)
            for slot in range(2):
                query_pos = shards[slot] * rows + across
                allowed.append((key_pos <= query_pos) & (key_pos >= starts_ref[slot]))
        for group in range(groups):
            span = slice(group * rows, (group + 1) * rows)
            scores = matmul(keys, turned_ref[:, span])
            if masked:
                scores = jnp.where(allowed[group // heads], scores, NEG_LARGE)
            scores_ref[to, span] = scores
            top_ref[:, span] = jnp.maximum(top_ref[:, span], jnp.max(fold(scores), axis=0))

    def masked(step, unused):
        measure(jnp.where(step == 0, 0, clear + step), True)
        return unused

    def plain(back, unused):
        measure(back, False)
        return unused

    def two_plain(pair, unused):
        measure(1 + 2 * pair, False, 2)
        return unused

    lax.fori_loop(0, last - clear + 1, masked, 0)
    twos = lax.div(clear, jnp.int32(2))
    lax.fori_loop(0, twos, two_plain, 0)
    lax.fori_loop(1 + 2 * twos, clear + 1, plain, 0)
    top = jnp.max(top_ref[...], axis=0, keepdims=True) * scale
    top_ref[...] = jnp.broadcast_to(top, top_ref.shape)

    def weigh(back, count):
        to = pl.ds(pl.multiple_of(back * rows, rows), count * rows)
        turned_values = jnp.concatenate(
            [pairs_ref[to, HEAD:].T, jnp.ones((16, count * rows), jnp.bfloat16)], axis=0
        )
        for group in range(groups):
            span = slice(group * rows, (group + 1) * rows)
            weights_ref[to, span] = jnp.exp2(
                scores_ref[to, span] * scale - top_ref[:1, span]
            ).astype(jnp.bfloat16)
        for more in range(count):
            keep(back + more).start()
        acc_ref[...] += matmul(turned_values, weights_ref[to, :])

    def weigh_two(pair, unused):
        weigh(2 * pair, 2)
        return unused

    def weigh_one(back, unused):
        weigh(back, 1)
        return unused

    def keep(back):
        to = pl.ds(pl.multiple_of(back * rows, rows), rows)
        return pltpu.make_async_copy(weights_ref.at[to], kept_ref.at[to], kept_sem.at[back])

    def kept(back, unused):
        keep(back).wait()
        return unused

    twos = lax.div(last + 1, jnp.int32(2))
    lax.fori_loop(0, twos, weigh_two, 0)
    lax.fori_loop(2 * twos, last + 1, weigh_one, 0)
    totals = acc_ref[HEAD : HEAD + 1, :]
    log_totals = top_ref[:1, :] + jnp.log2(totals)
    stats_ref[...] = jnp.concatenate([top_ref[:1, :], log_totals] + [top] * 6, axis=0)
    parts, rest = [], log_totals
    for _ in range(3):
        parts.append(rest.astype(jnp.bfloat16))
        rest = rest - parts[-1].astype(jnp.float32)
    sent_ref[HEAD:, :] = jnp.concatenate(
        parts + [jnp.zeros((EXTRA - 3, totals.shape[1]), jnp.bfloat16)], axis=0
    )
    inverse = 1.0 / totals
    for group in range(groups):
        span = slice(group * rows, (group + 1) * rows)
        result = acc_ref[:HEAD, span] * inverse[:, span]
        acc_ref[:HEAD, span] = result
        sent_ref[:HEAD, span] = result.astype(jnp.bfloat16)
    lax.fori_loop(0, last + 1, kept, 0)


def fetch(slot, kept_ref, weights_ref, kept_sem, rows):
    def copy(back):
        of = pl.ds(pl.multiple_of(back * rows, rows), rows)
        to = pl.ds(pl.multiple_of((back - slot) * rows, rows), rows)
        return pltpu.make_async_copy(kept_ref.at[of], weights_ref.at[to], kept_sem.at[back - slot])

    return copy


def fetch_all(first, stop, copy):
    def start(back, unused):
        copy(back).start()
        return unused

    lax.fori_loop(first, stop, start, 0)


def accumulate(
    first, stop, pairs_ref, weights_ref, copy, query_ref,
    scaled_ref, turned_scaled_ref, delta_ref, total_ref, move_ref, pair_grad_ref, slot,
):
    rows = move_ref.shape[0]
    groups = move_ref.shape[1] // rows
    root = 1.0 / math.sqrt(HEAD)

    def visit(back, unused):
        at = pl.ds(pl.multiple_of(back * rows, rows), rows)
        to = pl.ds(pl.multiple_of((back - slot) * rows, rows), rows)
        values = pairs_ref[at, HEAD:]
        turned_keys = pairs_ref[at, :HEAD].T
        copy(back).wait()
        for group in range(groups):
            span = slice(group * rows, (group + 1) * rows)
            prob_grad = matmul(values, turned_scaled_ref[:, span])
            move_ref[:, span] = (
                weights_ref[to, span].astype(jnp.float32) * (prob_grad - delta_ref[:, span])
            ).astype(jnp.bfloat16)
        pair_grad_ref[to, HEAD:] = matmul(weights_ref[to, :], scaled_ref[...]).astype(jnp.bfloat16)
        pair_grad_ref[to, :HEAD] = (matmul(move_ref[...], query_ref[...]) * root).astype(
            jnp.bfloat16
        )
        total_ref[...] += matmul(turned_keys, move_ref[...])
        return unused

    def unseen(back, unused):
        to = pl.ds(pl.multiple_of((back - slot) * rows, rows), rows)
        pair_grad_ref[to, :] = jnp.zeros((rows, 2 * HEAD), jnp.bfloat16)
        return unused

    lax.fori_loop(first, stop, visit, 0)
    lax.fori_loop(jnp.maximum(first, stop), slot + pair_grad_ref.shape[0] // rows, unseen, 0)


def hand_out(pair_grad_ref, block_refs):
    rows = block_refs[0].shape[0]
    for at, block_ref in enumerate(block_refs):
        block_ref[...] = pair_grad_ref[at * rows : (at + 1) * rows, :]


def backward_far_kernel(
    place_ref, stats_ref, arrived_ref, acc_ref, grad_ref, grad_other_ref,
    query_ref, query_other_ref, pairs_ref, kept_ref,
    out_ref, scaled_ref, turned_scaled_ref, delta_ref, total_ref, *rest, split,
):
    *block_refs, move_ref, stacked_ref, pair_grad_ref, weights_ref, kept_sem = rest
    rows = out_ref.shape[0]
    heads = grad_ref.shape[1] // HEAD
    groups = 2 * heads
    copy = fetch(split, kept_ref, weights_ref, kept_sem, rows)
    last = last_of(begins_of(place_ref), place_ref, rows)
    fetch_all(split, last + 1, copy)
    stack(stacked_ref, (query_ref, query_other_ref))
    total_ref[...] = jnp.zeros_like(total_ref)
    for group in range(groups):
        span = slice(group * rows, (group + 1) * rows)
        there = (group + heads) % groups
        theirs = slice(there * rows, (there + 1) * rows)
        other_log = arrived_ref[HEAD : HEAD + 1, theirs].astype(jnp.float32)
        for part in range(1, 3):
            other_log += arrived_ref[HEAD + part : HEAD + part + 1, theirs].astype(jnp.float32)
        own_top, own_log = stats_ref[0:1, span], stats_ref[1:2, span]
        most = jnp.maximum(own_log, other_log)
        log_totals = most + jnp.log2(jnp.exp2(own_log - most) + jnp.exp2(other_log - most))
        result = acc_ref[:HEAD, span] * jnp.exp2(own_log - log_totals) + arrived_ref[
            :HEAD, theirs
        ].astype(jnp.float32) * jnp.exp2(other_log - log_totals)
        result = result.astype(jnp.bfloat16)
        column = slice(group % heads * HEAD, (group % heads + 1) * HEAD)
        if group < heads:
            out_ref[:, column] = result.T
        grads = (grad_ref if group < heads else grad_other_ref)[:, column].T
        scaled = grads.astype(jnp.float32) * jnp.exp2(own_top - log_totals)
        delta_ref[:, span] = jnp.sum(result.astype(jnp.float32) * scaled, axis=0, keepdims=True)
        low = scaled.astype(jnp.bfloat16)
        turned_scaled_ref[:, span] = low
        scaled_ref[span, :] = low.T
    accumulate(
        split, last + 1, pairs_ref, weights_ref, copy, stacked_ref,
        scaled_ref, turned_scaled_ref, delta_ref, total_ref, move_ref, pair_grad_ref, split,
    )
    hand_out(pair_grad_ref, block_refs)


def backward_near_kernel(
    place_ref, scaled_ref, turned_scaled_ref, delta_ref, begun_ref,
    query_ref, query_other_ref, pairs_ref, kept_ref, *rest, first, ends,
):
    *out_refs, move_ref, stacked_ref, pair_grad_ref, weights_ref, kept_sem = rest
    rows = query_ref.shape[0]
    groups = turned_scaled_ref.shape[1] // rows
    heads = groups // 2
    root = 1.0 / math.sqrt(HEAD)
    if ends:
        query_grad_ref, query_grad_other_ref, *block_refs, total_ref = out_refs
    else:
        total_ref, *block_refs = out_refs
    stop = jnp.minimum(last_of(begins_of(place_ref), place_ref, rows) + 1, first + len(block_refs))
    copy = fetch(first, kept_ref, weights_ref, kept_sem, rows)
    fetch_all(first, stop, copy)
    stack(stacked_ref, (query_ref, query_other_ref))
    total_ref[...] = begun_ref[...]
    accumulate(
        first, stop, pairs_ref, weights_ref, copy, stacked_ref,
        scaled_ref, turned_scaled_ref, delta_ref, total_ref, move_ref, pair_grad_ref, first,
    )
    hand_out(pair_grad_ref, block_refs)
    if ends:
        for group in range(groups):
            span = slice(group * rows, (group + 1) * rows)
            column = slice(group % heads * HEAD, (group % heads + 1) * HEAD)
            to_ref = query_grad_ref if group < heads else query_grad_other_ref
            to_ref[:, column] = (total_ref[:, span] * root).astype(jnp.bfloat16).T


def smem():
    return pl.BlockSpec(memory_space=pltpu.SMEM)


def vmem():
    return pl.BlockSpec(memory_space=pltpu.VMEM)


def hbm():
    return pl.BlockSpec(memory_space=pltpu.HBM)


def swap_cores(value):
    return lax.ppermute(value, "core", [(0, 1), (1, 0)])


def cost(blocks, rows, wide, matmuls):
    return pl.CostEstimate(
        flops=2 * matmuls * blocks * rows * wide * HEAD,
        transcendentals=0,
        bytes_accessed=2 * blocks * rows * wide,
    )


def attend(place, queries, grad, blocks, split, send, swap=swap_cores):
    slots = len(blocks)
    rows, columns = queries[0].shape
    heads = columns // HEAD
    wide = 2 * heads * rows
    blocks, queries = lax.optimization_barrier((blocks, queries))
    blocks = [pltpu.with_memory_space_constraint(block, pltpu.HBM) for block in blocks]
    weights, pairs, acc, stats, sent = pl.pallas_call(
        forward_kernel,
        out_shape=(
            pltpu.HBM((slots * rows, wide), jnp.bfloat16),
            jax.ShapeDtypeStruct((slots * rows, 2 * HEAD), jnp.bfloat16),
            jax.ShapeDtypeStruct((HEAD + EXTRA, wide), jnp.float32),
            jax.ShapeDtypeStruct((8, wide), jnp.float32),
            jax.ShapeDtypeStruct((HEAD + EXTRA, wide), jnp.bfloat16),
        ),
        in_specs=[smem()] + [hbm(), vmem()] + [hbm()] * slots,
        out_specs=(hbm(),) + (vmem(),) * 4,
        scratch_shapes=[
            pltpu.VMEM((slots * rows, wide), jnp.float32),
            pltpu.VMEM((8, wide), jnp.float32),
            pltpu.VMEM((slots * rows, wide), jnp.bfloat16),
            pltpu.VMEM((HEAD, wide), jnp.bfloat16),
            pltpu.VMEM((2, 1, rows), jnp.int32),
            pltpu.VMEM((rows, columns), jnp.bfloat16),
            pltpu.SemaphoreType.DMA((slots,)),
            pltpu.SemaphoreType.DMA((slots,)),
            pltpu.SemaphoreType.DMA,
        ],
        compiler_params=pltpu.CompilerParams(vmem_limit_bytes=36 << 20),
        cost_estimate=cost(slots, rows, wide, 2),
        name="attend_forward",
    )(place, pltpu.with_memory_space_constraint(queries[0], pltpu.HBM), queries[1], *blocks)
    weights = pltpu.with_memory_space_constraint(weights, pltpu.HBM)
    arrived = swap(sent)
    grad, stats = lax.optimization_barrier((grad, stats))
    grad_other = swap(grad)
    half = jax.ShapeDtypeStruct((rows, columns), jnp.bfloat16)
    params = pltpu.CompilerParams(vmem_limit_bytes=20 << 20)
    move = pltpu.VMEM((rows, wide), jnp.bfloat16)

    def held(blocks):
        return [
            pltpu.VMEM((wide, HEAD), jnp.bfloat16),
            pltpu.VMEM((blocks * rows, 2 * HEAD), jnp.bfloat16),
            pltpu.VMEM((blocks * rows, wide), jnp.bfloat16),
            pltpu.SemaphoreType.DMA((blocks,)),
        ]

    block = jax.ShapeDtypeStruct((rows, 2 * HEAD), jnp.bfloat16)
    out, scaled, turned_scaled, delta, total, *far = pl.pallas_call(
        functools.partial(backward_far_kernel, split=split),
        out_shape=(
            half,
            jax.ShapeDtypeStruct((wide, HEAD), jnp.bfloat16),
            jax.ShapeDtypeStruct((HEAD, wide), jnp.bfloat16),
            jax.ShapeDtypeStruct((1, wide), jnp.float32),
            jax.ShapeDtypeStruct((HEAD, wide), jnp.float32),
        )
        + (block,) * (slots - split),
        in_specs=[smem()] + [vmem()] * 8 + [hbm()],
        out_specs=(vmem(),) * (5 + slots - split),
        scratch_shapes=[move] + held(slots - split),
        compiler_params=params,
        cost_estimate=cost(slots - split, rows, wide, 4),
        name="attend_backward_far",
    )(place, stats, arrived, acc, grad, grad_other, *queries, pairs, weights)
    sent_far = send(far, split)
    whole = jax.ShapeDtypeStruct((HEAD, wide), jnp.float32)

    def near_call(total, first, count, outs, scratch, ends, name):
        return pl.pallas_call(
            functools.partial(backward_near_kernel, first=first, ends=ends),
            out_shape=outs + (block,) * count,
            in_specs=[smem()] + [vmem()] * 7 + [hbm()],
            out_specs=(vmem(),) * (len(outs) + count),
            scratch_shapes=scratch + [move] + held(count),
            compiler_params=params,
            cost_estimate=cost(count, rows, wide, 4),
            name=name,
        )(place, scaled, turned_scaled, delta, total, *queries, pairs, weights)

    query_grad, query_grad_other, own, *near = near_call(
        total, 0, split, (half, half), [pltpu.VMEM((HEAD, wide), jnp.float32)], True,
        "attend_backward_near",
    )
    sent_near = send(near, 1)
    return out, query_grad, query_grad_other, own, sent_near, sent_far


def per_device(query, keys_values, doc_lengths, incoming_output_grad):
    chips = lax.axis_size("chip")
    query = query[0, :, 0, :]
    pairs = keys_values[0, :, 0, :]
    rows = query.shape[0]
    reach = min((LONGEST + 2 * rows - 1) // (2 * rows), chips - 1)
    slots = reach + 1
    blocks = [pairs] + [
        lax.ppermute(pairs, "chip", [(c, c + back) for c in range(chips - back)])
        for back in range(1, slots)
    ]
    sections = lax.axis_size("pipe")
    arrived = lax.ppermute(
        incoming_output_grad, "pipe", [(s, (s - 1) % sections) for s in range(sections)]
    )
    arrived, *blocks[1:3] = lax.optimization_barrier((arrived, *blocks[1:3]))
    grad = lax.all_to_all(arrived, "tensor", split_axis=2, concat_axis=1, tiled=True)[0, :, 0, :]
    position = jnp.stack([lax.axis_index("chip"), lax.axis_index("core")]).astype(jnp.int32)
    place = jnp.concatenate([position, doc_lengths[0]])
    split = (slots + 1) // 2

    def send(blocks, first):
        return [
            lax.ppermute(block, "chip", [(c, c - first - at) for c in range(first + at, chips)])
            for at, block in reversed(list(enumerate(blocks)))
        ]

    out, query_grad, query_grad_other, own, near, far = attend(
        place, (query, swap_cores(query)), grad, blocks, split, send
    )
    query_grad = query_grad.astype(jnp.float32) + swap_cores(query_grad_other).astype(jnp.float32)
    query_grad = query_grad.astype(jnp.bfloat16)
    sums = own.astype(jnp.float32)
    for sent in far:
        sums += sent.astype(jnp.float32)
    sums = lax.optimization_barrier(sums)
    for sent in near:
        sums += sent.astype(jnp.float32)
    pair_grad = sums.astype(jnp.bfloat16)
    return (out[None, :, None, :], query_grad[None, :, None, :], pair_grad[None, :, None, :])


def solution(mesh):
    shape = mesh.devices.shape
    split = Mesh(
        mesh.devices.reshape((shape[0] // 2, 2) + shape[1:]), ("chip", "core", "tensor", "pipe")
    )
    dp = ("chip", "core")
    by_head = P("pipe", dp, "tensor", None)
    in_specs = (by_head, by_head, P("pipe", None), P("pipe", dp + ("tensor",), None, None))
    return jax.shard_map(
        per_device, mesh=split, in_specs=in_specs, out_specs=(by_head,) * 3, check_vma=False
    )
```

```python
import functools
import math

import jax
import jax.numpy as jnp
from jax import lax
from jax.experimental import pallas as pl
from jax.experimental.pallas import tpu as pltpu
from jax.sharding import Mesh, PartitionSpec as P

NEG_LARGE = -1e30
LOG2E = math.log2(math.e)
HEAD = 128
LONGEST = 3072
EXTRA = 16


def matmul(left, right):
    return jnp.dot(left, right, preferred_element_type=jnp.float32)


def fold(array):
    return array.reshape(array.shape[0] // 8, 8, array.shape[1])


def begins_of(place_ref):
    begins = [jnp.int32(0)]
    for at in range(2, place_ref.shape[0] - 1):
        begins.append(begins[-1] + place_ref[at])
    return begins


def start_of(position, begins):
    start = jnp.zeros_like(position)
    for begin in begins:
        start = jnp.where(begin <= position, begin, start)
    return start


def last_of(begins, place_ref, rows):
    chip, core = place_ref[0], place_ref[1]
    first = start_of(2 * chip * rows, begins)
    return lax.div(2 * chip + core - lax.div(first, jnp.int32(rows)), jnp.int32(2))


def clear_of(begins, place_ref, rows):
    chip, core = place_ref[0], place_ref[1]
    start = start_of((2 * chip + 2) * rows - 1, begins)
    blocks = 2 * chip + core - lax.div(start + rows - 1, jnp.int32(rows))
    return jnp.maximum(lax.div(blocks, jnp.int32(2)), 0)


def stack(to_ref, query_refs):
    rows = query_refs[0].shape[0]
    heads = query_refs[0].shape[1] // HEAD
    for group in range(2 * heads):
        column = slice(group % heads * HEAD, (group % heads + 1) * HEAD)
        to_ref[group * rows : (group + 1) * rows, :] = query_refs[group // heads][:, column]


def forward_kernel(
    place_ref, query_hbm_ref, query_other_ref, *rest,
):
    *block_refs, kept_ref, pairs_ref, acc_ref, stats_ref, sent_ref = rest[:-9]
    scores_ref, top_ref, weights_ref, turned_ref, starts_ref, query_ref = rest[-9:-3]
    kept_sem, block_sem, query_sem = rest[-3:]
    rows = query_ref.shape[0]
    heads = query_ref.shape[1] // HEAD
    groups = 2 * heads
    scale = LOG2E / math.sqrt(HEAD)
    own_rows = pltpu.make_async_copy(query_hbm_ref, query_ref, query_sem)
    own_rows.start()
    begins = begins_of(place_ref)
    last, clear = last_of(begins, place_ref, rows), clear_of(begins, place_ref, rows)
    own = 2 * place_ref[0] + place_ref[1]
    shards = (own, 2 * place_ref[0] + 1 - place_ref[1])

    def bring(block_ref, back):
        to = pl.ds(pl.multiple_of(back * rows, rows), rows)
        return pltpu.make_async_copy(block_ref, pairs_ref.at[to], block_sem.at[back])

    for back, block_ref in enumerate(block_refs):
        @pl.when(back <= last)
        def start():
            bring(block_ref, back).start()

    along = lax.broadcasted_iota(jnp.int32, (1, rows), 1)
    for slot, rows_ref in ((1, query_other_ref), (0, query_ref)):
        if slot == 0:
            own_rows.wait()
        starts_ref[slot] = start_of(shards[slot] * rows + along, begins)
        for head in range(heads):
            span = slice((slot * heads + head) * rows, (slot * heads + head + 1) * rows)
            turned_ref[:, span] = rows_ref[:, head * HEAD : (head + 1) * HEAD].T
    top_ref[...] = jnp.full_like(top_ref, NEG_LARGE)
    acc_ref[...] = jnp.zeros_like(acc_ref)

    def measure(back, masked, count=1):
        to = pl.ds(pl.multiple_of(back * rows, rows), count * rows)
        for more in range(count):
            bring(block_refs[0], back + more).wait()
        keys = pairs_ref[to, :HEAD]
        allowed = []
        if masked:
            key_pos = (own - 2 * back) * rows + lax.broadcasted_iota(jnp.int32, (rows, rows), 0)
            across = lax.broadcasted_iota(jnp.int32, (rows, rows), 1)
            for slot in range(2):
                query_pos = shards[slot] * rows + across
                allowed.append((key_pos <= query_pos) & (key_pos >= starts_ref[slot]))
        for group in range(groups):
            span = slice(group * rows, (group + 1) * rows)
            scores = matmul(keys, turned_ref[:, span])
            if masked:
                scores = jnp.where(allowed[group // heads], scores, NEG_LARGE)
            scores_ref[to, span] = scores
            top_ref[:, span] = jnp.maximum(top_ref[:, span], jnp.max(fold(scores), axis=0))

    def masked(step, unused):
        measure(jnp.where(step == 0, 0, clear + step), True)
        return unused

    def plain(back, unused):
        measure(back, False)
        return unused

    def two_plain(pair, unused):
        measure(1 + 2 * pair, False, 2)
        return unused

    lax.fori_loop(0, last - clear + 1, masked, 0)
    twos = lax.div(clear, jnp.int32(2))
    lax.fori_loop(0, twos, two_plain, 0)
    lax.fori_loop(1 + 2 * twos, clear + 1, plain, 0)
    top = jnp.max(top_ref[...], axis=0, keepdims=True) * scale
    top_ref[...] = jnp.broadcast_to(top, top_ref.shape)

    def weigh(back, count):
        to = pl.ds(pl.multiple_of(back * rows, rows), count * rows)
        turned_values = jnp.concatenate(
            [pairs_ref[to, HEAD:].T, jnp.ones((16, count * rows), jnp.bfloat16)], axis=0
        )
        for group in range(groups):
            span = slice(group * rows, (group + 1) * rows)
            weights_ref[to, span] = jnp.exp2(
                scores_ref[to, span] * scale - top_ref[:1, span]
            ).astype(jnp.bfloat16)
        for more in range(count):
            keep(back + more).start()
        acc_ref[...] += matmul(turned_values, weights_ref[to, :])

    def weigh_two(pair, unused):
        weigh(2 * pair, 2)
        return unused

    def weigh_one(back, unused):
        weigh(back, 1)
        return unused

    def keep(back):
        to = pl.ds(pl.multiple_of(back * rows, rows), rows)
        return pltpu.make_async_copy(weights_ref.at[to], kept_ref.at[to], kept_sem.at[back])

    def kept(back, unused):
        keep(back).wait()
        return unused

    twos = lax.div(last + 1, jnp.int32(2))
    lax.fori_loop(0, twos, weigh_two, 0)
    lax.fori_loop(2 * twos, last + 1, weigh_one, 0)
    totals = acc_ref[HEAD : HEAD + 1, :]
    log_totals = top_ref[:1, :] + jnp.log2(totals)
    stats_ref[...] = jnp.concatenate([top_ref[:1, :], log_totals] + [top] * 6, axis=0)
    parts, rest = [], log_totals
    for _ in range(3):
        parts.append(rest.astype(jnp.bfloat16))
        rest = rest - parts[-1].astype(jnp.float32)
    sent_ref[HEAD:, :] = jnp.concatenate(
        parts + [jnp.zeros((EXTRA - 3, totals.shape[1]), jnp.bfloat16)], axis=0
    )
    inverse = 1.0 / totals
    for group in range(groups):
        span = slice(group * rows, (group + 1) * rows)
        result = acc_ref[:HEAD, span] * inverse[:, span]
        acc_ref[:HEAD, span] = result
        sent_ref[:HEAD, span] = result.astype(jnp.bfloat16)
    lax.fori_loop(0, last + 1, kept, 0)


def fetch(slot, kept_ref, weights_ref, kept_sem, rows):
    def copy(back):
        of = pl.ds(pl.multiple_of(back * rows, rows), rows)
        to = pl.ds(pl.multiple_of((back - slot) * rows, rows), rows)
        return pltpu.make_async_copy(kept_ref.at[of], weights_ref.at[to], kept_sem.at[back - slot])

    return copy


def fetch_all(first, stop, copy):
    def start(back, unused):
        copy(back).start()
        return unused

    lax.fori_loop(first, stop, start, 0)


def accumulate(
    first, stop, pairs_ref, weights_ref, copy, query_ref,
    scaled_ref, turned_scaled_ref, delta_ref, total_ref, move_ref, pair_grad_ref, slot,
):
    rows = move_ref.shape[0]
    groups = move_ref.shape[1] // rows
    root = 1.0 / math.sqrt(HEAD)

    def visit(back, unused):
        at = pl.ds(pl.multiple_of(back * rows, rows), rows)
        to = pl.ds(pl.multiple_of((back - slot) * rows, rows), rows)
        values = pairs_ref[at, HEAD:]
        turned_keys = pairs_ref[at, :HEAD].T
        copy(back).wait()
        for group in range(groups):
            span = slice(group * rows, (group + 1) * rows)
            prob_grad = matmul(values, turned_scaled_ref[:, span])
            move_ref[:, span] = (
                weights_ref[to, span].astype(jnp.float32) * (prob_grad - delta_ref[:, span])
            ).astype(jnp.bfloat16)
        pair_grad_ref[to, HEAD:] = matmul(weights_ref[to, :], scaled_ref[...]).astype(jnp.bfloat16)
        pair_grad_ref[to, :HEAD] = (matmul(move_ref[...], query_ref[...]) * root).astype(
            jnp.bfloat16
        )
        total_ref[...] += matmul(turned_keys, move_ref[...])
        return unused

    def unseen(back, unused):
        to = pl.ds(pl.multiple_of((back - slot) * rows, rows), rows)
        pair_grad_ref[to, :] = jnp.zeros((rows, 2 * HEAD), jnp.bfloat16)
        return unused

    lax.fori_loop(first, stop, visit, 0)
    lax.fori_loop(jnp.maximum(first, stop), slot + pair_grad_ref.shape[0] // rows, unseen, 0)


def hand_out(pair_grad_ref, block_refs):
    rows = block_refs[0].shape[0]
    for at, block_ref in enumerate(block_refs):
        block_ref[...] = pair_grad_ref[at * rows : (at + 1) * rows, :]


def backward_far_kernel(
    place_ref, stats_ref, arrived_ref, acc_ref, grad_ref, grad_other_ref,
    query_ref, query_other_ref, pairs_ref, kept_ref,
    out_ref, scaled_ref, turned_scaled_ref, delta_ref, total_ref, *rest, split,
):
    *block_refs, move_ref, stacked_ref, pair_grad_ref, weights_ref, kept_sem = rest
    rows = out_ref.shape[0]
    heads = grad_ref.shape[1] // HEAD
    groups = 2 * heads
    copy = fetch(split, kept_ref, weights_ref, kept_sem, rows)
    last = last_of(begins_of(place_ref), place_ref, rows)
    fetch_all(split, last + 1, copy)
    stack(stacked_ref, (query_ref, query_other_ref))
    total_ref[...] = jnp.zeros_like(total_ref)
    for group in range(groups):
        span = slice(group * rows, (group + 1) * rows)
        there = (group + heads) % groups
        theirs = slice(there * rows, (there + 1) * rows)
        other_log = arrived_ref[HEAD : HEAD + 1, theirs].astype(jnp.float32)
        for part in range(1, 3):
            other_log += arrived_ref[HEAD + part : HEAD + part + 1, theirs].astype(jnp.float32)
        own_top, own_log = stats_ref[0:1, span], stats_ref[1:2, span]
        most = jnp.maximum(own_log, other_log)
        log_totals = most + jnp.log2(jnp.exp2(own_log - most) + jnp.exp2(other_log - most))
        result = acc_ref[:HEAD, span] * jnp.exp2(own_log - log_totals) + arrived_ref[
            :HEAD, theirs
        ].astype(jnp.float32) * jnp.exp2(other_log - log_totals)
        result = result.astype(jnp.bfloat16)
        column = slice(group % heads * HEAD, (group % heads + 1) * HEAD)
        if group < heads:
            out_ref[:, column] = result.T
        grads = (grad_ref if group < heads else grad_other_ref)[:, column].T
        scaled = grads.astype(jnp.float32) * jnp.exp2(own_top - log_totals)
        delta_ref[:, span] = jnp.sum(result.astype(jnp.float32) * scaled, axis=0, keepdims=True)
        low = scaled.astype(jnp.bfloat16)
        turned_scaled_ref[:, span] = low
        scaled_ref[span, :] = low.T
    accumulate(
        split, last + 1, pairs_ref, weights_ref, copy, stacked_ref,
        scaled_ref, turned_scaled_ref, delta_ref, total_ref, move_ref, pair_grad_ref, split,
    )
    hand_out(pair_grad_ref, block_refs)


def backward_near_kernel(
    place_ref, scaled_ref, turned_scaled_ref, delta_ref, begun_ref,
    query_ref, query_other_ref, pairs_ref, kept_ref, *rest, first, ends,
):
    *out_refs, move_ref, stacked_ref, pair_grad_ref, weights_ref, kept_sem = rest
    rows = query_ref.shape[0]
    groups = turned_scaled_ref.shape[1] // rows
    heads = groups // 2
    root = 1.0 / math.sqrt(HEAD)
    if ends:
        query_grad_ref, query_grad_other_ref, *block_refs, total_ref = out_refs
    else:
        total_ref, *block_refs = out_refs
    stop = jnp.minimum(last_of(begins_of(place_ref), place_ref, rows) + 1, first + len(block_refs))
    copy = fetch(first, kept_ref, weights_ref, kept_sem, rows)
    fetch_all(first, stop, copy)
    stack(stacked_ref, (query_ref, query_other_ref))
    total_ref[...] = begun_ref[...]
    accumulate(
        first, stop, pairs_ref, weights_ref, copy, stacked_ref,
        scaled_ref, turned_scaled_ref, delta_ref, total_ref, move_ref, pair_grad_ref, first,
    )
    hand_out(pair_grad_ref, block_refs)
    if ends:
        for group in range(groups):
            span = slice(group * rows, (group + 1) * rows)
            column = slice(group % heads * HEAD, (group % heads + 1) * HEAD)
            to_ref = query_grad_ref if group < heads else query_grad_other_ref
            to_ref[:, column] = (total_ref[:, span] * root).astype(jnp.bfloat16).T


def smem():
    return pl.BlockSpec(memory_space=pltpu.SMEM)


def vmem():
    return pl.BlockSpec(memory_space=pltpu.VMEM)


def hbm():
    return pl.BlockSpec(memory_space=pltpu.HBM)


def swap_cores(value):
    return lax.ppermute(value, "core", [(0, 1), (1, 0)])


def cost(blocks, rows, wide, matmuls):
    return pl.CostEstimate(
        flops=2 * matmuls * blocks * rows * wide * HEAD,
        transcendentals=0,
        bytes_accessed=2 * blocks * rows * wide,
    )


def attend(place, queries, grad, blocks, split, send, swap=swap_cores):
    slots = len(blocks)
    rows, columns = queries[0].shape
    heads = columns // HEAD
    wide = 2 * heads * rows
    blocks, queries = lax.optimization_barrier((blocks, queries))
    blocks = [pltpu.with_memory_space_constraint(block, pltpu.HBM) for block in blocks]
    weights, pairs, acc, stats, sent = pl.pallas_call(
        forward_kernel,
        out_shape=(
            pltpu.HBM((slots * rows, wide), jnp.bfloat16),
            jax.ShapeDtypeStruct((slots * rows, 2 * HEAD), jnp.bfloat16),
            jax.ShapeDtypeStruct((HEAD + EXTRA, wide), jnp.float32),
            jax.ShapeDtypeStruct((8, wide), jnp.float32),
            jax.ShapeDtypeStruct((HEAD + EXTRA, wide), jnp.bfloat16),
        ),
        in_specs=[smem()] + [hbm(), vmem()] + [hbm()] * slots,
        out_specs=(hbm(),) + (vmem(),) * 4,
        scratch_shapes=[
            pltpu.VMEM((slots * rows, wide), jnp.float32),
            pltpu.VMEM((8, wide), jnp.float32),
            pltpu.VMEM((slots * rows, wide), jnp.bfloat16),
            pltpu.VMEM((HEAD, wide), jnp.bfloat16),
            pltpu.VMEM((2, 1, rows), jnp.int32),
            pltpu.VMEM((rows, columns), jnp.bfloat16),
            pltpu.SemaphoreType.DMA((slots,)),
            pltpu.SemaphoreType.DMA((slots,)),
            pltpu.SemaphoreType.DMA,
        ],
        compiler_params=pltpu.CompilerParams(vmem_limit_bytes=36 << 20),
        cost_estimate=cost(slots, rows, wide, 2),
        name="attend_forward",
    )(place, pltpu.with_memory_space_constraint(queries[0], pltpu.HBM), queries[1], *blocks)
    weights = pltpu.with_memory_space_constraint(weights, pltpu.HBM)
    arrived = swap(sent)
    grad, stats = lax.optimization_barrier((grad, stats))
    grad_other = swap(grad)
    half = jax.ShapeDtypeStruct((rows, columns), jnp.bfloat16)
    params = pltpu.CompilerParams(vmem_limit_bytes=22 << 20)
    move = pltpu.VMEM((rows, wide), jnp.bfloat16)

    def held(blocks):
        return [
            pltpu.VMEM((wide, HEAD), jnp.bfloat16),
            pltpu.VMEM((blocks * rows, 2 * HEAD), jnp.bfloat16),
            pltpu.VMEM((blocks * rows, wide), jnp.bfloat16),
            pltpu.SemaphoreType.DMA((blocks,)),
        ]

    block = jax.ShapeDtypeStruct((rows, 2 * HEAD), jnp.bfloat16)
    out, scaled, turned_scaled, delta, total, *far = pl.pallas_call(
        functools.partial(backward_far_kernel, split=split),
        out_shape=(
            half,
            jax.ShapeDtypeStruct((wide, HEAD), jnp.bfloat16),
            jax.ShapeDtypeStruct((HEAD, wide), jnp.bfloat16),
            jax.ShapeDtypeStruct((1, wide), jnp.float32),
            jax.ShapeDtypeStruct((HEAD, wide), jnp.float32),
        )
        + (block,) * (slots - split),
        in_specs=[smem()] + [vmem()] * 8 + [hbm()],
        out_specs=(vmem(),) * (5 + slots - split),
        scratch_shapes=[move] + held(slots - split),
        compiler_params=params,
        cost_estimate=cost(slots - split, rows, wide, 4),
        name="attend_backward_far",
    )(place, stats, arrived, acc, grad, grad_other, *queries, pairs, weights)
    sent_far = send(far, split)
    whole = jax.ShapeDtypeStruct((HEAD, wide), jnp.float32)

    def near_call(total, first, count, outs, scratch, ends, name):
        return pl.pallas_call(
            functools.partial(backward_near_kernel, first=first, ends=ends),
            out_shape=outs + (block,) * count,
            in_specs=[smem()] + [vmem()] * 7 + [hbm()],
            out_specs=(vmem(),) * (len(outs) + count),
            scratch_shapes=scratch + [move] + held(count),
            compiler_params=params,
            cost_estimate=cost(count, rows, wide, 4),
            name=name,
        )(place, scaled, turned_scaled, delta, total, *queries, pairs, weights)

    query_grad, query_grad_other, own, *near = near_call(
        total, 0, split, (half, half), [pltpu.VMEM((HEAD, wide), jnp.float32)], True,
        "attend_backward_near",
    )
    sent_near = send(near, 1)
    return out, query_grad, query_grad_other, own, sent_near, sent_far


def per_device(query, keys_values, doc_lengths, incoming_output_grad):
    chips = lax.axis_size("chip")
    query = query[0, :, 0, :]
    pairs = keys_values[0, :, 0, :]
    rows = query.shape[0]
    reach = min((LONGEST + 2 * rows - 1) // (2 * rows), chips - 1)
    slots = reach + 1
    blocks = [pairs] + [
        lax.ppermute(pairs, "chip", [(c, c + back) for c in range(chips - back)])
        for back in range(1, slots)
    ]
    sections = lax.axis_size("pipe")
    arrived = lax.ppermute(
        incoming_output_grad, "pipe", [(s, (s - 1) % sections) for s in range(sections)]
    )
    arrived, *blocks[1:3] = lax.optimization_barrier((arrived, *blocks[1:3]))
    grad = lax.all_to_all(arrived, "tensor", split_axis=2, concat_axis=1, tiled=True)[0, :, 0, :]
    position = jnp.stack([lax.axis_index("chip"), lax.axis_index("core")]).astype(jnp.int32)
    place = jnp.concatenate([position, doc_lengths[0]])
    split = slots // 2

    def send(blocks, first):
        return [
            lax.ppermute(block, "chip", [(c, c - first - at) for c in range(first + at, chips)])
            for at, block in reversed(list(enumerate(blocks)))
        ]

    out, query_grad, query_grad_other, own, near, far = attend(
        place, (query, swap_cores(query)), grad, blocks, split, send
    )
    query_grad = query_grad.astype(jnp.float32) + swap_cores(query_grad_other).astype(jnp.float32)
    query_grad = query_grad.astype(jnp.bfloat16)
    sums = own.astype(jnp.float32)
    for sent in far:
        sums += sent.astype(jnp.float32)
    sums = lax.optimization_barrier(sums)
    for sent in near:
        sums += sent.astype(jnp.float32)
    pair_grad = sums.astype(jnp.bfloat16)
    return (out[None, :, None, :], query_grad[None, :, None, :], pair_grad[None, :, None, :])


def solution(mesh):
    shape = mesh.devices.shape
    split = Mesh(
        mesh.devices.reshape((shape[0] // 2, 2) + shape[1:]), ("chip", "core", "tensor", "pipe")
    )
    dp = ("chip", "core")
    by_head = P("pipe", dp, "tensor", None)
    in_specs = (by_head, by_head, P("pipe", None), P("pipe", dp + ("tensor",), None, None))
    return jax.shard_map(
        per_device, mesh=split, in_specs=in_specs, out_specs=(by_head,) * 3, check_vma=False
    )
```

```python
import functools
import math

import jax
import jax.numpy as jnp
from jax import lax
from jax.experimental import pallas as pl
from jax.experimental.pallas import tpu as pltpu
from jax.sharding import Mesh, PartitionSpec as P

NEG_LARGE = -1e30
LOG2E = math.log2(math.e)
HEAD = 128
LONGEST = 3072
EXTRA = 16


def matmul(left, right):
    return jnp.dot(left, right, preferred_element_type=jnp.float32)


def fold(array):
    return array.reshape(array.shape[0] // 8, 8, array.shape[1])


def begins_of(place_ref):
    begins = [jnp.int32(0)]
    for at in range(2, place_ref.shape[0] - 1):
        begins.append(begins[-1] + place_ref[at])
    return begins


def start_of(position, begins):
    start = jnp.zeros_like(position)
    for begin in begins:
        start = jnp.where(begin <= position, begin, start)
    return start


def last_of(begins, place_ref, rows):
    chip, core = place_ref[0], place_ref[1]
    first = start_of(2 * chip * rows, begins)
    return lax.div(2 * chip + core - lax.div(first, jnp.int32(rows)), jnp.int32(2))


def clear_of(begins, place_ref, rows):
    chip, core = place_ref[0], place_ref[1]
    start = start_of((2 * chip + 2) * rows - 1, begins)
    blocks = 2 * chip + core - lax.div(start + rows - 1, jnp.int32(rows))
    return jnp.maximum(lax.div(blocks, jnp.int32(2)), 0)


def stack(to_ref, query_refs):
    rows = query_refs[0].shape[0]
    heads = query_refs[0].shape[1] // HEAD
    for group in range(2 * heads):
        column = slice(group % heads * HEAD, (group % heads + 1) * HEAD)
        to_ref[group * rows : (group + 1) * rows, :] = query_refs[group // heads][:, column]


def forward_kernel(
    place_ref, query_hbm_ref, query_other_ref, *rest,
):
    *block_refs, kept_ref, pairs_ref, acc_ref, stats_ref, sent_ref = rest[:-9]
    scores_ref, top_ref, weights_ref, turned_ref, starts_ref, query_ref = rest[-9:-3]
    kept_sem, block_sem, query_sem = rest[-3:]
    rows = query_ref.shape[0]
    heads = query_ref.shape[1] // HEAD
    groups = 2 * heads
    scale = LOG2E / math.sqrt(HEAD)
    own_rows = pltpu.make_async_copy(query_hbm_ref, query_ref, query_sem)
    own_rows.start()
    begins = begins_of(place_ref)
    last, clear = last_of(begins, place_ref, rows), clear_of(begins, place_ref, rows)
    own = 2 * place_ref[0] + place_ref[1]
    shards = (own, 2 * place_ref[0] + 1 - place_ref[1])

    def bring(block_ref, back):
        to = pl.ds(pl.multiple_of(back * rows, rows), rows)
        return pltpu.make_async_copy(block_ref, pairs_ref.at[to], block_sem.at[back])

    for back, block_ref in enumerate(block_refs):
        @pl.when(back <= last)
        def start():
            bring(block_ref, back).start()

    along = lax.broadcasted_iota(jnp.int32, (1, rows), 1)
    for slot, rows_ref in ((1, query_other_ref), (0, query_ref)):
        if slot == 0:
            own_rows.wait()
        starts_ref[slot] = start_of(shards[slot] * rows + along, begins)
        for head in range(heads):
            span = slice((slot * heads + head) * rows, (slot * heads + head + 1) * rows)
            turned_ref[:, span] = rows_ref[:, head * HEAD : (head + 1) * HEAD].T
    top_ref[...] = jnp.full_like(top_ref, NEG_LARGE)
    acc_ref[...] = jnp.zeros_like(acc_ref)

    def measure(back, masked, count=1):
        to = pl.ds(pl.multiple_of(back * rows, rows), count * rows)
        for more in range(count):
            bring(block_refs[0], back + more).wait()
        keys = pairs_ref[to, :HEAD]
        allowed = []
        if masked:
            key_pos = (own - 2 * back) * rows + lax.broadcasted_iota(jnp.int32, (rows, rows), 0)
            across = lax.broadcasted_iota(jnp.int32, (rows, rows), 1)
            for slot in range(2):
                query_pos = shards[slot] * rows + across
                allowed.append((key_pos <= query_pos) & (key_pos >= starts_ref[slot]))
        for group in range(groups):
            span = slice(group * rows, (group + 1) * rows)
            scores = matmul(keys, turned_ref[:, span])
            if masked:
                scores = jnp.where(allowed[group // heads], scores, NEG_LARGE)
            scores_ref[to, span] = scores
            top_ref[:, span] = jnp.maximum(top_ref[:, span], jnp.max(fold(scores), axis=0))

    def masked(step, unused):
        measure(jnp.where(step == 0, 0, clear + step), True)
        return unused

    def plain(back, unused):
        measure(back, False)
        return unused

    def two_plain(pair, unused):
        measure(1 + 2 * pair, False, 2)
        return unused

    lax.fori_loop(0, last - clear + 1, masked, 0)
    twos = lax.div(clear, jnp.int32(2))
    lax.fori_loop(0, twos, two_plain, 0)
    lax.fori_loop(1 + 2 * twos, clear + 1, plain, 0)
    top = jnp.max(top_ref[...], axis=0, keepdims=True) * scale
    top_ref[...] = jnp.broadcast_to(top, top_ref.shape)

    def weigh(back, count):
        to = pl.ds(pl.multiple_of(back * rows, rows), count * rows)
        turned_values = jnp.concatenate(
            [pairs_ref[to, HEAD:].T, jnp.ones((16, count * rows), jnp.bfloat16)], axis=0
        )
        for group in range(groups):
            span = slice(group * rows, (group + 1) * rows)
            weights_ref[to, span] = jnp.exp2(
                scores_ref[to, span] * scale - top_ref[:1, span]
            ).astype(jnp.bfloat16)
        for more in range(count):
            keep(back + more).start()
        acc_ref[...] += matmul(turned_values, weights_ref[to, :])

    def weigh_two(pair, unused):
        weigh(2 * pair, 2)
        return unused

    def weigh_one(back, unused):
        weigh(back, 1)
        return unused

    def keep(back):
        to = pl.ds(pl.multiple_of(back * rows, rows), rows)
        return pltpu.make_async_copy(weights_ref.at[to], kept_ref.at[to], kept_sem.at[back])

    def kept(back, unused):
        keep(back).wait()
        return unused

    twos = lax.div(last + 1, jnp.int32(2))
    lax.fori_loop(0, twos, weigh_two, 0)
    lax.fori_loop(2 * twos, last + 1, weigh_one, 0)
    totals = acc_ref[HEAD : HEAD + 1, :]
    log_totals = top_ref[:1, :] + jnp.log2(totals)
    stats_ref[...] = jnp.concatenate([top_ref[:1, :], log_totals] + [top] * 6, axis=0)
    parts, rest = [], log_totals
    for _ in range(3):
        parts.append(rest.astype(jnp.bfloat16))
        rest = rest - parts[-1].astype(jnp.float32)
    sent_ref[HEAD:, :] = jnp.concatenate(
        parts + [jnp.zeros((EXTRA - 3, totals.shape[1]), jnp.bfloat16)], axis=0
    )
    inverse = 1.0 / totals
    for group in range(groups):
        span = slice(group * rows, (group + 1) * rows)
        result = acc_ref[:HEAD, span] * inverse[:, span]
        acc_ref[:HEAD, span] = result
        sent_ref[:HEAD, span] = result.astype(jnp.bfloat16)
    lax.fori_loop(0, last + 1, kept, 0)


def fetch(slot, kept_ref, weights_ref, kept_sem, rows):
    def copy(back):
        of = pl.ds(pl.multiple_of(back * rows, rows), rows)
        to = pl.ds(pl.multiple_of((back - slot) * rows, rows), rows)
        return pltpu.make_async_copy(kept_ref.at[of], weights_ref.at[to], kept_sem.at[back - slot])

    return copy


def fetch_all(first, stop, copy):
    def start(back, unused):
        copy(back).start()
        return unused

    lax.fori_loop(first, stop, start, 0)


def accumulate(
    first, stop, pairs_ref, weights_ref, copy, query_ref,
    scaled_ref, turned_scaled_ref, delta_ref, total_ref, move_ref, pair_grad_ref, slot,
):
    rows = move_ref.shape[0]
    groups = move_ref.shape[1] // rows
    root = 1.0 / math.sqrt(HEAD)

    def visit(back, unused):
        at = pl.ds(pl.multiple_of(back * rows, rows), rows)
        to = pl.ds(pl.multiple_of((back - slot) * rows, rows), rows)
        values = pairs_ref[at, HEAD:]
        turned_keys = pairs_ref[at, :HEAD].T
        copy(back).wait()
        for group in range(groups):
            span = slice(group * rows, (group + 1) * rows)
            prob_grad = matmul(values, turned_scaled_ref[:, span])
            move_ref[:, span] = (
                weights_ref[to, span].astype(jnp.float32) * (prob_grad - delta_ref[:, span])
            ).astype(jnp.bfloat16)
        pair_grad_ref[to, HEAD:] = matmul(weights_ref[to, :], scaled_ref[...]).astype(jnp.bfloat16)
        pair_grad_ref[to, :HEAD] = (matmul(move_ref[...], query_ref[...]) * root).astype(
            jnp.bfloat16
        )
        total_ref[...] += matmul(turned_keys, move_ref[...])
        return unused

    def unseen(back, unused):
        to = pl.ds(pl.multiple_of((back - slot) * rows, rows), rows)
        pair_grad_ref[to, :] = jnp.zeros((rows, 2 * HEAD), jnp.bfloat16)
        return unused

    lax.fori_loop(first, stop, visit, 0)
    lax.fori_loop(jnp.maximum(first, stop), slot + pair_grad_ref.shape[0] // rows, unseen, 0)


def hand_out(pair_grad_ref, block_refs):
    rows = block_refs[0].shape[0]
    for at, block_ref in enumerate(block_refs):
        block_ref[...] = pair_grad_ref[at * rows : (at + 1) * rows, :]


def backward_far_kernel(
    place_ref, stats_ref, arrived_ref, acc_ref, grad_ref, grad_other_ref,
    query_ref, query_other_ref, pairs_ref, kept_ref,
    out_ref, scaled_ref, turned_scaled_ref, delta_ref, total_ref, *rest, split,
):
    *block_refs, move_ref, stacked_ref, pair_grad_ref, weights_ref, kept_sem = rest
    rows = out_ref.shape[0]
    heads = grad_ref.shape[1] // HEAD
    groups = 2 * heads
    copy = fetch(split, kept_ref, weights_ref, kept_sem, rows)
    last = last_of(begins_of(place_ref), place_ref, rows)
    fetch_all(split, last + 1, copy)
    stack(stacked_ref, (query_ref, query_other_ref))
    total_ref[...] = jnp.zeros_like(total_ref)
    for group in range(groups):
        span = slice(group * rows, (group + 1) * rows)
        there = (group + heads) % groups
        theirs = slice(there * rows, (there + 1) * rows)
        other_log = arrived_ref[HEAD : HEAD + 1, theirs].astype(jnp.float32)
        for part in range(1, 3):
            other_log += arrived_ref[HEAD + part : HEAD + part + 1, theirs].astype(jnp.float32)
        own_top, own_log = stats_ref[0:1, span], stats_ref[1:2, span]
        most = jnp.maximum(own_log, other_log)
        log_totals = most + jnp.log2(jnp.exp2(own_log - most) + jnp.exp2(other_log - most))
        result = acc_ref[:HEAD, span] * jnp.exp2(own_log - log_totals) + arrived_ref[
            :HEAD, theirs
        ].astype(jnp.float32) * jnp.exp2(other_log - log_totals)
        result = result.astype(jnp.bfloat16)
        column = slice(group % heads * HEAD, (group % heads + 1) * HEAD)
        if group < heads:
            out_ref[:, column] = result.T
        grads = (grad_ref if group < heads else grad_other_ref)[:, column].T
        scaled = grads.astype(jnp.float32) * jnp.exp2(own_top - log_totals)
        delta_ref[:, span] = jnp.sum(result.astype(jnp.float32) * scaled, axis=0, keepdims=True)
        low = scaled.astype(jnp.bfloat16)
        turned_scaled_ref[:, span] = low
        scaled_ref[span, :] = low.T
    accumulate(
        split, last + 1, pairs_ref, weights_ref, copy, stacked_ref,
        scaled_ref, turned_scaled_ref, delta_ref, total_ref, move_ref, pair_grad_ref, split,
    )
    hand_out(pair_grad_ref, block_refs)


def backward_near_kernel(
    place_ref, scaled_ref, turned_scaled_ref, delta_ref, begun_ref,
    query_ref, query_other_ref, pairs_ref, kept_ref, *rest, first, ends,
):
    *out_refs, move_ref, stacked_ref, pair_grad_ref, weights_ref, kept_sem = rest
    rows = query_ref.shape[0]
    groups = turned_scaled_ref.shape[1] // rows
    heads = groups // 2
    root = 1.0 / math.sqrt(HEAD)
    if ends:
        query_grad_ref, query_grad_other_ref, *block_refs, total_ref = out_refs
    else:
        total_ref, *block_refs = out_refs
    stop = jnp.minimum(last_of(begins_of(place_ref), place_ref, rows) + 1, first + len(block_refs))
    copy = fetch(first, kept_ref, weights_ref, kept_sem, rows)
    fetch_all(first, stop, copy)
    stack(stacked_ref, (query_ref, query_other_ref))
    total_ref[...] = begun_ref[...]
    accumulate(
        first, stop, pairs_ref, weights_ref, copy, stacked_ref,
        scaled_ref, turned_scaled_ref, delta_ref, total_ref, move_ref, pair_grad_ref, first,
    )
    hand_out(pair_grad_ref, block_refs)
    if ends:
        for group in range(groups):
            span = slice(group * rows, (group + 1) * rows)
            column = slice(group % heads * HEAD, (group % heads + 1) * HEAD)
            to_ref = query_grad_ref if group < heads else query_grad_other_ref
            to_ref[:, column] = (total_ref[:, span] * root).astype(jnp.bfloat16).T


def smem():
    return pl.BlockSpec(memory_space=pltpu.SMEM)


def vmem():
    return pl.BlockSpec(memory_space=pltpu.VMEM)


def hbm():
    return pl.BlockSpec(memory_space=pltpu.HBM)


def swap_cores(value):
    return lax.ppermute(value, "core", [(0, 1), (1, 0)])


def cost(blocks, rows, wide, matmuls):
    return pl.CostEstimate(
        flops=2 * matmuls * blocks * rows * wide * HEAD,
        transcendentals=0,
        bytes_accessed=2 * blocks * rows * wide,
    )


def attend(place, queries, grad, blocks, split, send, swap=swap_cores):
    slots = len(blocks)
    rows, columns = queries[0].shape
    heads = columns // HEAD
    wide = 2 * heads * rows
    blocks, queries = lax.optimization_barrier((blocks, queries))
    blocks = [pltpu.with_memory_space_constraint(block, pltpu.HBM) for block in blocks]
    weights, pairs, acc, stats, sent = pl.pallas_call(
        forward_kernel,
        out_shape=(
            pltpu.HBM((slots * rows, wide), jnp.bfloat16),
            jax.ShapeDtypeStruct((slots * rows, 2 * HEAD), jnp.bfloat16),
            jax.ShapeDtypeStruct((HEAD + EXTRA, wide), jnp.float32),
            jax.ShapeDtypeStruct((8, wide), jnp.float32),
            jax.ShapeDtypeStruct((HEAD + EXTRA, wide), jnp.bfloat16),
        ),
        in_specs=[smem()] + [hbm(), vmem()] + [hbm()] * slots,
        out_specs=(hbm(),) + (vmem(),) * 4,
        scratch_shapes=[
            pltpu.VMEM((slots * rows, wide), jnp.float32),
            pltpu.VMEM((8, wide), jnp.float32),
            pltpu.VMEM((slots * rows, wide), jnp.bfloat16),
            pltpu.VMEM((HEAD, wide), jnp.bfloat16),
            pltpu.VMEM((2, 1, rows), jnp.int32),
            pltpu.VMEM((rows, columns), jnp.bfloat16),
            pltpu.SemaphoreType.DMA((slots,)),
            pltpu.SemaphoreType.DMA((slots,)),
            pltpu.SemaphoreType.DMA,
        ],
        compiler_params=pltpu.CompilerParams(vmem_limit_bytes=36 << 20),
        cost_estimate=cost(slots, rows, wide, 2),
        name="attend_forward",
    )(place, pltpu.with_memory_space_constraint(queries[0], pltpu.HBM), queries[1], *blocks)
    weights = pltpu.with_memory_space_constraint(weights, pltpu.HBM)
    arrived = swap(sent)
    grad, stats = lax.optimization_barrier((grad, stats))
    grad_other = swap(grad)
    half = jax.ShapeDtypeStruct((rows, columns), jnp.bfloat16)
    params = pltpu.CompilerParams(vmem_limit_bytes=24 << 20)
    move = pltpu.VMEM((rows, wide), jnp.bfloat16)

    def held(blocks):
        return [
            pltpu.VMEM((wide, HEAD), jnp.bfloat16),
            pltpu.VMEM((blocks * rows, 2 * HEAD), jnp.bfloat16),
            pltpu.VMEM((blocks * rows, wide), jnp.bfloat16),
            pltpu.SemaphoreType.DMA((blocks,)),
        ]

    block = jax.ShapeDtypeStruct((rows, 2 * HEAD), jnp.bfloat16)
    out, scaled, turned_scaled, delta, total, *far = pl.pallas_call(
        functools.partial(backward_far_kernel, split=split),
        out_shape=(
            half,
            jax.ShapeDtypeStruct((wide, HEAD), jnp.bfloat16),
            jax.ShapeDtypeStruct((HEAD, wide), jnp.bfloat16),
            jax.ShapeDtypeStruct((1, wide), jnp.float32),
            jax.ShapeDtypeStruct((HEAD, wide), jnp.float32),
        )
        + (block,) * (slots - split),
        in_specs=[smem()] + [vmem()] * 8 + [hbm()],
        out_specs=(vmem(),) * (5 + slots - split),
        scratch_shapes=[move] + held(slots - split),
        compiler_params=params,
        cost_estimate=cost(slots - split, rows, wide, 4),
        name="attend_backward_far",
    )(place, stats, arrived, acc, grad, grad_other, *queries, pairs, weights)
    sent_far = send(far, split)
    whole = jax.ShapeDtypeStruct((HEAD, wide), jnp.float32)

    def near_call(total, first, count, outs, scratch, ends, name):
        return pl.pallas_call(
            functools.partial(backward_near_kernel, first=first, ends=ends),
            out_shape=outs + (block,) * count,
            in_specs=[smem()] + [vmem()] * 7 + [hbm()],
            out_specs=(vmem(),) * (len(outs) + count),
            scratch_shapes=scratch + [move] + held(count),
            compiler_params=params,
            cost_estimate=cost(count, rows, wide, 4),
            name=name,
        )(place, scaled, turned_scaled, delta, total, *queries, pairs, weights)

    query_grad, query_grad_other, own, *near = near_call(
        total, 0, split, (half, half), [pltpu.VMEM((HEAD, wide), jnp.float32)], True,
        "attend_backward_near",
    )
    sent_near = send(near, 1)
    return out, query_grad, query_grad_other, own, sent_near, sent_far


def per_device(query, keys_values, doc_lengths, incoming_output_grad):
    chips = lax.axis_size("chip")
    query = query[0, :, 0, :]
    pairs = keys_values[0, :, 0, :]
    rows = query.shape[0]
    reach = min((LONGEST + 2 * rows - 1) // (2 * rows), chips - 1)
    slots = reach + 1
    blocks = [pairs] + [
        lax.ppermute(pairs, "chip", [(c, c + back) for c in range(chips - back)])
        for back in range(1, slots)
    ]
    sections = lax.axis_size("pipe")
    arrived = lax.ppermute(
        incoming_output_grad, "pipe", [(s, (s - 1) % sections) for s in range(sections)]
    )
    arrived, *blocks[1:3] = lax.optimization_barrier((arrived, *blocks[1:3]))
    grad = lax.all_to_all(arrived, "tensor", split_axis=2, concat_axis=1, tiled=True)[0, :, 0, :]
    position = jnp.stack([lax.axis_index("chip"), lax.axis_index("core")]).astype(jnp.int32)
    place = jnp.concatenate([position, doc_lengths[0]])
    split = max(slots // 3, 1)

    def send(blocks, first):
        return [
            lax.ppermute(block, "chip", [(c, c - first - at) for c in range(first + at, chips)])
            for at, block in reversed(list(enumerate(blocks)))
        ]

    out, query_grad, query_grad_other, own, near, far = attend(
        place, (query, swap_cores(query)), grad, blocks, split, send
    )
    query_grad = query_grad.astype(jnp.float32) + swap_cores(query_grad_other).astype(jnp.float32)
    query_grad = query_grad.astype(jnp.bfloat16)
    sums = own.astype(jnp.float32)
    for sent in far:
        sums += sent.astype(jnp.float32)
    sums = lax.optimization_barrier(sums)
    for sent in near:
        sums += sent.astype(jnp.float32)
    pair_grad = sums.astype(jnp.bfloat16)
    return (out[None, :, None, :], query_grad[None, :, None, :], pair_grad[None, :, None, :])


def solution(mesh):
    shape = mesh.devices.shape
    split = Mesh(
        mesh.devices.reshape((shape[0] // 2, 2) + shape[1:]), ("chip", "core", "tensor", "pipe")
    )
    dp = ("chip", "core")
    by_head = P("pipe", dp, "tensor", None)
    in_specs = (by_head, by_head, P("pipe", None), P("pipe", dp + ("tensor",), None, None))
    return jax.shard_map(
        per_device, mesh=split, in_specs=in_specs, out_specs=(by_head,) * 3, check_vma=False
    )
```
